32 devices in a mesh: rep: 4 (over x, core), fsdp: 8 (over z, y).
Axes of the slice: x: 2, y: 2, z: 4, core: 2. Of those that a mesh axis runs over, the one named last changes fastest.
Arguments:
- patches: bfloat16 [96, 167, 768], P(('rep', 'fsdp')), may hold values from -6 to 6
- mask_places: int32 [96, 100], P(('rep', 'fsdp')), may hold values from 0 to 166, as said below
- square_weights: float32 [6, 768, 768], P(None, 'fsdp')
- square_first: float32 [6, 768, 768], P(None, 'fsdp'), may hold values from -5.722046e-06 to 5.722046e-06
- square_second: float32 [6, 768, 768], P(None, 'fsdp'), may hold values from 3.5321272e-15 to 3.532127e-14
- square_teacher: float32 [6, 768, 768], P(None, 'fsdp')
- feed_weights: float32 [1, 2, 768, 3072], P(None, None, 'fsdp')
- feed_first: float32 [1, 2, 768, 3072], P(None, None, 'fsdp'), may hold values from -5.722046e-06 to 5.722046e-06
- feed_second: float32 [1, 2, 768, 3072], P(None, None, 'fsdp'), may hold values from 3.5321272e-15 to 3.532127e-14
- feed_teacher: float32 [1, 2, 768, 3072], P(None, None, 'fsdp')
- vector_weights: float32 [184, 768], P(None, 'fsdp')
- vector_first: float32 [184, 768], P(None, 'fsdp'), may hold values from -5.722046e-06 to 5.722046e-06
- vector_second: float32 [184, 768], P(None, 'fsdp'), may hold values from 3.5321272e-15 to 3.532127e-14
- vector_teacher: float32 [184, 768], P(None, 'fsdp')
Outputs:
- loss: float32 [], replicated
- clip_norm: float32 [], replicated
- square_step: float32 [6, 768, 768], P(None, 'fsdp')
- square_first_new: float32 [6, 768, 768], P(None, 'fsdp')
- square_second_new: float32 [6, 768, 768], P(None, 'fsdp')
- square_teacher_step: float32 [6, 768, 768], P(None, 'fsdp')
- feed_step: float32 [1, 2, 768, 3072], P(None, None, 'fsdp')
- feed_first_new: float32 [1, 2, 768, 3072], P(None, None, 'fsdp')
- feed_second_new: float32 [1, 2, 768, 3072], P(None, None, 'fsdp')
- feed_teacher_step: float32 [1, 2, 768, 3072], P(None, None, 'fsdp')
- vector_step: float32 [184, 768], P(None, 'fsdp')
- vector_first_new: float32 [184, 768], P(None, 'fsdp')
- vector_second_new: float32 [184, 768], P(None, 'fsdp')
- vector_teacher_step: float32 [184, 768], P(None, 'fsdp')
The draws below stay inside these ranges and needn't reach their ends.
Inputs may be any that keep to these rules, and one draw needn't show every extreme that they name: `mask_places`: each row lists 100 different positions of its sample.
All inputs are finite; a program needn't handle non-finite values.
Results may differ from the reference program's by a relative error of at most 0.0015.
The reference program's roundings to bfloat16 on the way count: a program that leaves them out, or rounds other values in their place, can miss the bound.
Values may be sent and summed in bfloat16 or wider, within the bound.
No kernel may reach another device: no remote copies, remote signals or barrier semaphores. Data moves between devices by JAX's collectives and lax.ppermute only.
A program may use at most 320 MiB of HBM per device.

```python
import math
import jax
import jax.numpy as jnp
from jax import lax

D = 768
HEADS = 12
FF = 3072
SEQ = 167
MASKED = 100
LAYERS = 1
ADAM_STEP = 10
SAMP_DEV = 3
SAMPLES = 96
NSQ = 6
NVEC = 184
N_REP = 4


def draw_mask_places(key, part):
    scores = jax.random.randint(key, (SAMPLES, SEQ), 0, 1 << 20)
    scores = scores * SEQ + jnp.arange(SEQ, dtype=jnp.int32)[None, :]
    order = jnp.argsort(scores, axis=1)
    return order[:, :MASKED].astype(jnp.int32)


def unit_noise(key_rows, shape):
    return jax.random.normal(key_rows, shape, jnp.float32)


def square_student(key):
    base = unit_noise(jax.random.fold_in(key, 11), (NSQ, D, D))
    slots = jnp.arange(NSQ)
    output_slots = (slots >= 1) & (slots < NSQ - 1) & ((slots - 1) % 4 == 3)
    scaling = jnp.where(output_slots, 8.0, 1.0) * D ** (-0.5)
    return base * scaling[:, None, None]


def draw_square_weights(key, part):
    return square_student(key)


def draw_square_teacher(key, part):
    offset = 0.005 * unit_noise(jax.random.fold_in(key, 12), (NSQ, D, D))
    return square_student(key) + offset


def feed_student(key):
    return unit_noise(jax.random.fold_in(key, 31), (LAYERS, 2, D, FF)) * D ** (-0.5)


def draw_feed_weights(key, part):
    return feed_student(key)


def draw_feed_teacher(key, part):
    offset = 0.005 * unit_noise(jax.random.fold_in(key, 32), (LAYERS, 2, D, FF))
    return feed_student(key) + offset


def vector_student(key):
    noise = unit_noise(jax.random.fold_in(key, 21), (NVEC, D))
    rows = jnp.arange(NVEC)
    relative = rows - (2 + SEQ)
    in_layer = (relative >= 0) & (relative < 12 * LAYERS)
    within = relative % 12
    gain_rows = in_layer & ((within == 3) | (within == 6)) | (rows == NVEC - 3)
    spread = jnp.where(rows == 1, 1.0, jnp.where((rows >= 2) & (rows < 2 + SEQ), 0.5, 0.3))
    return jnp.where(gain_rows[:, None], 1.0 + 0.1 * noise, spread[:, None] * noise)


def draw_vector_weights(key, part):
    return vector_student(key)


def draw_vector_teacher(key, part):
    offset = 0.005 * unit_noise(jax.random.fold_in(key, 22), (NVEC, D))
    return vector_student(key) + offset


def block_scale(own_key, extent, split, smallest, largest):
    def one(axis_at, shards_of):
        heights = jax.random.uniform(jax.random.fold_in(jax.random.fold_in(own_key, 6), axis_at), (shards_of,), jnp.float32, smallest / len(split), largest / len(split))
        return jnp.repeat(jnp.exp(heights), extent[axis_at] // shards_of).reshape((-1,) + (1,) * (len(extent) - axis_at - 1))

    level = one(*split[0])
    for cut in split[1:]:
        level = level * one(*cut)
    return level


def bell_draw(stream_key, shape, deviation, most, cuts=(), kind=jnp.bfloat16):
    values = deviation * jax.random.normal(stream_key, shape, jnp.float32)
    if cuts:
        values = values * block_scale(stream_key, shape, cuts, -0.22, 0.18)
    return jnp.clip(values, -most, most).astype(kind)


def setup_inputs(seed: int = 0) -> dict:
    streams_of = jax.random.split(jax.random.key(seed), 15)
    patches = bell_draw(streams_of[0], (SAMPLES, SEQ, D), 1.0, 6.0, ((0, 32),))
    mask_places = draw_mask_places(jax.random.fold_in(streams_of[14], 71), 0)
    square_weights = draw_square_weights(jax.random.fold_in(streams_of[14], 71), 0)
    square_first = bell_draw(streams_of[3], (NSQ, D, D), (0.03 / (D * (SAMPLES * MASKED) ** 0.5)), 5.7220458984375e-06, ((1, 8),), jnp.float32)
    square_second = jnp.clip(jnp.exp(math.log(3.5321270512372535e-14) - 2.3025851 * jax.random.uniform(streams_of[4], (NSQ, D, D), jnp.float32) ** block_scale(streams_of[4], (NSQ, D, D), ((1, 8),), -0.2, 0.2)), 3.5321271782921956e-15, 3.5321270512372535e-14)
    square_teacher = draw_square_teacher(jax.random.fold_in(streams_of[14], 71), 0)
    feed_weights = draw_feed_weights(jax.random.fold_in(streams_of[14], 71), 0)
    feed_first = bell_draw(streams_of[7], (LAYERS, 2, D, FF), (0.03 / (D * (SAMPLES * MASKED) ** 0.5)), 5.7220458984375e-06, ((2, 8),), jnp.float32)
    feed_second = jnp.clip(jnp.exp(math.log(3.5321270512372535e-14) - 2.3025851 * jax.random.uniform(streams_of[8], (LAYERS, 2, D, FF), jnp.float32) ** block_scale(streams_of[8], (LAYERS, 2, D, FF), ((2, 8),), -0.2, 0.2)), 3.5321271782921956e-15, 3.5321270512372535e-14)
    feed_teacher = draw_feed_teacher(jax.random.fold_in(streams_of[14], 71), 0)
    vector_weights = draw_vector_weights(jax.random.fold_in(streams_of[14], 71), 0)
    vector_first = bell_draw(streams_of[11], (NVEC, D), (0.03 / (D * (SAMPLES * MASKED) ** 0.5)), 5.7220458984375e-06, ((1, 8),), jnp.float32)
    vector_second = jnp.clip(jnp.exp(math.log(3.5321270512372535e-14) - 2.3025851 * jax.random.uniform(streams_of[12], (NVEC, D), jnp.float32) ** block_scale(streams_of[12], (NVEC, D), ((1, 8),), -0.2, 0.2)), 3.5321271782921956e-15, 3.5321270512372535e-14)
    vector_teacher = draw_vector_teacher(jax.random.fold_in(streams_of[14], 71), 0)
    return dict(patches=patches, mask_places=mask_places, square_weights=square_weights, square_first=square_first, square_second=square_second, square_teacher=square_teacher, feed_weights=feed_weights, feed_first=feed_first, feed_second=feed_second, feed_teacher=feed_teacher, vector_weights=vector_weights, vector_first=vector_first, vector_second=vector_second, vector_teacher=vector_teacher)


@jax.custom_vjp
def low(v):
    return lax.optimization_barrier(v.astype(jnp.bfloat16)).astype(jnp.float32)

@jax.custom_vjp
def low_back(v):
    return v

def low_keep(v):
    return (low(v), None)

def low_pass(kept, grad):
    return (grad,)

def back_keep(v):
    return (v, None)

def back_low(kept, grad):
    return (low(grad),)
low.defvjp(low_keep, low_pass)
low_back.defvjp(back_keep, back_low)
ln_eps = 1e-05
beta_one = 0.9
beta_two = 0.999
adam_eps = 1e-08
learn_rate = 0.01
decay_rate = 0.05
ema_keep = 0.999
huber_delta = 1.0
clip_scale = 1.25

def rounded_both(values):
    return low_back(low(values))

def product(left, right):
    return jnp.dot(left, right, precision=lax.Precision.HIGHEST, preferred_element_type=jnp.float32)

def layer_norm(values, gain, shift):
    centred = values - lax.optimization_barrier(jnp.mean(values, axis=-1, keepdims=True))
    variance = lax.optimization_barrier(jnp.mean(centred * centred, axis=-1, keepdims=True))
    return centred * lax.rsqrt(variance + ln_eps) * gain + shift

def gelu_exact(values):
    return jax.nn.gelu(values, approximate=False)

def attention(query, key_rows, value_rows, group_size):
    head_dim = D // HEADS
    scaling = head_dim ** (-0.5)
    query_heads = query.reshape(group_size, SEQ, HEADS, head_dim)
    key_heads = key_rows.reshape(group_size, SEQ, HEADS, head_dim)
    value_heads = value_rows.reshape(group_size, SEQ, HEADS, head_dim)
    scores = low_back(jnp.einsum('sqhe,skhe->shqk', query_heads, key_heads, precision=lax.Precision.HIGHEST) * scaling)
    soft_weights = low(jax.nn.softmax(scores, axis=-1))
    attended = jnp.einsum('shqk,skhe->sqhe', soft_weights, value_heads, precision=lax.Precision.HIGHEST)
    return rounded_both(attended.reshape(group_size * SEQ, D))

def run_layer(hidden, square, feed, vector, layer_index, group_size):
    base = 2 + SEQ + 12 * layer_index
    matrices = low(square[1 + 4 * layer_index:5 + 4 * layer_index])
    feed_pair = low(feed[layer_index])
    hidden_low = low(hidden)
    query = rounded_both(product(hidden_low, matrices[0]) + vector[base])
    key_rows = rounded_both(product(hidden_low, matrices[1]))
    value_rows = rounded_both(product(hidden_low, matrices[2]) + vector[base + 1])
    attended = attention(query, key_rows, value_rows, group_size)
    branch = low_back(product(attended, matrices[3]) + vector[base + 2])
    normed = layer_norm(hidden + branch, vector[base + 3], vector[base + 4])
    pre_act = low_back(product(low(normed), feed_pair[0]) + vector[base + 8:base + 12].reshape(-1))
    activation = low(gelu_exact(pre_act))
    branch_two = low_back(product(activation, feed_pair[1].T) + vector[base + 5])
    return (layer_norm(normed + branch_two, vector[base + 6], vector[base + 7]), branch_two)

def instance_norm(values, group_size):
    blocks = values.reshape(group_size, SEQ, D)
    centred = blocks - lax.optimization_barrier(jnp.mean(blocks, axis=1, keepdims=True))
    variance = lax.optimization_barrier(jnp.mean(centred * centred, axis=1, keepdims=True))
    return (centred * lax.rsqrt(variance + ln_eps)).reshape(group_size * SEQ, D)

def teacher_targets(square, feed, vector, patch_rows, group_size):
    embed = product(patch_rows, low(square[0])) + vector[0]
    hidden = (embed.reshape(group_size, SEQ, D) + vector[2:2 + SEQ]).reshape(-1, D)
    target = jnp.zeros_like(hidden)
    for layer_index in range(LAYERS):
        hidden, branch_two = run_layer(hidden, square, feed, vector, layer_index, group_size)
        target = target + instance_norm(branch_two, group_size)
    return target * (1.0 / LAYERS)

def student_loss(square, feed, vector, patch_rows, mask_rows, target, group_size):
    embed = low_back(product(patch_rows, low(square[0])) + vector[0])
    masked = jnp.where(mask_rows > 0, vector[1], embed)
    hidden = (masked.reshape(group_size, SEQ, D) + vector[2:2 + SEQ]).reshape(-1, D)
    for layer_index in range(LAYERS):
        hidden, unused = run_layer(hidden, square, feed, vector, layer_index, group_size)
    final_base = 2 + SEQ + 12 * LAYERS
    final = layer_norm(hidden, vector[final_base], vector[final_base + 1])
    output = low_back(product(low(final), low(square[NSQ - 1])) + vector[final_base + 2])
    residue = output - target
    magnitude = jnp.abs(residue)
    huber_terms = jnp.where(magnitude <= huber_delta, 0.5 * residue * residue, huber_delta * (magnitude - 0.5 * huber_delta))
    return jnp.sum(huber_terms * mask_rows) * (1.0 / (SAMPLES * MASKED * D))

def adam_step(master, moment_one, moment_two, gradient, factor):
    clipped = gradient * factor
    one_new = beta_one * moment_one + (1.0 - beta_one) * clipped
    two_new = beta_two * moment_two + (1.0 - beta_two) * clipped * clipped
    one_hat = one_new / (1.0 - beta_one ** ADAM_STEP)
    two_hat = two_new / (1.0 - beta_two ** ADAM_STEP)
    step_value = -learn_rate * (one_hat / (jnp.sqrt(two_hat) + adam_eps) + decay_rate * master)
    return (step_value, one_new, two_new)

def teacher_move(master, teacher, step_value):
    return (1.0 - ema_keep) * (master - teacher + step_value)

def reference(patches, mask_places, square_weights, square_first, square_second, square_teacher, feed_weights, feed_first, feed_second, feed_teacher, vector_weights, vector_first, vector_second, vector_teacher):
    group_size = SAMP_DEV * N_REP
    group_count = SAMPLES // group_size
    places = jnp.arange(SEQ, dtype=jnp.int32)
    mask_ind = lax.optimization_barrier(jnp.sum((mask_places[:, :, None] == places[None, None, :]).astype(jnp.float32), axis=1))
    patch_groups = patches.astype(jnp.float32).reshape(group_count, group_size * SEQ, D)
    mask_groups = mask_ind.reshape(group_count, group_size * SEQ, 1)

    def group_step(carry, inputs):
        grad_square, grad_feed, grad_vector, loss_sum = carry
        patch_rows, mask_rows = inputs
        target = teacher_targets(square_teacher, feed_teacher, vector_teacher, patch_rows, group_size)

        def objective(square, feed, vector):
            return student_loss(square, feed, vector, patch_rows, mask_rows, target, group_size)
        loss_value, pullback = jax.vjp(objective, square_weights, feed_weights, vector_weights)
        part_square, part_feed, part_vector = pullback(jnp.ones((), jnp.float32))
        return ((grad_square + part_square, grad_feed + part_feed, grad_vector + part_vector, loss_sum + loss_value), None)
    start = (jnp.zeros_like(square_weights), jnp.zeros_like(feed_weights), jnp.zeros_like(vector_weights), jnp.zeros((), jnp.float32))
    (grad_square, grad_feed, grad_vector, loss_value), unused = lax.scan(group_step, start, (patch_groups, mask_groups))
    grad_norm = jnp.sqrt(jnp.sum(grad_square * grad_square) + jnp.sum(grad_feed * grad_feed) + jnp.sum(grad_vector * grad_vector))
    limit = clip_scale / math.sqrt(SAMPLES * MASKED)
    factor = limit / jnp.maximum(grad_norm, limit)
    square_step, square_one, square_two = adam_step(square_weights, square_first, square_second, grad_square, factor)
    feed_step, feed_one, feed_two = adam_step(feed_weights, feed_first, feed_second, grad_feed, factor)
    vector_step, vector_one, vector_two = adam_step(vector_weights, vector_first, vector_second, grad_vector, factor)
    square_moved = teacher_move(square_weights, square_teacher, square_step)
    feed_moved = teacher_move(feed_weights, feed_teacher, feed_step)
    vector_moved = teacher_move(vector_weights, vector_teacher, vector_step)
    return (loss_value, grad_norm, square_step, square_one, square_two, square_moved, feed_step, feed_one, feed_two, feed_moved, vector_step, vector_one, vector_two, vector_moved)
```

```python
import functools
import math

import jax
import jax.numpy as jnp
from jax import lax
from jax.experimental import pallas as pl
from jax.experimental.pallas import tpu as pltpu
from jax.sharding import PartitionSpec as P

HEADS = 12
ADAM_STEP = 10


ln_eps = 1e-05
beta_one = 0.9
beta_two = 0.999
adam_eps = 1e-08
learn_rate = 0.01
decay_rate = 0.05
ema_keep = 0.999
huber_delta = 1.0
clip_scale = 1.25

VMEM_LIMIT = 60 * 1024 * 1024
BF16 = jnp.bfloat16
F32 = jnp.float32


def to_low(values):
    return values.astype(BF16)


def matmul(left, right):
    return jnp.dot(left, right, preferred_element_type=F32)


def matmul_tn(left, right):
    return lax.dot_general(left, right, (((0,), (0,)), ((), ())), preferred_element_type=F32)


def matmul_nt(left, right):
    return lax.dot_general(left, right, (((1,), (1,)), ((), ())), preferred_element_type=F32)


tail_scale = 0.21
tail_terms = (
    0.08371158707086396,
    0.08506867712628283,
    0.06919339848407204,
    0.1248680487092072,
    -0.09391427181816406,
    0.34938494294095396,
    -0.3302388882989717,
    0.2835812219436135,
    -0.07165470896901999,
)


def gelu_exact(values):
    t = 1.0 / (1.0 + tail_scale * jnp.abs(values))
    tail = jnp.full_like(t, tail_terms[-1])
    for term in tail_terms[-2::-1]:
        tail = tail * t + term
    bell = jnp.exp(-0.5 * (values * values))
    tail = tail * t * bell
    normal = jnp.where(values < 0, tail, 1.0 - tail)
    return values * normal, normal + values * bell * (1.0 / math.sqrt(2.0 * math.pi))


def norm_parts(values):
    centred = values - jnp.mean(values, axis=-1, keepdims=True)
    inverse = lax.rsqrt(jnp.mean(centred * centred, axis=-1, keepdims=True) + ln_eps)
    return centred * inverse, inverse


def norm_back(grad, hat, inverse, gain):
    scaled = grad * gain
    return inverse * (
        scaled
        - jnp.mean(scaled, axis=-1, keepdims=True)
        - hat * jnp.mean(scaled * hat, axis=-1, keepdims=True)
    )


def any_spec():
    return pl.BlockSpec(memory_space=pl.ANY)


def vmem_spec():
    return pl.BlockSpec(memory_space=pltpu.VMEM)


def smem_spec():
    return pl.BlockSpec(memory_space=pltpu.SMEM)


def swap(values, stage):
    axis, bit = stage
    return lax.ppermute(values, axis, [(i, i ^ bit) for i in range(lax.axis_size(axis))])


def fsdp_bits():
    count = lax.axis_size("fsdp")
    return [1 << k for k in reversed(range(count.bit_length() - 1))]


def stage_order(kind):
    stages = [("fsdp", bit) for bit in fsdp_bits()]
    place = len(stages) if kind == 0 else len(stages) - 1
    return stages[:place] + [("rep", 2)] + stages[place:]


def gather_unit(mine, kind):
    arrays, labels = [mine], [[(0, 0)]]
    stages = stage_order(kind)
    for number, (axis, bit) in enumerate(stages):
        got = [swap(a, (axis, bit)) for a in arrays]
        moved = [
            [(u ^ bit, e) if axis == "rep" else (u, e ^ bit) for u, e in block] for block in labels
        ]
        if number < len(stages) - 1:
            arrays = [jnp.concatenate([arrays[0], got[0]], axis=0)]
            labels = [labels[0] + moved[0]]
        else:
            arrays, labels = arrays + got, labels + moved
    got = [swap(a, ("rep", 1)) for a in arrays]
    moved = [[(u ^ 1, e) for u, e in block] for block in labels]
    return arrays + got, labels + moved


class Group:
    def __init__(self, mine, kind, wide, where):
        self.arrays, self.labels = gather_unit(mine, kind)
        self.wide = wide
        self.rows, self.width = mine.shape
        count = lax.axis_size("fsdp")
        depth = self.rows * count
        self.shape = (depth, 4 * self.width) if wide else (4, depth, self.width)
        self.blocks = sum(len(block) for block in self.labels)
        if self.rows % 16:
            flat = jnp.concatenate(self.arrays, axis=0).reshape(-1, self.rows, self.width)
            order = [label for block in self.labels for label in block]
            place = {label: number for number, label in enumerate(order)}
            table = jnp.array(
                [[place[(u, e)] for e in range(count)] for u in range(4)], jnp.int32
            )
            units = jnp.arange(4, dtype=jnp.int32)[:, None] ^ where[0]
            owners = jnp.arange(count, dtype=jnp.int32)[None] ^ where[1]
            whole = flat[table[units, owners]].reshape(4, depth, self.width)
            if wide:
                whole = whole.transpose(1, 0, 2).reshape(depth, 4 * self.width)
            self.arrays, self.labels, self.blocks = [whole], None, 1

    def copies(self, where_ref, arrays, out, sems):
        if self.labels is None:
            return [pltpu.make_async_copy(arrays[0], out, sems.at[0])]
        rep, own = where_ref[0], where_ref[1]
        copies = []
        for array, block in zip(arrays, self.labels):
            for number, (u, e) in enumerate(block):
                unit = jnp.bitwise_xor(rep, u)
                rows = pl.ds(pl.multiple_of(jnp.bitwise_xor(own, e) * self.rows, 16), self.rows)
                if self.wide:
                    columns = pl.ds(pl.multiple_of(unit * self.width, 128), self.width)
                    target = out.at[rows, columns]
                else:
                    target = out.at[unit, rows, :]
                source = array.at[pl.ds(number * self.rows, self.rows), :]
                copies.append(pltpu.make_async_copy(source, target, sems.at[len(copies)]))
        return copies


class Loading:
    def __init__(self, copies, ref):
        self.pending, self.ref = copies, ref
        for copy in copies:
            copy.start()

    def __call__(self):
        for copy in self.pending:
            copy.wait()
        self.pending = []
        return self.ref


def call(body, name, where, groups, ins, outs, scratch=(), flops=0):
    sizes = [len(group.arrays) for group in groups]

    def kernel(where_ref, *refs):
        refs = list(refs)
        arrays = [[refs.pop(0) for _ in range(size)] for size in sizes]
        in_refs = [refs.pop(0) for _ in ins]
        out_refs = [refs.pop(0) for _ in outs]
        places = [refs.pop(0) for _ in groups]
        sems = [refs.pop(0) for _ in groups]
        loads = [
            Loading(group.copies(where_ref, given, place, sem), place)
            for group, given, place, sem in zip(groups, arrays, places, sems)
        ]
        body(where_ref, loads, in_refs, out_refs, refs)

    return pl.pallas_call(
        kernel,
        out_shape=tuple(jax.ShapeDtypeStruct(*out) for out in outs),
        in_specs=[smem_spec()] + [any_spec()] * sum(sizes) + [vmem_spec()] * len(ins),
        out_specs=(vmem_spec(),) * len(outs),
        scratch_shapes=[pltpu.VMEM(group.shape, BF16) for group in groups]
        + [pltpu.SemaphoreType.DMA((group.blocks,)) for group in groups]
        + list(scratch),
        compiler_params=pltpu.CompilerParams(vmem_limit_bytes=VMEM_LIMIT),
        cost_estimate=pl.CostEstimate(flops=flops, bytes_accessed=1 << 20, transcendentals=0),
        name=name,
    )(where, *[array for group in groups for array in group.arrays], *ins)


def vector_kernel(where_ref, pieces_ref, out_ref):
    count, width = pieces_ref.shape[0], pieces_ref.shape[3]
    for k in range(count):
        out_ref[:, :, k * width : (k + 1) * width] = pieces_ref[jnp.bitwise_xor(where_ref[1], k)]


def gather_vectors(mine, where):
    pieces = mine[None]
    for bit in reversed(fsdp_bits()):
        pieces = jnp.concatenate([pieces, swap(pieces, ("fsdp", bit))], axis=0)
    count, two, rows, width = pieces.shape
    return pl.pallas_call(
        vector_kernel,
        out_shape=jax.ShapeDtypeStruct((two, rows, count * width), mine.dtype),
        in_specs=[smem_spec(), vmem_spec()],
        out_specs=vmem_spec(),
        compiler_params=pltpu.CompilerParams(vmem_limit_bytes=VMEM_LIMIT),
        name="gather_vectors",
    )(where, pieces)


def reduce_order(kind):
    stages = [("fsdp", bit) for bit in reversed(fsdp_bits())]
    place = 0 if kind == 0 else 1
    return stages[:place] + [("rep", 2)] + stages[place:]


def grad_kernel(unit_of, kind_stages, rows, width, where_ref, *refs):
    count = len(unit_of)
    lefts, rights = refs[:count], refs[count : 2 * count]
    keep, send = refs[2 * count], refs[2 * count + 1]
    rep, own = where_ref[0], where_ref[1]
    owners = lefts[0].shape[1] // rows
    for pair in range(count):
        left = lefts[pair][...]
        for column, unit in unit_of[pair]:
            product = matmul_tn(left, rights[pair][:, column : column + width])
            shifted = jnp.bitwise_xor(rep, unit)
            for other, target in ((0, keep), (1, send)):

                @pl.when(jnp.bitwise_and(shifted, 1) == other)
                def _():
                    for f in range(owners):
                        apart = jnp.bitwise_xor(own, f)
                        position = 0
                        for axis, bit in kind_stages:
                            value = shifted if axis == "rep" else apart
                            position = position * 2 + jnp.where(
                                jnp.bitwise_and(value, bit) != 0, 1, 0
                            )
                        target[pl.ds(pl.multiple_of(position * rows, 8), rows), :] = product[
                            f * rows : (f + 1) * rows, :
                        ]


def unit_grads(pairs, unit_of, kind, width, where):
    depth = pairs[0][0].shape[1]
    rows = depth // lax.axis_size("fsdp")
    shape = jax.ShapeDtypeStruct((2 * depth, width), F32)
    flops = sum(2 * left.shape[0] * depth * width * len(units) for (left, _), units in zip(pairs, unit_of))
    return pl.pallas_call(
        functools.partial(grad_kernel, unit_of, reduce_order(kind), rows, width),
        out_shape=(shape, shape),
        in_specs=[smem_spec()] + [vmem_spec()] * (2 * len(pairs)),
        out_specs=(vmem_spec(), vmem_spec()),
        compiler_params=pltpu.CompilerParams(vmem_limit_bytes=VMEM_LIMIT),
        cost_estimate=pl.CostEstimate(
            flops=flops, bytes_accessed=16 * depth * width, transcendentals=0
        ),
        name="unit_grads",
    )(where, *[left for left, _ in pairs], *[right for _, right in pairs])


def reduce_units(keep, send, kind):
    got = swap(send, ("rep", 1))
    for stage in reduce_order(kind):
        half = keep.shape[0] // 2
        send = keep[half:] + got[half:]
        keep = keep[:half] + got[:half]
        got = swap(send, stage)
    return keep + got


def share_units(own):
    far = swap(own, ("rep", 2))
    near, cross = swap(own, ("rep", 1)), swap(far, ("rep", 1))
    return jnp.stack([own, near, far, cross])


def scores_of(query, key_rows, valid, scaling):
    scores = matmul_nt(query, key_rows) * scaling
    return jnp.where(valid, scores, -1e30)


def attention_kernel(seq_len, head_dim, q_ref, k_ref, v_ref, out_ref, log_ref):
    rows, model_width = q_ref.shape
    scaling = head_dim**-0.5
    valid = lax.broadcasted_iota(jnp.int32, (rows, rows), 1) < seq_len
    lane = lax.broadcasted_iota(jnp.int32, (rows, 2 * head_dim), 1)
    zero = jnp.zeros((rows, 2 * head_dim), BF16)
    for pair in range(model_width // (2 * head_dim)):
        columns = slice(pair * 2 * head_dim, (pair + 1) * 2 * head_dim)
        query, key_rows, values = q_ref[:, columns], k_ref[:, columns], v_ref[:, columns]
        results = []
        for sub in range(2):
            picked = lane >= head_dim if sub else lane < head_dim
            scores = scores_of(jnp.where(picked, query, zero), key_rows, valid, scaling)
            highest = jnp.max(scores, axis=-1, keepdims=True)
            logsum = highest + jnp.log(jnp.sum(jnp.exp(scores - highest), axis=-1, keepdims=True))
            log_ref[:, 2 * pair + sub : 2 * pair + sub + 1] = logsum
            results.append(matmul(to_low(jnp.exp(scores - logsum)), values))
        out_ref[:, columns] = to_low(jnp.where(lane < head_dim, results[0], results[1]))


def attention_forward(query, key_rows, value_rows, samples, seq_len):
    row_count, model_width = query.shape
    rows = row_count // samples
    head_dim = model_width // HEADS
    block = pl.BlockSpec((rows, model_width), lambda i: (i, 0))
    small = pl.BlockSpec((rows, 128), lambda i: (i, 0))
    return pl.pallas_call(
        functools.partial(attention_kernel, seq_len, head_dim),
        grid=(samples,),
        out_shape=(
            jax.ShapeDtypeStruct(query.shape, BF16),
            jax.ShapeDtypeStruct((row_count, 128), F32),
        ),
        in_specs=[block] * 3,
        out_specs=(block, small),
        compiler_params=pltpu.CompilerParams(vmem_limit_bytes=VMEM_LIMIT),
        cost_estimate=pl.CostEstimate(
            flops=4 * row_count * rows * model_width,
            bytes_accessed=8 * row_count * model_width,
            transcendentals=2 * row_count * rows * HEADS,
        ),
        name="attention",
    )(query, key_rows, value_rows)


def attention_back_kernel(
    seq_len, head_dim, q_ref, k_ref, v_ref, da_ref, log_ref, dq_ref, dk_ref, dv_ref
):
    rows, model_width = q_ref.shape
    scaling = head_dim**-0.5
    valid = lax.broadcasted_iota(jnp.int32, (rows, rows), 1) < seq_len
    lane = lax.broadcasted_iota(jnp.int32, (rows, 2 * head_dim), 1)
    zero = jnp.zeros((rows, 2 * head_dim), BF16)
    for pair in range(model_width // (2 * head_dim)):
        columns = slice(pair * 2 * head_dim, (pair + 1) * 2 * head_dim)
        query, key_rows = q_ref[:, columns], k_ref[:, columns]
        values, grad = v_ref[:, columns], da_ref[:, columns]
        results = []
        for sub in range(2):
            picked = lane >= head_dim if sub else lane < head_dim
            scores = scores_of(jnp.where(picked, query, zero), key_rows, valid, scaling)
            soft = jnp.exp(scores - log_ref[:, 2 * pair + sub : 2 * pair + sub + 1])
            grad_soft = matmul_nt(jnp.where(picked, grad, zero), values)
            total = jnp.sum(grad_soft * soft, axis=-1, keepdims=True)
            grad_scores = to_low(soft * (grad_soft - total))
            results.append(
                (
                    matmul(grad_scores, key_rows) * scaling,
                    matmul_tn(grad_scores, query) * scaling,
                    matmul_tn(to_low(soft), grad),
                )
            )
        for target, first, second in zip((dq_ref, dk_ref, dv_ref), *results):
            target[:, columns] = to_low(jnp.where(lane < head_dim, first, second))


def attention_backward(query, key_rows, value_rows, logsum, grad, samples, seq_len):
    row_count, model_width = query.shape
    rows = row_count // samples
    head_dim = model_width // HEADS
    block = pl.BlockSpec((rows, model_width), lambda i: (i, 0))
    small = pl.BlockSpec((rows, 128), lambda i: (i, 0))
    return pl.pallas_call(
        functools.partial(attention_back_kernel, seq_len, head_dim),
        grid=(samples,),
        out_shape=(jax.ShapeDtypeStruct(query.shape, BF16),) * 3,
        in_specs=[block] * 4 + [small],
        out_specs=(block,) * 3,
        compiler_params=pltpu.CompilerParams(vmem_limit_bytes=VMEM_LIMIT),
        cost_estimate=pl.CostEstimate(
            flops=10 * row_count * rows * model_width,
            bytes_accessed=14 * row_count * model_width,
            transcendentals=row_count * rows * HEADS,
        ),
        name="attention_back",
    )(query, key_rows, value_rows, grad, logsum)


TILE = 256


def tiles(width, body):
    def step(number, carry):
        body(pl.ds(pl.multiple_of(number * TILE, TILE), TILE))
        return carry

    lax.fori_loop(0, width // TILE, step, 0)


def embed_body(samples, masked, base, where_ref, loads, ins, outs, scratch):
    patch_ref, vec_ref, pos_ref = ins[:3]
    hid_ref, low_ref, q_ref, k_ref, v_ref = outs
    weights = loads[0]()
    rows = patch_ref.shape[0] // samples
    width = patch_ref.shape[1]

    def embed(columns):
        product = matmul(patch_ref[...], weights[0, :, columns]) + vec_ref[0:1, columns]
        if masked:
            product = jnp.where(ins[3][...] > 0, vec_ref[1:2, columns], product)
        for s in range(samples):
            part = product[s * rows : (s + 1) * rows] + pos_ref[:, columns]
            hid_ref[s * rows : (s + 1) * rows, columns] = part
            low_ref[s * rows : (s + 1) * rows, columns] = to_low(part)

    tiles(width, embed)

    def project(columns):
        low = low_ref[...]
        q_ref[:, columns] = to_low(
            matmul(low, weights[1, :, columns]) + vec_ref[base : base + 1, columns]
        )
        k_ref[:, columns] = to_low(matmul(low, weights[2, :, columns]))
        v_ref[:, columns] = to_low(
            matmul(low, weights[3, :, columns]) + vec_ref[base + 1 : base + 2, columns]
        )

    tiles(width, project)


def feed_forward(samples, base, unit, loads, ins, student, refs):
    att_ref, hid_ref, vec_ref = ins
    sum_ref, low_ref, act_ref = refs[:3]
    rows, width = hid_ref.shape[0] // samples, hid_ref.shape[1]
    squares = loads[0]()

    def project(columns):
        sum_ref[:, columns] = (
            hid_ref[:, columns]
            + matmul(att_ref[...], squares[unit, :, columns])
            + vec_ref[base + 2 : base + 3, columns]
        )

    tiles(width, project)
    for s in range(samples):
        part = slice(s * rows, (s + 1) * rows)
        hat, inverse = norm_parts(sum_ref[part, :])
        if student:
            refs[3][part, :], refs[4][part, :] = hat, inverse
        normed = hat * vec_ref[base + 3 : base + 4, :] + vec_ref[base + 4 : base + 5, :]
        sum_ref[part, :] = normed
        low_ref[part, :] = to_low(normed)
    up = loads[1]()
    hidden_units = up.shape[1]

    def widen(columns, bias):
        pre_act = matmul(low_ref[...], up[:, columns]) + bias
        value, slope = gelu_exact(pre_act)
        act_ref[:, columns] = to_low(value)
        if student:
            refs[5][:, columns] = slope

    for quarter in range(4):
        size = hidden_units // 4

        def step(number, carry, quarter=quarter):
            inner = pl.ds(pl.multiple_of(number * TILE, TILE), TILE)
            outer = pl.ds(pl.multiple_of(quarter * size + number * TILE, TILE), TILE)
            widen(outer, vec_ref[base + 8 + quarter : base + 9 + quarter, inner])
            return carry

        lax.fori_loop(0, size // TILE, step, 0)
    down = loads[2]()

    def narrow(columns, target_ref, residual):
        branch = (
            matmul_nt(act_ref[...], down[columns, :]) + vec_ref[base + 5 : base + 6, columns]
        )
        target_ref[:, columns] = sum_ref[:, columns] + branch if residual else branch

    return narrow


def teacher_body(samples, seq_len, base, where_ref, loads, ins, outs, scratch):
    target_ref = outs[0]
    narrow = feed_forward(samples, base, 0, loads, ins, False, scratch)
    rows, width = target_ref.shape[0] // samples, target_ref.shape[1]
    tiles(width, lambda columns: narrow(columns, target_ref, False))
    valid = lax.broadcasted_iota(jnp.int32, (rows, width), 0) < seq_len
    for s in range(samples):
        part = slice(s * rows, (s + 1) * rows)
        values = target_ref[part, :]
        total = jnp.sum(jnp.where(valid, values, 0.0), axis=0, keepdims=True)
        centred = values - total * (1.0 / seq_len)
        spread = jnp.sum(jnp.where(valid, centred * centred, 0.0), axis=0, keepdims=True)
        target_ref[part, :] = centred * lax.rsqrt(spread * (1.0 / seq_len) + ln_eps)


def student_body(samples, base, loss_scale, where_ref, loads, ins, outs, scratch):
    target_ref, mask_ref = ins[3:]
    final_ref, dy_ref, gb2_ref, g2_ref, act_ref, slope_ref, low_ref, hat_ref, inv_ref = outs[:9]
    rows_ref, loss_ref = outs[9:]
    sum_ref, hat2_ref, hatf_ref, gf_ref, inv2_ref, invf_ref = scratch
    narrow = feed_forward(
        samples, base, 1, loads, ins[:3], True, (sum_ref, low_ref, act_ref, hat_ref, inv_ref, slope_ref)
    )
    vec_ref = ins[2]
    squares = loads[0]()
    width = sum_ref.shape[1]
    rows = sum_ref.shape[0] // samples
    final_base = base + 12
    tiles(width, lambda columns: narrow(columns, gf_ref, True))
    for s in range(samples):
        part = slice(s * rows, (s + 1) * rows)
        hat, inverse = norm_parts(gf_ref[part, :])
        hat2_ref[part, :], inv2_ref[part, :] = hat, inverse
        result = hat * vec_ref[base + 6 : base + 7, :] + vec_ref[base + 7 : base + 8, :]
        hat, inverse = norm_parts(result)
        hatf_ref[part, :], invf_ref[part, :] = hat, inverse
        final_ref[part, :] = to_low(
            hat * vec_ref[final_base : final_base + 1, :]
            + vec_ref[final_base + 1 : final_base + 2, :]
        )
    rows_ref[...] = jnp.zeros_like(rows_ref)
    loss_ref[...] = jnp.zeros_like(loss_ref)

    def head(columns):
        output = matmul(final_ref[...], squares[2, :, columns])
        residue = output + vec_ref[final_base + 2 : final_base + 3, columns] - target_ref[:, columns]
        magnitude = jnp.abs(residue)
        terms = jnp.where(
            magnitude <= huber_delta,
            0.5 * residue * residue,
            huber_delta * (magnitude - 0.5 * huber_delta),
        )
        loss_ref[...] += jnp.sum(
            jnp.sum(terms * mask_ref[...], axis=0, keepdims=True), axis=1, keepdims=True
        )
        grad = to_low(jnp.clip(residue, -huber_delta, huber_delta) * mask_ref[...] * loss_scale)
        dy_ref[:, columns] = grad
        rows_ref[0:1, columns] = jnp.sum(grad.astype(F32), axis=0, keepdims=True)

    tiles(width, head)

    def back(columns):
        gf_ref[:, columns] = matmul_nt(dy_ref[...], squares[2, columns, :])

    tiles(width, back)
    for s in range(samples):
        part = slice(s * rows, (s + 1) * rows)
        grad, hat = gf_ref[part, :], hatf_ref[part, :]
        rows_ref[1:2, :] += jnp.sum(grad * hat, axis=0, keepdims=True)
        rows_ref[2:3, :] += jnp.sum(grad, axis=0, keepdims=True)
        grad = norm_back(grad, hat, invf_ref[part, :], vec_ref[final_base : final_base + 1, :])
        hat = hat2_ref[part, :]
        rows_ref[3:4, :] += jnp.sum(grad * hat, axis=0, keepdims=True)
        rows_ref[4:5, :] += jnp.sum(grad, axis=0, keepdims=True)
        grad = norm_back(grad, hat, inv2_ref[part, :], vec_ref[base + 6 : base + 7, :])
        g2_ref[part, :] = grad
        low = to_low(grad)
        gb2_ref[part, :] = low
        rows_ref[5:6, :] += jnp.sum(low.astype(F32), axis=0, keepdims=True)


def feed_back_body(samples, base, where_ref, loads, ins, outs, scratch):
    gb2_ref, g2_ref, slope_ref, hat_ref, inv_ref, vec_ref = ins
    gpre_ref, gfirst_ref, gbranch_ref, gatt_ref, rows_ref, up_ref = outs
    grad_ref = scratch[0]
    squares, up, down = loads
    down = down()
    width, hidden_units = down.shape
    rows = gb2_ref.shape[0] // samples

    def widen(columns):
        grad = to_low(matmul(gb2_ref[...], down[:, columns]) * slope_ref[:, columns])
        gpre_ref[:, columns] = grad
        up_ref[:, columns] = jnp.sum(grad.astype(F32), axis=0, keepdims=True)

    tiles(hidden_units, widen)
    up = up()

    def narrow(columns):
        grad_ref[:, columns] = g2_ref[:, columns] + matmul_nt(gpre_ref[...], up[columns, :])

    tiles(width, narrow)
    rows_ref[...] = jnp.zeros_like(rows_ref)
    for s in range(samples):
        part = slice(s * rows, (s + 1) * rows)
        grad, hat = grad_ref[part, :], hat_ref[part, :]
        rows_ref[0:1, :] += jnp.sum(grad * hat, axis=0, keepdims=True)
        rows_ref[1:2, :] += jnp.sum(grad, axis=0, keepdims=True)
        grad = norm_back(grad, hat, inv_ref[part, :], vec_ref[base + 3 : base + 4, :])
        gfirst_ref[part, :] = grad
        low = to_low(grad)
        gbranch_ref[part, :] = low
        rows_ref[2:3, :] += jnp.sum(low.astype(F32), axis=0, keepdims=True)
    squares = squares()

    def project(columns):
        gatt_ref[:, columns] = to_low(matmul_nt(gbranch_ref[...], squares[1, columns, :]))

    tiles(width, project)


def embed_back_body(samples, seq_len, base, where_ref, loads, ins, outs, scratch):
    gq_ref, gk_ref, gv_ref, gfirst_ref, mask_ref, after_ref, inner_ref, up_ref = ins
    ge_ref, pieces_ref = outs
    all_ref, pos_ref = scratch
    weights = loads[0]()
    width = gq_ref.shape[1]
    rows = gq_ref.shape[0] // samples

    def project(columns):
        grad = gfirst_ref[:, columns] + matmul_nt(gq_ref[...], weights[1, columns, :])
        grad += matmul_nt(gk_ref[...], weights[2, columns, :])
        grad += matmul_nt(gv_ref[...], weights[3, columns, :])
        hidden = grad * mask_ref[...]
        all_ref[1:2, columns] = jnp.sum(hidden, axis=0, keepdims=True)
        low = to_low(grad * (1.0 - mask_ref[...]))
        ge_ref[:, columns] = low
        all_ref[0:1, columns] = jnp.sum(low.astype(F32), axis=0, keepdims=True)
        total = grad[0:rows]
        for s in range(1, samples):
            total += grad[s * rows : (s + 1) * rows]
        pos_ref[:, columns] = total
        all_ref[base : base + 1, columns] = jnp.sum(
            gq_ref[:, columns].astype(F32), axis=0, keepdims=True
        )
        all_ref[base + 1 : base + 2, columns] = jnp.sum(
            gv_ref[:, columns].astype(F32), axis=0, keepdims=True
        )

    tiles(width, project)
    all_ref[2 : 2 + seq_len, :] = pos_ref[0:seq_len, :]
    all_ref[base + 2 : base + 3, :] = inner_ref[2:3, :]
    all_ref[base + 3 : base + 5, :] = inner_ref[0:2, :]
    all_ref[base + 5 : base + 6, :] = after_ref[5:6, :]
    all_ref[base + 6 : base + 8, :] = after_ref[3:5, :]
    for k in range(4):
        all_ref[base + 8 + k : base + 9 + k, :] = up_ref[:, k * width : (k + 1) * width]
    all_ref[base + 12 : base + 14, :] = after_ref[1:3, :]
    all_ref[base + 14 : base + 15, :] = after_ref[0:1, :]
    count, _, size = pieces_ref.shape
    for k in range(count):
        pieces_ref[jnp.bitwise_xor(where_ref[1], k)] = all_ref[:, k * size : (k + 1) * size]


def adam_step(master, moment_one, moment_two, gradient, factor):
    clipped = gradient * factor
    one_new = beta_one * moment_one + (1.0 - beta_one) * clipped
    two_new = beta_two * moment_two + (1.0 - beta_two) * clipped * clipped
    one_hat = one_new / (1.0 - beta_one**ADAM_STEP)
    two_hat = two_new / (1.0 - beta_two**ADAM_STEP)
    step_value = -learn_rate * (one_hat / (jnp.sqrt(two_hat) + adam_eps) + decay_rate * master)
    return (step_value, one_new, two_new)


def teacher_move(master, teacher, step_value):
    return (1.0 - ema_keep) * (master - teacher + step_value)


def per_device(
    patches,
    mask_places,
    square_weights,
    square_first,
    square_second,
    square_teacher,
    feed_weights,
    feed_first,
    feed_second,
    feed_teacher,
    vector_weights,
    vector_first,
    vector_second,
    vector_teacher,
):
    samples, seq_len, model_width = patches.shape
    total_masked = samples * mask_places.shape[1] * lax.axis_size("rep") * lax.axis_size("fsdp")
    rep, own = lax.axis_index("rep"), lax.axis_index("fsdp")
    where = jnp.stack([rep, own]).astype(jnp.int32)
    pad_len = -(-seq_len // 8) * 8
    row_count = samples * pad_len
    hidden_units = feed_weights.shape[3]
    patch_rows = jnp.pad(patches, ((0, 0), (0, pad_len - seq_len), (0, 0))).reshape(
        row_count, model_width
    )
    places = jnp.arange(pad_len, dtype=jnp.int32)
    mask_rows = jnp.sum(
        (mask_places[:, :, None] == places[None, None, :]).astype(F32), axis=1
    ).reshape(row_count, 1)

    def pick(array, index):
        return to_low(lax.dynamic_index_in_dim(array, index, keepdims=False))

    def columns_of(array, number):
        width = array.shape[3] // 4
        return to_low(lax.dynamic_slice_in_dim(array[0, number], rep * width, width, axis=1))

    vector_old_new = gather_vectors(jnp.stack([vector_weights, vector_teacher]), where)
    vector_all, vector_old = vector_old_new[0], vector_old_new[1]
    entry_t = Group(pick(square_teacher, rep), 0, False, where)
    entry_s = Group(pick(square_weights, rep), 1, False, where)
    others = jnp.where(
        rep == 0, to_low(square_teacher[4]), pick(square_weights, jnp.clip(rep + 3, 4, 5))
    )
    outer = Group(others, 0, False, where)
    up_t = Group(columns_of(feed_teacher, 0), 1, True, where)
    down_t = Group(columns_of(feed_teacher, 1), 0, True, where)
    up_s = Group(columns_of(feed_weights, 0), 1, True, where)
    down_s = Group(columns_of(feed_weights, 1), 0, True, where)
    base = 2 + seq_len
    wide, square = 2 * row_count * model_width * hidden_units, 2 * row_count * model_width**2

    def positions(vector):
        return jnp.pad(vector[2 : 2 + seq_len], ((0, pad_len - seq_len), (0, 0)))

    full, low_full = ((row_count, model_width), F32), ((row_count, model_width), BF16)
    low_wide, full_wide = ((row_count, hidden_units), BF16), ((row_count, hidden_units), F32)
    column = ((row_count, 1), F32)

    def entry(group, vector, masked, name):
        return call(
            functools.partial(embed_body, samples, masked, base),
            name,
            where,
            [group],
            [patch_rows, vector, positions(vector)] + ([mask_rows] if masked else []),
            [full] + [low_full] * 4,
            flops=4 * square,
        )

    hidden_t, _, query, key_rows, value_rows = entry(entry_t, vector_old, False, "embed_t")
    attended, _ = attention_forward(query, key_rows, value_rows, samples, seq_len)
    (target,) = call(
        functools.partial(teacher_body, samples, seq_len, base),
        "layer_t",
        where,
        [outer, up_t, down_t],
        [attended, hidden_t, vector_old],
        [full],
        [pltpu.VMEM(*full), pltpu.VMEM(*low_full), pltpu.VMEM(*low_wide)],
        flops=square + 2 * wide,
    )
    hidden, hidden_low, query, key_rows, value_rows = entry(entry_s, vector_all, True, "embed_s")
    attended, logsum = attention_forward(query, key_rows, value_rows, samples, seq_len)
    loss_scale = 1.0 / (total_masked * model_width)
    (
        final_low,
        grad_output,
        grad_branch_two,
        grad_second,
        activation,
        slope,
        normed_low,
        hat_first,
        inverse_first,
        rows_after,
        loss_sum,
    ) = call(
        functools.partial(student_body, samples, base, loss_scale),
        "layer_s",
        where,
        [outer, up_s, down_s],
        [attended, hidden, vector_all, target, mask_rows],
        [low_full] * 3
        + [full, low_wide, full_wide, low_full, full, column, ((8, model_width), F32), ((1, 1), F32)],
        [pltpu.VMEM(*full)] * 4 + [pltpu.VMEM(*column)] * 2,
        flops=3 * square + 2 * wide,
    )
    loss_local = loss_sum[0, 0] * loss_scale

    unit = model_width
    quarters = [[(k * unit, k) for k in range(4)]]
    down_g = unit_grads([(grad_branch_two, activation)], quarters, 0, unit, where)
    grad_branch_two, *down_g = lax.optimization_barrier((grad_branch_two, *down_g))
    grad_pre, grad_first, grad_branch, grad_attended, rows_inner, rows_up = call(
        functools.partial(feed_back_body, samples, base),
        "feed_back",
        where,
        [outer, up_s, down_s],
        [grad_branch_two, grad_second, slope, hat_first, inverse_first, vector_all],
        [low_wide, full, low_full, low_full, ((8, model_width), F32), ((1, hidden_units), F32)],
        [pltpu.VMEM(*full)],
        flops=square + 2 * wide,
    )
    up_g = unit_grads([(normed_low, grad_pre)], quarters, 1, unit, where)
    halves = [[(0, 0), (unit // 2, 1)], [(0, 2), (unit // 2, 3)]]
    edge_g = unit_grads(
        [(final_low, grad_output), (attended, grad_branch)], halves, 0, unit // 2, where
    )
    grad_attended, *both = lax.optimization_barrier((grad_attended, *up_g, *edge_g))
    up_g, edge_g = both[:2], both[2:]
    grad_query, grad_key, grad_value = attention_backward(
        query, key_rows, value_rows, logsum, grad_attended, samples, seq_len
    )
    vector_count = vector_all.shape[0]
    count = lax.axis_size("fsdp")
    grad_embed, pieces = call(
        functools.partial(embed_back_body, samples, seq_len, base),
        "embed_back",
        where,
        [entry_s],
        [grad_query, grad_key, grad_value, grad_first, mask_rows, rows_after, rows_inner, rows_up],
        [low_full, ((count, vector_count, model_width // count), F32)],
        [pltpu.VMEM((vector_count, model_width), F32), pltpu.VMEM((pad_len, model_width), F32)],
        flops=3 * square,
    )
    singles = [[(0, k)] for k in range(4)]
    qkv_g = unit_grads(
        [(hidden_low, grad_query), (hidden_low, grad_key), (hidden_low, grad_value), (patch_rows, grad_embed)],
        singles,
        1,
        unit,
        where,
    )

    down_own = reduce_units(*down_g, 0)
    up_own = reduce_units(*up_g, 1)
    edge_own = reduce_units(*edge_g, 0)
    qkv_own = reduce_units(*qkv_g, 1)
    for bit in fsdp_bits():
        half = pieces.shape[0] // 2
        pieces = pieces[:half] + swap(pieces[half:], ("fsdp", bit))
    vector_share = pieces[0]
    for bit in (2, 1):
        vector_share = vector_share + swap(vector_share, ("rep", bit))
    squares_own = (
        jnp.sum(down_own * down_own)
        + jnp.sum(up_own * up_own)
        + jnp.sum(edge_own * edge_own)
        + jnp.sum(qkv_own * qkv_own)
        + 0.25 * jnp.sum(vector_share * vector_share)
    )
    totals = jnp.stack([squares_own, loss_local])
    for bit in fsdp_bits():
        totals = totals + swap(totals, ("fsdp", bit))
    for bit in (2, 1):
        totals = totals + swap(totals, ("rep", bit))
    norm_squared, loss_value = totals[0], totals[1]

    def ordered(own_units):
        shared = share_units(own_units)
        return [lax.dynamic_index_in_dim(shared, rep ^ k, keepdims=False) for k in range(4)]

    down_u, up_u, edge_u, qkv_u = ordered(down_own), ordered(up_own), ordered(edge_own), ordered(qkv_own)
    feed_grad = jnp.stack([jnp.concatenate(up_u, axis=1), jnp.concatenate(down_u, axis=1)])[None]
    square_grad = jnp.stack(
        [
            qkv_u[3],
            qkv_u[0],
            qkv_u[1],
            qkv_u[2],
            jnp.concatenate(edge_u[2:], axis=1),
            jnp.concatenate(edge_u[:2], axis=1),
        ]
    )
    grad_norm = jnp.sqrt(norm_squared)
    limit = clip_scale / math.sqrt(total_masked)
    factor = limit / jnp.maximum(grad_norm, limit)
    square_step, square_one, square_two = adam_step(
        square_weights, square_first, square_second, square_grad, factor
    )
    feed_step, feed_one, feed_two = adam_step(
        feed_weights, feed_first, feed_second, feed_grad, factor
    )
    vector_step, vector_one, vector_two = adam_step(
        vector_weights, vector_first, vector_second, vector_share, factor
    )
    square_moved = teacher_move(square_weights, square_teacher, square_step)
    feed_moved = teacher_move(feed_weights, feed_teacher, feed_step)
    vector_moved = teacher_move(vector_weights, vector_teacher, vector_step)
    return (
        loss_value,
        grad_norm,
        square_step,
        square_one,
        square_two,
        square_moved,
        feed_step,
        feed_one,
        feed_two,
        feed_moved,
        vector_step,
        vector_one,
        vector_two,
        vector_moved,
    )


def solution(mesh):
    placed = (
        P(("rep", "fsdp"), None, None),
        P(("rep", "fsdp"), None),
        P(None, "fsdp", None),
        P(None, "fsdp", None),
        P(None, "fsdp", None),
        P(None, "fsdp", None),
        P(None, None, "fsdp", None),
        P(None, None, "fsdp", None),
        P(None, None, "fsdp", None),
        P(None, None, "fsdp", None),
        P(None, "fsdp"),
        P(None, "fsdp"),
        P(None, "fsdp"),
        P(None, "fsdp"),
    )
    return jax.shard_map(
        per_device,
        mesh=mesh,
        in_specs=placed,
        out_specs=(
            P(),
            P(),
            P(None, "fsdp", None),
            P(None, "fsdp", None),
            P(None, "fsdp", None),
            P(None, "fsdp", None),
            P(None, None, "fsdp", None),
            P(None, None, "fsdp", None),
            P(None, None, "fsdp", None),
            P(None, None, "fsdp", None),
            P(None, "fsdp"),
            P(None, "fsdp"),
            P(None, "fsdp"),
            P(None, "fsdp"),
        ),
        check_vma=False,
    )
```

```python
import functools
import math

import jax
import jax.numpy as jnp
from jax import lax
from jax.experimental import pallas as pl
from jax.experimental.pallas import tpu as pltpu
from jax.sharding import PartitionSpec as P

HEADS = 12
ADAM_STEP = 10


ln_eps = 1e-05
beta_one = 0.9
beta_two = 0.999
adam_eps = 1e-08
learn_rate = 0.01
decay_rate = 0.05
ema_keep = 0.999
huber_delta = 1.0
clip_scale = 1.25

VMEM_LIMIT = 60 * 1024 * 1024
SMALL = pl.CostEstimate(flops=0, bytes_accessed=1024, transcendentals=0)
BF16 = jnp.bfloat16
F32 = jnp.float32


def to_low(values):
    return values.astype(BF16)


def matmul(left, right):
    return jnp.dot(left, right, preferred_element_type=F32)


def matmul_tn(left, right):
    return lax.dot_general(left, right, (((0,), (0,)), ((), ())), preferred_element_type=F32)


def matmul_nt(left, right):
    return lax.dot_general(left, right, (((1,), (1,)), ((), ())), preferred_element_type=F32)


tail_scale = 0.21
tail_terms = (
    0.08371158707086396,
    0.08506867712628283,
    0.06919339848407204,
    0.1248680487092072,
    -0.09391427181816406,
    0.34938494294095396,
    -0.3302388882989717,
    0.2835812219436135,
    -0.07165470896901999,
)


def gelu_exact(values):
    t = 1.0 / (1.0 + tail_scale * jnp.abs(values))
    tail = jnp.full_like(t, tail_terms[-1])
    for term in tail_terms[-2::-1]:
        tail = tail * t + term
    bell = jnp.exp(-0.5 * (values * values))
    tail = tail * t * bell
    normal = jnp.where(values < 0, tail, 1.0 - tail)
    return values * normal, normal + values * bell * (1.0 / math.sqrt(2.0 * math.pi))


def norm_parts(values):
    centred = values - jnp.mean(values, axis=-1, keepdims=True)
    inverse = lax.rsqrt(jnp.mean(centred * centred, axis=-1, keepdims=True) + ln_eps)
    return centred * inverse, inverse


def norm_back(grad, hat, inverse, gain):
    scaled = grad * gain
    return inverse * (
        scaled
        - jnp.mean(scaled, axis=-1, keepdims=True)
        - hat * jnp.mean(scaled * hat, axis=-1, keepdims=True)
    )


def any_spec():
    return pl.BlockSpec(memory_space=pl.ANY)


def vmem_spec():
    return pl.BlockSpec(memory_space=pltpu.VMEM)


def smem_spec():
    return pl.BlockSpec(memory_space=pltpu.SMEM)


def swap(values, stage):
    axis, bit = stage
    return lax.ppermute(values, axis, [(i, i ^ bit) for i in range(lax.axis_size(axis))])


def fsdp_bits():
    count = lax.axis_size("fsdp")
    return [1 << k for k in reversed(range(count.bit_length() - 1))]


def stage_order(kind):
    stages = [("fsdp", bit) for bit in fsdp_bits()]
    place = len(stages) if kind == 0 else len(stages) - 1
    return stages[:place] + [("rep", 2)] + stages[place:]


def tie(*values):
    return lax.optimization_barrier(values)


class Group:
    def __init__(self, mine, kind, wide, where, before=None):
        self.wide, self.where = wide, where
        self.rows, self.width = mine.shape
        count = lax.axis_size("fsdp")
        depth = self.rows * count
        self.shape = (depth, 4 * self.width) if wide else (4, depth, self.width)
        self.blocks = 4 * count
        if before is not None:
            mine, before.arrays[0] = tie(mine, before.arrays[0])
        self.arrays, self.labels = [mine], [[(0, 0)]]
        self.stages = stage_order(kind)
        self.step()

    def step(self):
        axis, bit = self.stages.pop(0)
        got = swap(self.arrays[0], (axis, bit))
        moved = [
            (u ^ bit, e) if axis == "rep" else (u, e ^ bit) for u, e in self.labels[0]
        ]
        if self.stages:
            self.arrays = [jnp.concatenate([self.arrays[0], got], axis=0)]
            self.labels = [self.labels[0] + moved]
        else:
            self.arrays, self.labels = self.arrays + [got], self.labels + [moved]

    def fabric(self):
        while self.stages:
            self.step()
        return self

    def finish(self):
        self.arrays = self.arrays + [swap(a, ("rep", 1)) for a in self.arrays]
        self.labels = self.labels + [[(u ^ 1, e) for u, e in block] for block in self.labels]
        if self.rows % 16:
            count = lax.axis_size("fsdp")
            flat = jnp.concatenate(self.arrays, axis=0).reshape(-1, self.rows, self.width)
            order = [label for block in self.labels for label in block]
            place = {label: number for number, label in enumerate(order)}
            table = jnp.array(
                [[place[(u, e)] for e in range(count)] for u in range(4)], jnp.int32
            )
            units = jnp.arange(4, dtype=jnp.int32)[:, None] ^ self.where[0]
            owners = jnp.arange(count, dtype=jnp.int32)[None] ^ self.where[1]
            whole = flat[table[units, owners]].reshape(4, -1, self.width)
            self.whole(whole)
        return self

    def whole(self, units):
        if self.wide:
            units = units.transpose(1, 0, 2).reshape(self.shape)
        self.arrays, self.labels, self.blocks = [units], None, 1

    def copies(self, where_ref, arrays, out, sems):
        if self.labels is None:
            return [pltpu.make_async_copy(arrays[0], out, sems.at[0])]
        rep, own = where_ref[0], where_ref[1]
        copies = []
        for array, block in zip(arrays, self.labels):
            for number, (u, e) in enumerate(block):
                unit = jnp.bitwise_xor(rep, u)
                rows = pl.ds(pl.multiple_of(jnp.bitwise_xor(own, e) * self.rows, 16), self.rows)
                if self.wide:
                    columns = pl.ds(pl.multiple_of(unit * self.width, 128), self.width)
                    target = out.at[rows, columns]
                else:
                    target = out.at[unit, rows, :]
                source = array.at[pl.ds(number * self.rows, self.rows), :]
                copies.append(pltpu.make_async_copy(source, target, sems.at[len(copies)]))
        return copies


class Gathered(Group):
    def __init__(self, gathered, number, groups, wide, where):
        count = lax.axis_size("fsdp")
        self.wide, self.where = wide, where
        self.rows, self.width = gathered.shape[0] // (4 * count * groups), gathered.shape[1]
        depth = self.rows * count
        self.shape = (depth, 4 * self.width) if wide else (4, depth, self.width)
        self.arrays, self.labels, self.blocks = [gathered], (), 4 * count
        self.number, self.groups = number, groups
        if self.rows % 16:
            blocks = gathered.reshape(count, 4, groups, self.rows, self.width)[:, :, number]
            self.whole(blocks.transpose(1, 0, 2, 3).reshape(4, depth, self.width))

    def copies(self, where_ref, arrays, out, sems):
        if self.labels is None:
            return [pltpu.make_async_copy(arrays[0], out, sems.at[0])]
        copies = []
        for place in range(self.blocks):
            owner, unit = place // 4, place % 4
            rows = slice(owner * self.rows, (owner + 1) * self.rows)
            if self.wide:
                target = out.at[rows, unit * self.width : (unit + 1) * self.width]
            else:
                target = out.at[unit, rows, :]
            first = (place * self.groups + self.number) * self.rows
            source = arrays[0].at[first : first + self.rows, :]
            copies.append(pltpu.make_async_copy(source, target, sems.at[place]))
        return copies


class Loading:
    def __init__(self, copies, ref):
        self.pending, self.ref = copies, ref
        for copy in copies:
            copy.start()

    def __call__(self):
        for copy in self.pending:
            copy.wait()
        self.pending = []
        return self.ref


def call(body, name, where, groups, ins, outs, scratch=()):
    sizes = [len(group.arrays) for group in groups]

    def kernel(where_ref, *refs):
        refs = list(refs)
        arrays = [[refs.pop(0) for _ in range(size)] for size in sizes]
        in_refs = [refs.pop(0) for _ in ins]
        out_refs = [refs.pop(0) for _ in outs]
        places = [refs.pop(0) for _ in groups]
        sems = [refs.pop(0) for _ in groups]
        loads = [
            Loading(group.copies(where_ref, given, place, sem), place)
            for group, given, place, sem in zip(groups, arrays, places, sems)
        ]
        body(where_ref, loads, in_refs, out_refs, refs)

    return pl.pallas_call(
        kernel,
        out_shape=tuple(jax.ShapeDtypeStruct(*out) for out in outs),
        in_specs=[smem_spec()] + [any_spec()] * sum(sizes) + [vmem_spec()] * len(ins),
        out_specs=(vmem_spec(),) * len(outs),
        scratch_shapes=[pltpu.VMEM(group.shape, BF16) for group in groups]
        + [pltpu.SemaphoreType.DMA((group.blocks,)) for group in groups]
        + list(scratch),
        compiler_params=pltpu.CompilerParams(vmem_limit_bytes=VMEM_LIMIT),
        cost_estimate=SMALL,
        name=name,
    )(where, *[array for group in groups for array in group.arrays], *ins)


def vector_kernel(pieces_ref, out_ref):
    count, width = pieces_ref.shape[0], pieces_ref.shape[3]
    for k in range(count):
        out_ref[:, :, k * width : (k + 1) * width] = pieces_ref[k]


def gather_vectors(mine):
    pieces = lax.all_gather(mine, "fsdp", axis=0)
    count, two, rows, width = pieces.shape
    return pl.pallas_call(
        vector_kernel,
        out_shape=jax.ShapeDtypeStruct((two, rows, count * width), mine.dtype),
        in_specs=[vmem_spec()],
        out_specs=vmem_spec(),
        compiler_params=pltpu.CompilerParams(vmem_limit_bytes=VMEM_LIMIT),
        name="gather_vectors",
    )(pieces)


def reduce_order(kind):
    stages = [("fsdp", bit) for bit in reversed(fsdp_bits())]
    place = 0 if kind == 0 else 1
    return stages[:place] + [("rep", 2)] + stages[place:]


def grad_kernel(unit_of, kind_stages, rows, width, where_ref, *refs):
    count = len(unit_of)
    lefts, rights = refs[:count], refs[count : 2 * count]
    keep, send = refs[2 * count], refs[2 * count + 1]
    rep, own = where_ref[0], where_ref[1]
    owners = lefts[0].shape[1] // rows
    for pair in range(count):
        left = lefts[pair][...]
        for column, unit in unit_of[pair]:
            product = matmul_tn(left, rights[pair][:, column : column + width])
            shifted = jnp.bitwise_xor(rep, unit)
            for other, target in ((0, keep), (1, send)):

                @pl.when(jnp.bitwise_and(shifted, 1) == other)
                def _():
                    for f in range(owners):
                        apart = jnp.bitwise_xor(own, f)
                        position = 0
                        for axis, bit in kind_stages:
                            value = shifted if axis == "rep" else apart
                            position = position * 2 + jnp.where(
                                jnp.bitwise_and(value, bit) != 0, 1, 0
                            )
                        target[pl.ds(pl.multiple_of(position * rows, 8), rows), :] = product[
                            f * rows : (f + 1) * rows, :
                        ]


def unit_grads(pairs, unit_of, kind, width, where):
    depth = pairs[0][0].shape[1]
    rows = depth // lax.axis_size("fsdp")
    shape = jax.ShapeDtypeStruct((2 * depth, width), F32)
    return Summing(
        *pl.pallas_call(
            functools.partial(grad_kernel, unit_of, reduce_order(kind), rows, width),
            out_shape=(shape, shape),
            in_specs=[smem_spec()] + [vmem_spec()] * (2 * len(pairs)),
            out_specs=(vmem_spec(), vmem_spec()),
            compiler_params=pltpu.CompilerParams(vmem_limit_bytes=VMEM_LIMIT),
            cost_estimate=SMALL,
            name="unit_grads",
        )(where, *[left for left, _ in pairs], *[right for _, right in pairs]),
        kind,
    )


class Summing:
    def __init__(self, keep, send, kind):
        self.parts, self.stages = (keep, send), [("rep", 1)] + reduce_order(kind)

    def step(self):
        keep, send = self.parts
        got = swap(send, self.stages.pop(0))
        if self.stages:
            half = keep.shape[0] // 2
            self.parts = keep[:half] + got[:half], keep[half:] + got[half:]
        else:
            self.parts = (keep + got,)

    def finish(self):
        while self.stages:
            self.step()
        return self.parts[0]


def tie_sums(values, *sums):
    tied = tie(*values, *[part for one in sums for part in one.parts])
    values, parts = tied[: len(values)], list(tied[len(values) :])
    for one in sums:
        one.parts = tuple(parts.pop(0) for _ in one.parts)
    return values


def owner_kernel(count, width, left_ref, right_ref, out_ref):
    rows = left_ref.shape[1] // count
    left = left_ref[...]
    for unit in range(4):
        product = matmul_tn(left, right_ref[:, unit * width : (unit + 1) * width])
        for owner in range(count):
            place = (owner * 4 + unit) * rows
            out_ref[place : place + rows, :] = product[owner * rows : (owner + 1) * rows, :]


def owner_grads(left, right):
    depth, width = left.shape[1], right.shape[1] // 4
    return pl.pallas_call(
        functools.partial(owner_kernel, lax.axis_size("fsdp"), width),
        out_shape=jax.ShapeDtypeStruct((4 * depth, width), F32),
        in_specs=[vmem_spec()] * 2,
        out_specs=vmem_spec(),
        compiler_params=pltpu.CompilerParams(vmem_limit_bytes=VMEM_LIMIT),
        cost_estimate=SMALL,
        name="owner_grads",
    )(left, right)


def share_units(own):
    far = swap(own, ("rep", 2))
    near, cross = swap(own, ("rep", 1)), swap(far, ("rep", 1))
    return jnp.stack([own, near, far, cross])


def scores_of(query, key_rows, valid, scaling):
    scores = matmul_nt(query, key_rows) * scaling
    return jnp.where(valid, scores, -1e30)


def attention_kernel(seq_len, head_dim, q_ref, k_ref, v_ref, out_ref, log_ref):
    rows, model_width = q_ref.shape
    scaling = head_dim**-0.5
    valid = lax.broadcasted_iota(jnp.int32, (rows, rows), 1) < seq_len
    lane = lax.broadcasted_iota(jnp.int32, (rows, 2 * head_dim), 1)
    zero = jnp.zeros((rows, 2 * head_dim), BF16)
    for pair in range(model_width // (2 * head_dim)):
        columns = slice(pair * 2 * head_dim, (pair + 1) * 2 * head_dim)
        query, key_rows, values = q_ref[:, columns], k_ref[:, columns], v_ref[:, columns]
        results = []
        for sub in range(2):
            picked = lane >= head_dim if sub else lane < head_dim
            scores = scores_of(jnp.where(picked, query, zero), key_rows, valid, scaling)
            highest = jnp.max(scores, axis=-1, keepdims=True)
            logsum = highest + jnp.log(jnp.sum(jnp.exp(scores - highest), axis=-1, keepdims=True))
            log_ref[:, 2 * pair + sub : 2 * pair + sub + 1] = logsum
            results.append(matmul(to_low(jnp.exp(scores - logsum)), values))
        out_ref[:, columns] = to_low(jnp.where(lane < head_dim, results[0], results[1]))


def attention_forward(query, key_rows, value_rows, samples, seq_len):
    row_count, model_width = query.shape
    rows = row_count // samples
    head_dim = model_width // HEADS
    block = pl.BlockSpec((rows, model_width), lambda i: (i, 0))
    small = pl.BlockSpec((rows, 128), lambda i: (i, 0))
    return pl.pallas_call(
        functools.partial(attention_kernel, seq_len, head_dim),
        grid=(samples,),
        out_shape=(
            jax.ShapeDtypeStruct(query.shape, BF16),
            jax.ShapeDtypeStruct((row_count, 128), F32),
        ),
        in_specs=[block] * 3,
        out_specs=(block, small),
        compiler_params=pltpu.CompilerParams(vmem_limit_bytes=VMEM_LIMIT),
        cost_estimate=SMALL,
        name="attention",
    )(query, key_rows, value_rows)


def attention_back_kernel(
    seq_len, head_dim, q_ref, k_ref, v_ref, da_ref, log_ref, dq_ref, dk_ref, dv_ref
):
    rows, model_width = q_ref.shape
    scaling = head_dim**-0.5
    valid = lax.broadcasted_iota(jnp.int32, (rows, rows), 1) < seq_len
    lane = lax.broadcasted_iota(jnp.int32, (rows, 2 * head_dim), 1)
    zero = jnp.zeros((rows, 2 * head_dim), BF16)
    for pair in range(model_width // (2 * head_dim)):
        columns = slice(pair * 2 * head_dim, (pair + 1) * 2 * head_dim)
        query, key_rows = q_ref[:, columns], k_ref[:, columns]
        values, grad = v_ref[:, columns], da_ref[:, columns]
        results = []
        for sub in range(2):
            picked = lane >= head_dim if sub else lane < head_dim
            scores = scores_of(jnp.where(picked, query, zero), key_rows, valid, scaling)
            soft = jnp.exp(scores - log_ref[:, 2 * pair + sub : 2 * pair + sub + 1])
            grad_soft = matmul_nt(jnp.where(picked, grad, zero), values)
            total = jnp.sum(grad_soft * soft, axis=-1, keepdims=True)
            grad_scores = to_low(soft * (grad_soft - total))
            results.append(
                (
                    matmul(grad_scores, key_rows) * scaling,
                    matmul_tn(grad_scores, query) * scaling,
                    matmul_tn(to_low(soft), grad),
                )
            )
        for target, first, second in zip((dq_ref, dk_ref, dv_ref), *results):
            target[:, columns] = to_low(jnp.where(lane < head_dim, first, second))


def attention_backward(query, key_rows, value_rows, logsum, grad, samples, seq_len):
    row_count, model_width = query.shape
    rows = row_count // samples
    head_dim = model_width // HEADS
    block = pl.BlockSpec((rows, model_width), lambda i: (i, 0))
    small = pl.BlockSpec((rows, 128), lambda i: (i, 0))
    return pl.pallas_call(
        functools.partial(attention_back_kernel, seq_len, head_dim),
        grid=(samples,),
        out_shape=(jax.ShapeDtypeStruct(query.shape, BF16),) * 3,
        in_specs=[block] * 4 + [small],
        out_specs=(block,) * 3,
        compiler_params=pltpu.CompilerParams(vmem_limit_bytes=VMEM_LIMIT),
        cost_estimate=SMALL,
        name="attention_back",
    )(query, key_rows, value_rows, grad, logsum)


TILE = 256


def tiles(width, body):
    def step(number, carry):
        body(pl.ds(pl.multiple_of(number * TILE, TILE), TILE))
        return carry

    lax.fori_loop(0, width // TILE, step, 0)


def embed_body(samples, masked, base, where_ref, loads, ins, outs, scratch):
    patch_ref, vec_ref, pos_ref = ins[:3]
    hid_ref, low_ref, q_ref, k_ref, v_ref = outs
    weights = loads[0]()
    rows = patch_ref.shape[0] // samples
    width = patch_ref.shape[1]

    def embed(columns):
        product = matmul(patch_ref[...], weights[0, :, columns]) + vec_ref[0:1, columns]
        if masked:
            product = jnp.where(ins[3][...] > 0, vec_ref[1:2, columns], product)
        for s in range(samples):
            part = product[s * rows : (s + 1) * rows] + pos_ref[:, columns]
            hid_ref[s * rows : (s + 1) * rows, columns] = part
            low_ref[s * rows : (s + 1) * rows, columns] = to_low(part)

    tiles(width, embed)

    def project(columns):
        low = low_ref[...]
        q_ref[:, columns] = to_low(
            matmul(low, weights[1, :, columns]) + vec_ref[base : base + 1, columns]
        )
        k_ref[:, columns] = to_low(matmul(low, weights[2, :, columns]))
        v_ref[:, columns] = to_low(
            matmul(low, weights[3, :, columns]) + vec_ref[base + 1 : base + 2, columns]
        )

    tiles(width, project)


def feed_forward(samples, base, unit, loads, ins, student, refs):
    att_ref, hid_ref, vec_ref = ins
    sum_ref, low_ref, act_ref = refs[:3]
    rows, width = hid_ref.shape[0] // samples, hid_ref.shape[1]
    squares = loads[0]()

    def project(columns):
        sum_ref[:, columns] = (
            hid_ref[:, columns]
            + matmul(att_ref[...], squares[unit, :, columns])
            + vec_ref[base + 2 : base + 3, columns]
        )

    tiles(width, project)
    for s in range(samples):
        part = slice(s * rows, (s + 1) * rows)
        hat, inverse = norm_parts(sum_ref[part, :])
        if student:
            refs[3][part, :], refs[4][part, :] = hat, inverse
        normed = hat * vec_ref[base + 3 : base + 4, :] + vec_ref[base + 4 : base + 5, :]
        sum_ref[part, :] = normed
        low_ref[part, :] = to_low(normed)
    up = loads[1]()
    hidden_units = up.shape[1]

    def widen(columns, bias):
        pre_act = matmul(low_ref[...], up[:, columns]) + bias
        value, slope = gelu_exact(pre_act)
        act_ref[:, columns] = to_low(value)
        if student:
            refs[5][:, columns] = slope

    for quarter in range(4):
        size = hidden_units // 4

        def step(number, carry, quarter=quarter):
            inner = pl.ds(pl.multiple_of(number * TILE, TILE), TILE)
            outer = pl.ds(pl.multiple_of(quarter * size + number * TILE, TILE), TILE)
            widen(outer, vec_ref[base + 8 + quarter : base + 9 + quarter, inner])
            return carry

        lax.fori_loop(0, size // TILE, step, 0)
    down = loads[2]()

    def narrow(columns, target_ref, residual):
        branch = (
            matmul_nt(act_ref[...], down[columns, :]) + vec_ref[base + 5 : base + 6, columns]
        )
        target_ref[:, columns] = sum_ref[:, columns] + branch if residual else branch

    return narrow


def teacher_body(samples, seq_len, base, where_ref, loads, ins, outs, scratch):
    target_ref = outs[0]
    narrow = feed_forward(samples, base, 0, loads, ins, False, scratch)
    rows, width = target_ref.shape[0] // samples, target_ref.shape[1]
    tiles(width, lambda columns: narrow(columns, target_ref, False))
    valid = lax.broadcasted_iota(jnp.int32, (rows, width), 0) < seq_len
    for s in range(samples):
        part = slice(s * rows, (s + 1) * rows)
        values = target_ref[part, :]
        total = jnp.sum(jnp.where(valid, values, 0.0), axis=0, keepdims=True)
        centred = values - total * (1.0 / seq_len)
        spread = jnp.sum(jnp.where(valid, centred * centred, 0.0), axis=0, keepdims=True)
        target_ref[part, :] = centred * lax.rsqrt(spread * (1.0 / seq_len) + ln_eps)


def student_body(samples, base, loss_scale, where_ref, loads, ins, outs, scratch):
    target_ref, mask_ref = ins[3:]
    final_ref, dy_ref, gb2_ref, g2_ref, act_ref, slope_ref, low_ref, hat_ref, inv_ref = outs[:9]
    rows_ref, loss_ref = outs[9:]
    sum_ref, hat2_ref, hatf_ref, gf_ref, inv2_ref, invf_ref = scratch
    narrow = feed_forward(
        samples, base, 1, loads, ins[:3], True, (sum_ref, low_ref, act_ref, hat_ref, inv_ref, slope_ref)
    )
    vec_ref = ins[2]
    squares = loads[0]()
    width = sum_ref.shape[1]
    rows = sum_ref.shape[0] // samples
    final_base = base + 12
    tiles(width, lambda columns: narrow(columns, gf_ref, True))
    for s in range(samples):
        part = slice(s * rows, (s + 1) * rows)
        hat, inverse = norm_parts(gf_ref[part, :])
        hat2_ref[part, :], inv2_ref[part, :] = hat, inverse
        result = hat * vec_ref[base + 6 : base + 7, :] + vec_ref[base + 7 : base + 8, :]
        hat, inverse = norm_parts(result)
        hatf_ref[part, :], invf_ref[part, :] = hat, inverse
        final_ref[part, :] = to_low(
            hat * vec_ref[final_base : final_base + 1, :]
            + vec_ref[final_base + 1 : final_base + 2, :]
        )
    rows_ref[...] = jnp.zeros_like(rows_ref)
    loss_ref[...] = jnp.zeros_like(loss_ref)

    def head(columns):
        output = matmul(final_ref[...], squares[2, :, columns])
        residue = output + vec_ref[final_base + 2 : final_base + 3, columns] - target_ref[:, columns]
        magnitude = jnp.abs(residue)
        terms = jnp.where(
            magnitude <= huber_delta,
            0.5 * residue * residue,
            huber_delta * (magnitude - 0.5 * huber_delta),
        )
        loss_ref[...] += jnp.sum(
            jnp.sum(terms * mask_ref[...], axis=0, keepdims=True), axis=1, keepdims=True
        )
        grad = to_low(jnp.clip(residue, -huber_delta, huber_delta) * mask_ref[...] * loss_scale)
        dy_ref[:, columns] = grad
        rows_ref[0:1, columns] = jnp.sum(grad.astype(F32), axis=0, keepdims=True)

    tiles(width, head)

    def back(columns):
        gf_ref[:, columns] = matmul_nt(dy_ref[...], squares[2, columns, :])

    tiles(width, back)
    for s in range(samples):
        part = slice(s * rows, (s + 1) * rows)
        grad, hat = gf_ref[part, :], hatf_ref[part, :]
        rows_ref[1:2, :] += jnp.sum(grad * hat, axis=0, keepdims=True)
        rows_ref[2:3, :] += jnp.sum(grad, axis=0, keepdims=True)
        grad = norm_back(grad, hat, invf_ref[part, :], vec_ref[final_base : final_base + 1, :])
        hat = hat2_ref[part, :]
        rows_ref[3:4, :] += jnp.sum(grad * hat, axis=0, keepdims=True)
        rows_ref[4:5, :] += jnp.sum(grad, axis=0, keepdims=True)
        grad = norm_back(grad, hat, inv2_ref[part, :], vec_ref[base + 6 : base + 7, :])
        g2_ref[part, :] = grad
        low = to_low(grad)
        gb2_ref[part, :] = low
        rows_ref[5:6, :] += jnp.sum(low.astype(F32), axis=0, keepdims=True)


def feed_back_body(samples, base, where_ref, loads, ins, outs, scratch):
    gb2_ref, g2_ref, slope_ref, hat_ref, inv_ref, vec_ref = ins
    gpre_ref, gfirst_ref, gbranch_ref, gatt_ref, rows_ref, up_ref = outs
    grad_ref = scratch[0]
    squares, up, down = loads
    down = down()
    width, hidden_units = down.shape
    rows = gb2_ref.shape[0] // samples

    def widen(columns):
        grad = to_low(matmul(gb2_ref[...], down[:, columns]) * slope_ref[:, columns])
        gpre_ref[:, columns] = grad
        up_ref[:, columns] = jnp.sum(grad.astype(F32), axis=0, keepdims=True)

    tiles(hidden_units, widen)
    up = up()

    def narrow(columns):
        grad_ref[:, columns] = g2_ref[:, columns] + matmul_nt(gpre_ref[...], up[columns, :])

    tiles(width, narrow)
    rows_ref[...] = jnp.zeros_like(rows_ref)
    for s in range(samples):
        part = slice(s * rows, (s + 1) * rows)
        grad, hat = grad_ref[part, :], hat_ref[part, :]
        rows_ref[0:1, :] += jnp.sum(grad * hat, axis=0, keepdims=True)
        rows_ref[1:2, :] += jnp.sum(grad, axis=0, keepdims=True)
        grad = norm_back(grad, hat, inv_ref[part, :], vec_ref[base + 3 : base + 4, :])
        gfirst_ref[part, :] = grad
        low = to_low(grad)
        gbranch_ref[part, :] = low
        rows_ref[2:3, :] += jnp.sum(low.astype(F32), axis=0, keepdims=True)
    squares = squares()

    def project(columns):
        gatt_ref[:, columns] = to_low(matmul_nt(gbranch_ref[...], squares[1, columns, :]))

    tiles(width, project)


def embed_back_body(samples, seq_len, base, where_ref, loads, ins, outs, scratch):
    gq_ref, gk_ref, gv_ref, gfirst_ref, mask_ref, after_ref, inner_ref, up_ref = ins
    ge_ref, pieces_ref = outs
    all_ref, pos_ref = scratch
    weights = loads[0]()
    width = gq_ref.shape[1]
    rows = gq_ref.shape[0] // samples

    def project(columns):
        grad = gfirst_ref[:, columns] + matmul_nt(gq_ref[...], weights[1, columns, :])
        grad += matmul_nt(gk_ref[...], weights[2, columns, :])
        grad += matmul_nt(gv_ref[...], weights[3, columns, :])
        hidden = grad * mask_ref[...]
        all_ref[1:2, columns] = jnp.sum(hidden, axis=0, keepdims=True)
        low = to_low(grad * (1.0 - mask_ref[...]))
        ge_ref[:, columns] = low
        all_ref[0:1, columns] = jnp.sum(low.astype(F32), axis=0, keepdims=True)
        total = grad[0:rows]
        for s in range(1, samples):
            total += grad[s * rows : (s + 1) * rows]
        pos_ref[:, columns] = total
        all_ref[base : base + 1, columns] = jnp.sum(
            gq_ref[:, columns].astype(F32), axis=0, keepdims=True
        )
        all_ref[base + 1 : base + 2, columns] = jnp.sum(
            gv_ref[:, columns].astype(F32), axis=0, keepdims=True
        )

    tiles(width, project)
    all_ref[2 : 2 + seq_len, :] = pos_ref[0:seq_len, :]
    all_ref[base + 2 : base + 3, :] = inner_ref[2:3, :]
    all_ref[base + 3 : base + 5, :] = inner_ref[0:2, :]
    all_ref[base + 5 : base + 6, :] = after_ref[5:6, :]
    all_ref[base + 6 : base + 8, :] = after_ref[3:5, :]
    for k in range(4):
        all_ref[base + 8 + k : base + 9 + k, :] = up_ref[:, k * width : (k + 1) * width]
    all_ref[base + 12 : base + 14, :] = after_ref[1:3, :]
    all_ref[base + 14 : base + 15, :] = after_ref[0:1, :]
    count, _, size = pieces_ref.shape
    for k in range(count):
        pieces_ref[jnp.bitwise_xor(where_ref[1], k)] = all_ref[:, k * size : (k + 1) * size]


def adam_step(master, moment_one, moment_two, gradient, factor):
    clipped = gradient * factor
    one_new = beta_one * moment_one + (1.0 - beta_one) * clipped
    two_new = beta_two * moment_two + (1.0 - beta_two) * clipped * clipped
    one_hat = one_new / (1.0 - beta_one**ADAM_STEP)
    two_hat = two_new / (1.0 - beta_two**ADAM_STEP)
    step_value = -learn_rate * (one_hat / (jnp.sqrt(two_hat) + adam_eps) + decay_rate * master)
    return (step_value, one_new, two_new)


def teacher_move(master, teacher, step_value):
    return (1.0 - ema_keep) * (master - teacher + step_value)


def per_device(
    patches,
    mask_places,
    square_weights,
    square_first,
    square_second,
    square_teacher,
    feed_weights,
    feed_first,
    feed_second,
    feed_teacher,
    vector_weights,
    vector_first,
    vector_second,
    vector_teacher,
):
    samples, seq_len, model_width = patches.shape
    total_masked = samples * mask_places.shape[1] * lax.axis_size("rep") * lax.axis_size("fsdp")
    rep, own = lax.axis_index("rep"), lax.axis_index("fsdp")
    where = jnp.stack([rep, own]).astype(jnp.int32)
    pad_len = -(-seq_len // 8) * 8
    row_count = samples * pad_len
    hidden_units = feed_weights.shape[3]
    patch_rows = jnp.pad(patches, ((0, 0), (0, pad_len - seq_len), (0, 0))).reshape(
        row_count, model_width
    )
    places = jnp.arange(pad_len, dtype=jnp.int32)
    mask_rows = jnp.sum(
        (mask_places[:, :, None] == places[None, None, :]).astype(F32), axis=1
    ).reshape(row_count, 1)

    def pick(array, index):
        return to_low(lax.dynamic_index_in_dim(array, index, keepdims=False))

    def columns_of(array, number):
        width = array.shape[3] // 4
        return to_low(lax.dynamic_slice_in_dim(array[0, number], rep * width, width, axis=1))

    vector_old_new = gather_vectors(jnp.stack([vector_weights, vector_teacher]))
    vector_all, vector_old = vector_old_new[0], vector_old_new[1]
    both_s = lax.all_gather(
        jnp.concatenate([columns_of(feed_weights, 0), columns_of(feed_weights, 1)]),
        ("fsdp", "rep"),
        axis=0,
        tiled=True,
    )
    up_s = Gathered(both_s, 0, 2, True, where)
    down_s = Gathered(both_s, 1, 2, True, where)
    others = jnp.where(
        rep == 0, to_low(square_teacher[4]), pick(square_weights, jnp.clip(rep + 3, 4, 5))
    )
    entry_t = Group(pick(square_teacher, rep), 0, False, where)
    entry_s = Group(pick(square_weights, rep), 1, False, where, entry_t)
    outer = Group(others, 0, False, where, entry_s)
    up_t = Group(columns_of(feed_teacher, 0), 1, True, where, outer)
    down_t = Group(columns_of(feed_teacher, 1), 0, True, where, up_t)
    for group in (entry_t, entry_s, outer, up_t, down_t):
        group.fabric()
    base = 2 + seq_len

    def positions(vector):
        return jnp.pad(vector[2 : 2 + seq_len], ((0, pad_len - seq_len), (0, 0)))

    full, low_full = ((row_count, model_width), F32), ((row_count, model_width), BF16)
    low_wide, full_wide = ((row_count, hidden_units), BF16), ((row_count, hidden_units), F32)
    column = ((row_count, 1), F32)

    def entry(group, vector, masked, name):
        return call(
            functools.partial(embed_body, samples, masked, base),
            name,
            where,
            [group],
            [patch_rows, vector, positions(vector)] + ([mask_rows] if masked else []),
            [full] + [low_full] * 4,
        )

    hidden_t, _, query, key_rows, value_rows = entry(
        entry_t.finish(), vector_old, False, "embed_t"
    )
    attended_t, _ = attention_forward(query, key_rows, value_rows, samples, seq_len)
    entry_s.arrays[0], attended_t = tie(entry_s.arrays[0], attended_t)
    hidden, hidden_low, query, key_rows, value_rows = entry(
        entry_s.finish(), vector_all, True, "embed_s"
    )
    attended, logsum = attention_forward(query, key_rows, value_rows, samples, seq_len)
    outer.finish(), up_t.finish()
    down_t.arrays[0], attended = tie(down_t.arrays[0], attended)
    down_t.finish()
    (target,) = call(
        functools.partial(teacher_body, samples, seq_len, base),
        "layer_t",
        where,
        [outer, up_t, down_t],
        [attended_t, hidden_t, vector_old],
        [full],
        [pltpu.VMEM(*full), pltpu.VMEM(*low_full), pltpu.VMEM(*low_wide)],
    )
    loss_scale = 1.0 / (total_masked * model_width)
    (
        final_low,
        grad_output,
        grad_branch_two,
        grad_second,
        activation,
        slope,
        normed_low,
        hat_first,
        inverse_first,
        rows_after,
        loss_sum,
    ) = call(
        functools.partial(student_body, samples, base, loss_scale),
        "layer_s",
        where,
        [outer, up_s, down_s],
        [attended, hidden, vector_all, target, mask_rows],
        [low_full] * 3
        + [full, low_wide, full_wide, low_full, full, column, ((8, model_width), F32), ((1, 1), F32)],
        [pltpu.VMEM(*full)] * 4 + [pltpu.VMEM(*column)] * 2,
    )
    loss_local = loss_sum[0, 0] * loss_scale

    unit = model_width
    down_g = owner_grads(grad_branch_two, activation)
    grad_branch_two, down_g = tie(grad_branch_two, down_g)
    down_own = lax.psum_scatter(down_g, ("fsdp", "rep"), scatter_dimension=0, tiled=True)
    grad_pre, grad_first, grad_branch, grad_attended, rows_inner, rows_up = call(
        functools.partial(feed_back_body, samples, base),
        "feed_back",
        where,
        [outer, up_s, down_s],
        [grad_branch_two, grad_second, slope, hat_first, inverse_first, vector_all],
        [low_wide, full, low_full, low_full, ((8, model_width), F32), ((1, hidden_units), F32)],
        [pltpu.VMEM(*full)],
    )
    half = unit // 2

    def up_half(grad, number):
        places = [[(k * unit + number * half, k) for k in range(4)]]
        return unit_grads([(normed_low, grad)], places, number, half, where)

    up_a = up_half(grad_pre, 0)
    (grad_pre,) = tie_sums([grad_pre], up_a)
    up_b = up_half(grad_pre, 1)
    up_a.step()
    (grad_branch,) = tie_sums([grad_branch], up_a, up_b)
    halves = [[(0, 0), (half, 1)], [(0, 2), (half, 3)]]
    edge_g = unit_grads(
        [(final_low, grad_output), (attended, grad_branch)], halves, 0, half, where
    )
    up_b.step()
    (grad_attended,) = tie_sums([grad_attended], up_b, edge_g)
    grad_query, grad_key, grad_value = attention_backward(
        query, key_rows, value_rows, logsum, grad_attended, samples, seq_len
    )
    edge_g.step()
    grad_query, grad_key, grad_value = tie_sums([grad_query, grad_key, grad_value], edge_g)
    vector_count = vector_all.shape[0]
    count = lax.axis_size("fsdp")
    grad_embed, pieces = call(
        functools.partial(embed_back_body, samples, seq_len, base),
        "embed_back",
        where,
        [entry_s],
        [grad_query, grad_key, grad_value, grad_first, mask_rows, rows_after, rows_inner, rows_up],
        [low_full, ((count, vector_count, model_width // count), F32)],
        [pltpu.VMEM((vector_count, model_width), F32), pltpu.VMEM((pad_len, model_width), F32)],
    )

    def entry_half(grad, number):
        pairs = [(hidden_low, grad_query), (hidden_low, grad_key), (hidden_low, grad_value), (patch_rows, grad)]
        return unit_grads(pairs, [[(number * half, k)] for k in range(4)], number, half, where)

    up_a.step()
    (grad_embed,) = tie_sums([grad_embed], up_a)
    qkv_a = entry_half(grad_embed, 0)
    edge_g.step()
    (grad_embed,) = tie_sums([grad_embed], edge_g, qkv_a)
    qkv_b = entry_half(grad_embed, 1)
    qkv_a.step()
    up_b.step()
    tie_sums([], up_b, qkv_a)

    up_own = jnp.concatenate([up_a.finish(), up_b.finish()], axis=1)
    edge_own = edge_g.finish()
    qkv_own = jnp.concatenate([qkv_a.finish(), qkv_b.finish()], axis=1)
    for bit in fsdp_bits():
        count = pieces.shape[0] // 2
        pieces = pieces[:count] + swap(pieces[count:], ("fsdp", bit))
    vector_share = pieces[0]
    for bit in (2, 1):
        vector_share = vector_share + swap(vector_share, ("rep", bit))
    squares_own = (
        jnp.sum(down_own * down_own)
        + jnp.sum(up_own * up_own)
        + jnp.sum(edge_own * edge_own)
        + jnp.sum(qkv_own * qkv_own)
        + 0.25 * jnp.sum(vector_share * vector_share)
    )
    totals = jnp.stack([squares_own, loss_local])
    for bit in fsdp_bits():
        totals = totals + swap(totals, ("fsdp", bit))
    for bit in (2, 1):
        totals = totals + swap(totals, ("rep", bit))
    norm_squared, loss_value = totals[0], totals[1]

    def ordered(own_units):
        shared = share_units(own_units)
        return [lax.dynamic_index_in_dim(shared, rep ^ k, keepdims=False) for k in range(4)]

    early_u, qkv_u = ordered(jnp.concatenate([down_own, up_own, edge_own], axis=1)), ordered(qkv_own)
    down_u = [own[:, :unit] for own in early_u]
    up_u = [own[:, unit : 2 * unit] for own in early_u]
    edge_u = [own[:, 2 * unit :] for own in early_u]
    feed_grad = jnp.stack([jnp.concatenate(up_u, axis=1), jnp.concatenate(down_u, axis=1)])[None]
    square_grad = jnp.stack(
        [
            qkv_u[3],
            qkv_u[0],
            qkv_u[1],
            qkv_u[2],
            jnp.concatenate(edge_u[2:], axis=1),
            jnp.concatenate(edge_u[:2], axis=1),
        ]
    )
    grad_norm = jnp.sqrt(norm_squared)
    limit = clip_scale / math.sqrt(total_masked)
    factor = limit / jnp.maximum(grad_norm, limit)
    square_step, square_one, square_two = adam_step(
        square_weights, square_first, square_second, square_grad, factor
    )
    feed_step, feed_one, feed_two = adam_step(
        feed_weights, feed_first, feed_second, feed_grad, factor
    )
    vector_step, vector_one, vector_two = adam_step(
        vector_weights, vector_first, vector_second, vector_share, factor
    )
    square_moved = teacher_move(square_weights, square_teacher, square_step)
    feed_moved = teacher_move(feed_weights, feed_teacher, feed_step)
    vector_moved = teacher_move(vector_weights, vector_teacher, vector_step)
    return (
        loss_value,
        grad_norm,
        square_step,
        square_one,
        square_two,
        square_moved,
        feed_step,
        feed_one,
        feed_two,
        feed_moved,
        vector_step,
        vector_one,
        vector_two,
        vector_moved,
    )


def solution(mesh):
    placed = (
        P(("rep", "fsdp"), None, None),
        P(("rep", "fsdp"), None),
        P(None, "fsdp", None),
        P(None, "fsdp", None),
        P(None, "fsdp", None),
        P(None, "fsdp", None),
        P(None, None, "fsdp", None),
        P(None, None, "fsdp", None),
        P(None, None, "fsdp", None),
        P(None, None, "fsdp", None),
        P(None, "fsdp"),
        P(None, "fsdp"),
        P(None, "fsdp"),
        P(None, "fsdp"),
    )
    return jax.shard_map(
        per_device,
        mesh=mesh,
        in_specs=placed,
        out_specs=(
            P(),
            P(),
            P(None, "fsdp", None),
            P(None, "fsdp", None),
            P(None, "fsdp", None),
            P(None, "fsdp", None),
            P(None, None, "fsdp", None),
            P(None, None, "fsdp", None),
            P(None, None, "fsdp", None),
            P(None, None, "fsdp", None),
            P(None, "fsdp"),
            P(None, "fsdp"),
            P(None, "fsdp"),
            P(None, "fsdp"),
        ),
        check_vma=False,
    )
```

```python
import functools
import math

import jax
import jax.numpy as jnp
from jax import lax
from jax.experimental import pallas as pl
from jax.experimental.pallas import tpu as pltpu
from jax.sharding import PartitionSpec as P

HEADS = 12
ADAM_STEP = 10


ln_eps = 1e-05
beta_one = 0.9
beta_two = 0.999
adam_eps = 1e-08
learn_rate = 0.01
decay_rate = 0.05
ema_keep = 0.999
huber_delta = 1.0
clip_scale = 1.25

VMEM_LIMIT = 60 * 1024 * 1024
SHARE = 0.0
MICROSECONDS = dict(
    gather_vectors=3,
    embed_t=9,
    embed_s=9,
    attention=7,
    layer_t=23,
    layer_s=33,
    owner_grads=8,
    feed_back=23,
    unit_grads=7,
    attention_back=16,
    embed_back=9,
)


def cost(name):
    flops = int(SHARE * MICROSECONDS[name] * 1.15e9)
    return pl.CostEstimate(flops=flops, bytes_accessed=1024, transcendentals=0)
BF16 = jnp.bfloat16
F32 = jnp.float32


def to_low(values):
    return values.astype(BF16)


def matmul(left, right):
    return jnp.dot(left, right, preferred_element_type=F32)


def matmul_tn(left, right):
    return lax.dot_general(left, right, (((0,), (0,)), ((), ())), preferred_element_type=F32)


def matmul_nt(left, right):
    return lax.dot_general(left, right, (((1,), (1,)), ((), ())), preferred_element_type=F32)


tail_scale = 0.21
tail_terms = (
    0.08371158707086396,
    0.08506867712628283,
    0.06919339848407204,
    0.1248680487092072,
    -0.09391427181816406,
    0.34938494294095396,
    -0.3302388882989717,
    0.2835812219436135,
    -0.07165470896901999,
)


def gelu_exact(values):
    t = 1.0 / (1.0 + tail_scale * jnp.abs(values))
    tail = jnp.full_like(t, tail_terms[-1])
    for term in tail_terms[-2::-1]:
        tail = tail * t + term
    bell = jnp.exp(-0.5 * (values * values))
    tail = tail * t * bell
    normal = jnp.where(values < 0, tail, 1.0 - tail)
    return values * normal, normal + values * bell * (1.0 / math.sqrt(2.0 * math.pi))


def norm_parts(values):
    centred = values - jnp.mean(values, axis=-1, keepdims=True)
    inverse = lax.rsqrt(jnp.mean(centred * centred, axis=-1, keepdims=True) + ln_eps)
    return centred * inverse, inverse


def norm_back(grad, hat, inverse, gain):
    scaled = grad * gain
    return inverse * (
        scaled
        - jnp.mean(scaled, axis=-1, keepdims=True)
        - hat * jnp.mean(scaled * hat, axis=-1, keepdims=True)
    )


def any_spec():
    return pl.BlockSpec(memory_space=pl.ANY)


def vmem_spec():
    return pl.BlockSpec(memory_space=pltpu.VMEM)


def smem_spec():
    return pl.BlockSpec(memory_space=pltpu.SMEM)


def swap(values, stage):
    axis, bit = stage
    return lax.ppermute(values, axis, [(i, i ^ bit) for i in range(lax.axis_size(axis))])


def fsdp_bits():
    count = lax.axis_size("fsdp")
    return [1 << k for k in reversed(range(count.bit_length() - 1))]


def stage_order(kind):
    stages = [("fsdp", bit) for bit in fsdp_bits()]
    place = len(stages) if kind == 0 else len(stages) - 1
    return stages[:place] + [("rep", 2)] + stages[place:]


def tie(*values):
    return lax.optimization_barrier(values)


class Group:
    def __init__(self, mine, kind, wide, where, before=None):
        self.wide, self.where = wide, where
        self.rows, self.width = mine.shape
        count = lax.axis_size("fsdp")
        depth = self.rows * count
        self.shape = (depth, 4 * self.width) if wide else (4, depth, self.width)
        self.blocks = 4 * count
        if before is not None:
            mine, before.arrays[0] = tie(mine, before.arrays[0])
        self.arrays, self.labels = [mine], [[(0, 0)]]
        self.stages = stage_order(kind)
        self.step()

    def step(self):
        axis, bit = self.stages.pop(0)
        got = swap(self.arrays[0], (axis, bit))
        moved = [
            (u ^ bit, e) if axis == "rep" else (u, e ^ bit) for u, e in self.labels[0]
        ]
        if self.stages:
            self.arrays = [jnp.concatenate([self.arrays[0], got], axis=0)]
            self.labels = [self.labels[0] + moved]
        else:
            self.arrays, self.labels = self.arrays + [got], self.labels + [moved]

    def fabric(self):
        while self.stages:
            self.step()
        return self

    def finish(self):
        self.arrays = self.arrays + [swap(a, ("rep", 1)) for a in self.arrays]
        self.labels = self.labels + [[(u ^ 1, e) for u, e in block] for block in self.labels]
        if self.rows % 16:
            count = lax.axis_size("fsdp")
            flat = jnp.concatenate(self.arrays, axis=0).reshape(-1, self.rows, self.width)
            order = [label for block in self.labels for label in block]
            place = {label: number for number, label in enumerate(order)}
            table = jnp.array(
                [[place[(u, e)] for e in range(count)] for u in range(4)], jnp.int32
            )
            units = jnp.arange(4, dtype=jnp.int32)[:, None] ^ self.where[0]
            owners = jnp.arange(count, dtype=jnp.int32)[None] ^ self.where[1]
            whole = flat[table[units, owners]].reshape(4, -1, self.width)
            self.whole(whole)
        return self

    def whole(self, units):
        if self.wide:
            units = units.transpose(1, 0, 2).reshape(self.shape)
        self.arrays, self.labels, self.blocks = [units], None, 1

    def copies(self, where_ref, arrays, out, sems):
        if self.labels is None:
            return [pltpu.make_async_copy(arrays[0], out, sems.at[0])]
        rep, own = where_ref[0], where_ref[1]
        copies = []
        for array, block in zip(arrays, self.labels):
            for number, (u, e) in enumerate(block):
                unit = jnp.bitwise_xor(rep, u)
                rows = pl.ds(pl.multiple_of(jnp.bitwise_xor(own, e) * self.rows, 16), self.rows)
                if self.wide:
                    columns = pl.ds(pl.multiple_of(unit * self.width, 128), self.width)
                    target = out.at[rows, columns]
                else:
                    target = out.at[unit, rows, :]
                source = array.at[pl.ds(number * self.rows, self.rows), :]
                copies.append(pltpu.make_async_copy(source, target, sems.at[len(copies)]))
        return copies


def tie_groups(values, *groups):
    tied = tie(*values, *[array for group in groups for array in group.arrays])
    values, arrays = tied[: len(values)], list(tied[len(values) :])
    for group in groups:
        group.arrays = [arrays.pop(0) for _ in group.arrays]
    return values


class Gathered(Group):
    def __init__(self, gathered, number, groups, wide, where):
        count = lax.axis_size("fsdp")
        self.wide, self.where = wide, where
        self.rows, self.width = gathered.shape[0] // (4 * count * groups), gathered.shape[1]
        depth = self.rows * count
        self.shape = (depth, 4 * self.width) if wide else (4, depth, self.width)
        self.arrays, self.labels, self.blocks = [gathered], (), 4 * count
        self.number, self.groups = number, groups
        if self.rows % 16:
            blocks = gathered.reshape(count, 4, groups, self.rows, self.width)[:, :, number]
            self.whole(blocks.transpose(1, 0, 2, 3).reshape(4, depth, self.width))

    def copies(self, where_ref, arrays, out, sems):
        if self.labels is None:
            return [pltpu.make_async_copy(arrays[0], out, sems.at[0])]
        copies = []
        for place in range(self.blocks):
            owner, unit = place // 4, place % 4
            rows = slice(owner * self.rows, (owner + 1) * self.rows)
            if self.wide:
                target = out.at[rows, unit * self.width : (unit + 1) * self.width]
            else:
                target = out.at[unit, rows, :]
            first = (place * self.groups + self.number) * self.rows
            source = arrays[0].at[first : first + self.rows, :]
            copies.append(pltpu.make_async_copy(source, target, sems.at[place]))
        return copies


class Loading:
    def __init__(self, copies, ref):
        self.pending, self.ref = copies, ref
        for copy in copies:
            copy.start()

    def __call__(self):
        for copy in self.pending:
            copy.wait()
        self.pending = []
        return self.ref


def call(body, name, where, groups, ins, outs, scratch=()):
    sizes = [len(group.arrays) for group in groups]

    def kernel(where_ref, *refs):
        refs = list(refs)
        arrays = [[refs.pop(0) for _ in range(size)] for size in sizes]
        in_refs = [refs.pop(0) for _ in ins]
        out_refs = [refs.pop(0) for _ in outs]
        places = [refs.pop(0) for _ in groups]
        sems = [refs.pop(0) for _ in groups]
        loads = [
            Loading(group.copies(where_ref, given, place, sem), place)
            for group, given, place, sem in zip(groups, arrays, places, sems)
        ]
        body(where_ref, loads, in_refs, out_refs, refs)

    return pl.pallas_call(
        kernel,
        out_shape=tuple(jax.ShapeDtypeStruct(*out) for out in outs),
        in_specs=[smem_spec()] + [any_spec()] * sum(sizes) + [vmem_spec()] * len(ins),
        out_specs=(vmem_spec(),) * len(outs),
        scratch_shapes=[pltpu.VMEM(group.shape, BF16) for group in groups]
        + [pltpu.SemaphoreType.DMA((group.blocks,)) for group in groups]
        + list(scratch),
        compiler_params=pltpu.CompilerParams(vmem_limit_bytes=VMEM_LIMIT),
        cost_estimate=cost(name),
        name=name,
    )(where, *[array for group in groups for array in group.arrays], *ins)


def vector_kernel(where_ref, pieces_ref, out_ref):
    _, two, rows, width = pieces_ref.shape
    count = pieces_ref.shape[0] // 4
    for u in range(4):
        for k in range(count):
            place = jnp.bitwise_xor(where_ref[0], u) * count + jnp.bitwise_xor(where_ref[1], k)
            out_ref[:, u * rows : (u + 1) * rows, k * width : (k + 1) * width] = pieces_ref[place]


def gather_vectors(both, where):
    rows = -(-both.shape[1] // 32) * 8
    both = jnp.pad(both, ((0, 0), (0, 4 * rows - both.shape[1]), (0, 0)))
    pieces = lax.dynamic_slice_in_dim(both, where[0] * rows, rows, axis=1)[None]
    for stage in [("fsdp", bit) for bit in reversed(fsdp_bits())] + [("rep", 1), ("rep", 2)]:
        pieces = jnp.concatenate([pieces, swap(pieces, stage)], axis=0)
    return pieces


def place_vectors(pieces, where):
    count, two, rows, width = pieces.shape
    return pl.pallas_call(
        vector_kernel,
        out_shape=jax.ShapeDtypeStruct((two, 4 * rows, count // 4 * width), pieces.dtype),
        in_specs=[smem_spec(), vmem_spec()],
        out_specs=vmem_spec(),
        compiler_params=pltpu.CompilerParams(vmem_limit_bytes=VMEM_LIMIT),
        cost_estimate=cost("gather_vectors"),
        name="gather_vectors",
    )(where, pieces)


def reduce_order(kind):
    stages = [("fsdp", bit) for bit in reversed(fsdp_bits())]
    place = 0 if kind == 0 else 1
    return stages[:place] + [("rep", 2)] + stages[place:]


def position(stages, unit, owner):
    place = 0
    for axis, bit in stages:
        value = unit if axis == "rep" else owner
        place = place * 2 + jnp.where(jnp.bitwise_and(value, bit) != 0, 1, 0)
    return place


def grad_kernel(unit_of, kind_stages, rows, width, where_ref, *refs):
    count = len(unit_of)
    lefts, rights = refs[:count], refs[count : 2 * count]
    keep, send = refs[2 * count], refs[2 * count + 1]
    rep, own = where_ref[0], where_ref[1]
    owners = lefts[0].shape[1] // rows
    for pair in range(count):
        left = lefts[pair][...]
        for column, unit in unit_of[pair]:
            product = matmul_tn(left, rights[pair][:, column : column + width])
            shifted = jnp.bitwise_xor(rep, unit)
            for other, target in ((0, keep), (1, send)):

                @pl.when(jnp.bitwise_and(shifted, 1) == other)
                def _():
                    for f in range(owners):
                        place = position(kind_stages, shifted, jnp.bitwise_xor(own, f))
                        target[pl.ds(pl.multiple_of(place * rows, 8), rows), :] = product[
                            f * rows : (f + 1) * rows, :
                        ]


def unit_grads(pairs, unit_of, kind, width, where):
    depth = pairs[0][0].shape[1]
    rows = depth // lax.axis_size("fsdp")
    shape = jax.ShapeDtypeStruct((2 * depth, width), F32)
    return Summing(
        *pl.pallas_call(
            functools.partial(grad_kernel, unit_of, reduce_order(kind), rows, width),
            out_shape=(shape, shape),
            in_specs=[smem_spec()] + [vmem_spec()] * (2 * len(pairs)),
            out_specs=(vmem_spec(), vmem_spec()),
            compiler_params=pltpu.CompilerParams(vmem_limit_bytes=VMEM_LIMIT),
            cost_estimate=cost("unit_grads"),
            name="unit_grads",
        )(where, *[left for left, _ in pairs], *[right for _, right in pairs]),
        kind,
    )


class Summing:
    def __init__(self, keep, send, kind):
        self.parts, self.stages = (keep, send), [("rep", 1)] + reduce_order(kind)

    def step(self):
        keep, send = self.parts
        got = swap(send, self.stages.pop(0))
        if self.stages:
            half = keep.shape[0] // 2
            self.parts = keep[:half] + got[:half], keep[half:] + got[half:]
        else:
            self.parts = (keep + got,)

    def finish(self):
        while self.stages:
            self.step()
        return self.parts[0]


def tie_sums(values, *sums):
    tied = tie(*values, *[part for one in sums for part in one.parts])
    values, parts = tied[: len(values)], list(tied[len(values) :])
    for one in sums:
        one.parts = tuple(parts.pop(0) for _ in one.parts)
    return values


def owner_kernel(count, width, left_ref, right_ref, out_ref):
    rows = left_ref.shape[1] // count
    left = left_ref[...]
    for unit in range(4):
        product = matmul_tn(left, right_ref[:, unit * width : (unit + 1) * width])
        for owner in range(count):
            place = (owner * 4 + unit) * rows
            out_ref[place : place + rows, :] = product[owner * rows : (owner + 1) * rows, :]


def owner_grads(left, right):
    depth, width = left.shape[1], right.shape[1] // 4
    return pl.pallas_call(
        functools.partial(owner_kernel, lax.axis_size("fsdp"), width),
        out_shape=jax.ShapeDtypeStruct((4 * depth, width), F32),
        in_specs=[vmem_spec()] * 2,
        out_specs=vmem_spec(),
        compiler_params=pltpu.CompilerParams(vmem_limit_bytes=VMEM_LIMIT),
        cost_estimate=cost("owner_grads"),
        name="owner_grads",
    )(left, right)


def share_units(own):
    far = swap(own, ("rep", 2))
    near, cross = swap(own, ("rep", 1)), swap(far, ("rep", 1))
    return jnp.stack([own, near, far, cross])


def scores_of(query, key_rows, valid, scaling):
    scores = matmul_nt(query, key_rows) * scaling
    return jnp.where(valid, scores, -1e30)


def attention_kernel(seq_len, head_dim, q_ref, k_ref, v_ref, out_ref, log_ref):
    rows, model_width = q_ref.shape
    scaling = head_dim**-0.5
    valid = lax.broadcasted_iota(jnp.int32, (rows, rows), 1) < seq_len
    lane = lax.broadcasted_iota(jnp.int32, (rows, 2 * head_dim), 1)
    zero = jnp.zeros((rows, 2 * head_dim), BF16)
    for pair in range(model_width // (2 * head_dim)):
        columns = slice(pair * 2 * head_dim, (pair + 1) * 2 * head_dim)
        query, key_rows, values = q_ref[:, columns], k_ref[:, columns], v_ref[:, columns]
        results = []
        for sub in range(2):
            picked = lane >= head_dim if sub else lane < head_dim
            scores = scores_of(jnp.where(picked, query, zero), key_rows, valid, scaling)
            highest = jnp.max(scores, axis=-1, keepdims=True)
            logsum = highest + jnp.log(jnp.sum(jnp.exp(scores - highest), axis=-1, keepdims=True))
            log_ref[:, 2 * pair + sub : 2 * pair + sub + 1] = logsum
            results.append(matmul(to_low(jnp.exp(scores - logsum)), values))
        out_ref[:, columns] = to_low(jnp.where(lane < head_dim, results[0], results[1]))


def attention_forward(query, key_rows, value_rows, samples, seq_len):
    row_count, model_width = query.shape
    rows = row_count // samples
    head_dim = model_width // HEADS
    block = pl.BlockSpec((rows, model_width), lambda i: (i, 0))
    small = pl.BlockSpec((rows, 128), lambda i: (i, 0))
    return pl.pallas_call(
        functools.partial(attention_kernel, seq_len, head_dim),
        grid=(samples,),
        out_shape=(
            jax.ShapeDtypeStruct(query.shape, BF16),
            jax.ShapeDtypeStruct((row_count, 128), F32),
        ),
        in_specs=[block] * 3,
        out_specs=(block, small),
        compiler_params=pltpu.CompilerParams(vmem_limit_bytes=VMEM_LIMIT),
        cost_estimate=cost("attention"),
        name="attention",
    )(query, key_rows, value_rows)


def attention_back_kernel(
    seq_len, head_dim, q_ref, k_ref, v_ref, da_ref, log_ref, dq_ref, dk_ref, dv_ref
):
    rows, model_width = q_ref.shape
    scaling = head_dim**-0.5
    valid = lax.broadcasted_iota(jnp.int32, (rows, rows), 1) < seq_len
    lane = lax.broadcasted_iota(jnp.int32, (rows, 2 * head_dim), 1)
    zero = jnp.zeros((rows, 2 * head_dim), BF16)
    for pair in range(model_width // (2 * head_dim)):
        columns = slice(pair * 2 * head_dim, (pair + 1) * 2 * head_dim)
        query, key_rows = q_ref[:, columns], k_ref[:, columns]
        values, grad = v_ref[:, columns], da_ref[:, columns]
        results = []
        for sub in range(2):
            picked = lane >= head_dim if sub else lane < head_dim
            scores = scores_of(jnp.where(picked, query, zero), key_rows, valid, scaling)
            soft = jnp.exp(scores - log_ref[:, 2 * pair + sub : 2 * pair + sub + 1])
            grad_soft = matmul_nt(jnp.where(picked, grad, zero), values)
            total = jnp.sum(grad_soft * soft, axis=-1, keepdims=True)
            grad_scores = to_low(soft * (grad_soft - total))
            results.append(
                (
                    matmul(grad_scores, key_rows) * scaling,
                    matmul_tn(grad_scores, query) * scaling,
                    matmul_tn(to_low(soft), grad),
                )
            )
        for target, first, second in zip((dq_ref, dk_ref, dv_ref), *results):
            target[:, columns] = to_low(jnp.where(lane < head_dim, first, second))


def attention_backward(query, key_rows, value_rows, logsum, grad, samples, seq_len):
    row_count, model_width = query.shape
    rows = row_count // samples
    head_dim = model_width // HEADS
    block = pl.BlockSpec((rows, model_width), lambda i: (i, 0))
    small = pl.BlockSpec((rows, 128), lambda i: (i, 0))
    return pl.pallas_call(
        functools.partial(attention_back_kernel, seq_len, head_dim),
        grid=(samples,),
        out_shape=(jax.ShapeDtypeStruct(query.shape, BF16),) * 3,
        in_specs=[block] * 4 + [small],
        out_specs=(block,) * 3,
        compiler_params=pltpu.CompilerParams(vmem_limit_bytes=VMEM_LIMIT),
        cost_estimate=cost("attention_back"),
        name="attention_back",
    )(query, key_rows, value_rows, grad, logsum)


TILE = 256


def tiles(width, body):
    def step(number, carry):
        body(pl.ds(pl.multiple_of(number * TILE, TILE), TILE))
        return carry

    lax.fori_loop(0, width // TILE, step, 0)


def embed_body(samples, masked, base, where_ref, loads, ins, outs, scratch):
    patch_ref, vec_ref, pos_ref = ins[:3]
    hid_ref, low_ref, q_ref, k_ref, v_ref = outs
    weights = loads[0]()
    rows = patch_ref.shape[0] // samples
    width = patch_ref.shape[1]

    def embed(columns):
        product = matmul(patch_ref[...], weights[0, :, columns]) + vec_ref[0:1, columns]
        if masked:
            product = jnp.where(ins[3][...] > 0, vec_ref[1:2, columns], product)
        for s in range(samples):
            part = product[s * rows : (s + 1) * rows] + pos_ref[:, columns]
            hid_ref[s * rows : (s + 1) * rows, columns] = part
            low_ref[s * rows : (s + 1) * rows, columns] = to_low(part)

    tiles(width, embed)

    def project(columns):
        low = low_ref[...]
        q_ref[:, columns] = to_low(
            matmul(low, weights[1, :, columns]) + vec_ref[base : base + 1, columns]
        )
        k_ref[:, columns] = to_low(matmul(low, weights[2, :, columns]))
        v_ref[:, columns] = to_low(
            matmul(low, weights[3, :, columns]) + vec_ref[base + 1 : base + 2, columns]
        )

    tiles(width, project)


def feed_forward(samples, base, unit, loads, ins, student, refs):
    att_ref, hid_ref, vec_ref = ins
    sum_ref, low_ref, act_ref = refs[:3]
    rows, width = hid_ref.shape[0] // samples, hid_ref.shape[1]
    squares = loads[0]()

    def project(columns):
        sum_ref[:, columns] = (
            hid_ref[:, columns]
            + matmul(att_ref[...], squares[unit, :, columns])
            + vec_ref[base + 2 : base + 3, columns]
        )

    tiles(width, project)
    for s in range(samples):
        part = slice(s * rows, (s + 1) * rows)
        hat, inverse = norm_parts(sum_ref[part, :])
        if student:
            refs[3][part, :], refs[4][part, :] = hat, inverse
        normed = hat * vec_ref[base + 3 : base + 4, :] + vec_ref[base + 4 : base + 5, :]
        sum_ref[part, :] = normed
        low_ref[part, :] = to_low(normed)
    up = loads[1]()
    hidden_units = up.shape[1]

    def widen(columns, bias):
        pre_act = matmul(low_ref[...], up[:, columns]) + bias
        value, slope = gelu_exact(pre_act)
        act_ref[:, columns] = to_low(value)
        if student:
            refs[5][:, columns] = slope

    for quarter in range(4):
        size = hidden_units // 4

        def step(number, carry, quarter=quarter):
            inner = pl.ds(pl.multiple_of(number * TILE, TILE), TILE)
            outer = pl.ds(pl.multiple_of(quarter * size + number * TILE, TILE), TILE)
            widen(outer, vec_ref[base + 8 + quarter : base + 9 + quarter, inner])
            return carry

        lax.fori_loop(0, size // TILE, step, 0)
    down = loads[2]()

    def narrow(columns, target_ref, residual):
        branch = (
            matmul_nt(act_ref[...], down[columns, :]) + vec_ref[base + 5 : base + 6, columns]
        )
        target_ref[:, columns] = sum_ref[:, columns] + branch if residual else branch

    return narrow


def teacher_body(samples, seq_len, base, where_ref, loads, ins, outs, scratch):
    target_ref = outs[0]
    narrow = feed_forward(samples, base, 0, loads, ins, False, scratch)
    rows, width = target_ref.shape[0] // samples, target_ref.shape[1]
    tiles(width, lambda columns: narrow(columns, target_ref, False))
    valid = lax.broadcasted_iota(jnp.int32, (rows, width), 0) < seq_len
    for s in range(samples):
        part = slice(s * rows, (s + 1) * rows)
        values = target_ref[part, :]
        total = jnp.sum(jnp.where(valid, values, 0.0), axis=0, keepdims=True)
        centred = values - total * (1.0 / seq_len)
        spread = jnp.sum(jnp.where(valid, centred * centred, 0.0), axis=0, keepdims=True)
        target_ref[part, :] = centred * lax.rsqrt(spread * (1.0 / seq_len) + ln_eps)


def student_body(samples, base, loss_scale, where_ref, loads, ins, outs, scratch):
    target_ref, mask_ref = ins[3:]
    final_ref, dy_ref, gb2_ref, g2_ref, act_ref, slope_ref, low_ref, hat_ref, inv_ref = outs[:9]
    rows_ref, loss_ref = outs[9:]
    sum_ref, hat2_ref, hatf_ref, gf_ref, inv2_ref, invf_ref = scratch
    narrow = feed_forward(
        samples, base, 1, loads, ins[:3], True, (sum_ref, low_ref, act_ref, hat_ref, inv_ref, slope_ref)
    )
    vec_ref = ins[2]
    squares = loads[0]()
    width = sum_ref.shape[1]
    rows = sum_ref.shape[0] // samples
    final_base = base + 12
    tiles(width, lambda columns: narrow(columns, gf_ref, True))
    for s in range(samples):
        part = slice(s * rows, (s + 1) * rows)
        hat, inverse = norm_parts(gf_ref[part, :])
        hat2_ref[part, :], inv2_ref[part, :] = hat, inverse
        result = hat * vec_ref[base + 6 : base + 7, :] + vec_ref[base + 7 : base + 8, :]
        hat, inverse = norm_parts(result)
        hatf_ref[part, :], invf_ref[part, :] = hat, inverse
        final_ref[part, :] = to_low(
            hat * vec_ref[final_base : final_base + 1, :]
            + vec_ref[final_base + 1 : final_base + 2, :]
        )
    rows_ref[...] = jnp.zeros_like(rows_ref)
    loss_ref[...] = jnp.zeros_like(loss_ref)

    def head(columns):
        output = matmul(final_ref[...], squares[2, :, columns])
        residue = output + vec_ref[final_base + 2 : final_base + 3, columns] - target_ref[:, columns]
        magnitude = jnp.abs(residue)
        terms = jnp.where(
            magnitude <= huber_delta,
            0.5 * residue * residue,
            huber_delta * (magnitude - 0.5 * huber_delta),
        )
        loss_ref[...] += jnp.sum(
            jnp.sum(terms * mask_ref[...], axis=0, keepdims=True), axis=1, keepdims=True
        )
        grad = to_low(jnp.clip(residue, -huber_delta, huber_delta) * mask_ref[...] * loss_scale)
        dy_ref[:, columns] = grad
        rows_ref[0:1, columns] = jnp.sum(grad.astype(F32), axis=0, keepdims=True)

    tiles(width, head)

    def back(columns):
        gf_ref[:, columns] = matmul_nt(dy_ref[...], squares[2, columns, :])

    tiles(width, back)
    for s in range(samples):
        part = slice(s * rows, (s + 1) * rows)
        grad, hat = gf_ref[part, :], hatf_ref[part, :]
        rows_ref[1:2, :] += jnp.sum(grad * hat, axis=0, keepdims=True)
        rows_ref[2:3, :] += jnp.sum(grad, axis=0, keepdims=True)
        grad = norm_back(grad, hat, invf_ref[part, :], vec_ref[final_base : final_base + 1, :])
        hat = hat2_ref[part, :]
        rows_ref[3:4, :] += jnp.sum(grad * hat, axis=0, keepdims=True)
        rows_ref[4:5, :] += jnp.sum(grad, axis=0, keepdims=True)
        grad = norm_back(grad, hat, inv2_ref[part, :], vec_ref[base + 6 : base + 7, :])
        g2_ref[part, :] = grad
        low = to_low(grad)
        gb2_ref[part, :] = low
        rows_ref[5:6, :] += jnp.sum(low.astype(F32), axis=0, keepdims=True)


def feed_back_body(samples, base, where_ref, loads, ins, outs, scratch):
    gb2_ref, g2_ref, slope_ref, hat_ref, inv_ref, vec_ref = ins
    gpre_ref, gfirst_ref, gbranch_ref, gatt_ref, rows_ref, up_ref = outs
    grad_ref = scratch[0]
    squares, up, down = loads
    down = down()
    width, hidden_units = down.shape
    rows = gb2_ref.shape[0] // samples

    def widen(columns):
        grad = to_low(matmul(gb2_ref[...], down[:, columns]) * slope_ref[:, columns])
        gpre_ref[:, columns] = grad
        up_ref[:, columns] = jnp.sum(grad.astype(F32), axis=0, keepdims=True)

    tiles(hidden_units, widen)
    up = up()

    def narrow(columns):
        grad_ref[:, columns] = g2_ref[:, columns] + matmul_nt(gpre_ref[...], up[columns, :])

    tiles(width, narrow)
    rows_ref[...] = jnp.zeros_like(rows_ref)
    for s in range(samples):
        part = slice(s * rows, (s + 1) * rows)
        grad, hat = grad_ref[part, :], hat_ref[part, :]
        rows_ref[0:1, :] += jnp.sum(grad * hat, axis=0, keepdims=True)
        rows_ref[1:2, :] += jnp.sum(grad, axis=0, keepdims=True)
        grad = norm_back(grad, hat, inv_ref[part, :], vec_ref[base + 3 : base + 4, :])
        gfirst_ref[part, :] = grad
        low = to_low(grad)
        gbranch_ref[part, :] = low
        rows_ref[2:3, :] += jnp.sum(low.astype(F32), axis=0, keepdims=True)
    squares = squares()

    def project(columns):
        gatt_ref[:, columns] = to_low(matmul_nt(gbranch_ref[...], squares[1, columns, :]))

    tiles(width, project)


def embed_back_body(samples, seq_len, base, stages, where_ref, loads, ins, outs, scratch):
    gq_ref, gk_ref, gv_ref, gfirst_ref, mask_ref, after_ref, inner_ref, up_ref = ins
    ge_ref, keep_ref, send_ref = outs
    all_ref, pos_ref = scratch
    weights = loads[0]()
    width = gq_ref.shape[1]
    rows = gq_ref.shape[0] // samples

    def project(columns):
        grad = gfirst_ref[:, columns] + matmul_nt(gq_ref[...], weights[1, columns, :])
        grad += matmul_nt(gk_ref[...], weights[2, columns, :])
        grad += matmul_nt(gv_ref[...], weights[3, columns, :])
        hidden = grad * mask_ref[...]
        all_ref[1:2, columns] = jnp.sum(hidden, axis=0, keepdims=True)
        low = to_low(grad * (1.0 - mask_ref[...]))
        ge_ref[:, columns] = low
        all_ref[0:1, columns] = jnp.sum(low.astype(F32), axis=0, keepdims=True)
        total = grad[0:rows]
        for s in range(1, samples):
            total += grad[s * rows : (s + 1) * rows]
        pos_ref[:, columns] = total
        all_ref[base : base + 1, columns] = jnp.sum(
            gq_ref[:, columns].astype(F32), axis=0, keepdims=True
        )
        all_ref[base + 1 : base + 2, columns] = jnp.sum(
            gv_ref[:, columns].astype(F32), axis=0, keepdims=True
        )

    tiles(width, project)
    all_ref[2 : 2 + seq_len, :] = pos_ref[0:seq_len, :]
    all_ref[base + 2 : base + 3, :] = inner_ref[2:3, :]
    all_ref[base + 3 : base + 5, :] = inner_ref[0:2, :]
    all_ref[base + 5 : base + 6, :] = after_ref[5:6, :]
    all_ref[base + 6 : base + 8, :] = after_ref[3:5, :]
    for k in range(4):
        all_ref[base + 8 + k : base + 9 + k, :] = up_ref[:, k * width : (k + 1) * width]
    all_ref[base + 12 : base + 14, :] = after_ref[1:3, :]
    all_ref[base + 14 : base + 15, :] = after_ref[0:1, :]
    quarter, size = keep_ref.shape[1:]
    used = base + 15
    all_ref[used:, :] = jnp.zeros_like(all_ref[used:, :])
    for unit in range(4):
        shifted = jnp.bitwise_xor(where_ref[0], unit)
        for other, target in ((0, keep_ref), (1, send_ref)):

            @pl.when(jnp.bitwise_and(shifted, 1) == other)
            def _():
                for f in range(width // size):
                    place = position(stages, shifted, jnp.bitwise_xor(where_ref[1], f))
                    target[place] = all_ref[
                        unit * quarter : (unit + 1) * quarter, f * size : (f + 1) * size
                    ]


def adam_step(master, moment_one, moment_two, gradient, factor):
    clipped = gradient * factor
    one_new = beta_one * moment_one + (1.0 - beta_one) * clipped
    two_new = beta_two * moment_two + (1.0 - beta_two) * clipped * clipped
    one_hat = one_new / (1.0 - beta_one**ADAM_STEP)
    two_hat = two_new / (1.0 - beta_two**ADAM_STEP)
    step_value = -learn_rate * (one_hat / (jnp.sqrt(two_hat) + adam_eps) + decay_rate * master)
    return (step_value, one_new, two_new)


def teacher_move(master, teacher, step_value):
    return (1.0 - ema_keep) * (master - teacher + step_value)


def per_device(
    patches,
    mask_places,
    square_weights,
    square_first,
    square_second,
    square_teacher,
    feed_weights,
    feed_first,
    feed_second,
    feed_teacher,
    vector_weights,
    vector_first,
    vector_second,
    vector_teacher,
):
    samples, seq_len, model_width = patches.shape
    total_masked = samples * mask_places.shape[1] * lax.axis_size("rep") * lax.axis_size("fsdp")
    rep, own = lax.axis_index("rep"), lax.axis_index("fsdp")
    where = jnp.stack([rep, own]).astype(jnp.int32)
    pad_len = -(-seq_len // 8) * 8
    row_count = samples * pad_len
    hidden_units = feed_weights.shape[3]
    patch_rows = jnp.pad(patches, ((0, 0), (0, pad_len - seq_len), (0, 0))).reshape(
        row_count, model_width
    )
    places = jnp.arange(pad_len, dtype=jnp.int32)
    mask_rows = jnp.sum(
        (mask_places[:, :, None] == places[None, None, :]).astype(F32), axis=1
    ).reshape(row_count, 1)

    def pick(array, index):
        return to_low(lax.dynamic_index_in_dim(array, index, keepdims=False))

    def columns_of(array, number):
        width = array.shape[3] // 4
        return to_low(lax.dynamic_slice_in_dim(array[0, number], rep * width, width, axis=1))

    pieces = gather_vectors(jnp.stack([vector_weights, vector_teacher]), where)
    both_s = lax.all_gather(
        jnp.concatenate([columns_of(feed_weights, 0), columns_of(feed_weights, 1)]),
        ("fsdp", "rep"),
        axis=0,
        tiled=True,
    )
    up_s = Gathered(both_s, 0, 2, True, where)
    down_s = Gathered(both_s, 1, 2, True, where)
    others = jnp.where(
        rep == 0, to_low(square_teacher[4]), pick(square_weights, jnp.clip(rep + 3, 4, 5))
    )
    entry_t = Group(pick(square_teacher, rep), 0, False, where)
    entry_s = Group(pick(square_weights, rep), 1, False, where, entry_t)
    outer = Group(others, 0, False, where, entry_s)
    up_t = Group(columns_of(feed_teacher, 0), 1, True, where, outer)
    down_t = Group(columns_of(feed_teacher, 1), 0, True, where, up_t)
    entry_t.step(), entry_t.step()
    (pieces,) = tie_groups([pieces], entry_t)
    vector_old_new = place_vectors(pieces, where)
    vector_all, vector_old = vector_old_new[0], vector_old_new[1]
    for group in (entry_t, entry_s, outer):
        group.fabric()
    for group in (up_t, down_t):
        group.step(), group.step()
    (patch_rows_t,) = tie_groups([patch_rows], up_t)
    base = 2 + seq_len

    def positions(vector):
        return jnp.pad(vector[2 : 2 + seq_len], ((0, pad_len - seq_len), (0, 0)))

    full, low_full = ((row_count, model_width), F32), ((row_count, model_width), BF16)
    low_wide, full_wide = ((row_count, hidden_units), BF16), ((row_count, hidden_units), F32)
    column = ((row_count, 1), F32)

    def entry(patch_rows, group, vector, masked, name):
        return call(
            functools.partial(embed_body, samples, masked, base),
            name,
            where,
            [group],
            [patch_rows, vector, positions(vector)] + ([mask_rows] if masked else []),
            [full] + [low_full] * 4,
        )

    hidden_t, _, query, key_rows, value_rows = entry(
        patch_rows_t, entry_t.finish(), vector_old, False, "embed_t"
    )
    up_t.fabric()
    (query,) = tie_groups([query], down_t)
    down_t.fabric()
    attended_t, _ = attention_forward(query, key_rows, value_rows, samples, seq_len)
    (attended_t,) = tie_groups([attended_t], entry_s, outer)
    hidden, hidden_low, query, key_rows, value_rows = entry(
        patch_rows, entry_s.finish(), vector_all, True, "embed_s"
    )
    attended, logsum = attention_forward(query, key_rows, value_rows, samples, seq_len)
    outer.finish()
    (attended,) = tie_groups([attended], up_t, down_t)
    up_t.finish(), down_t.finish()
    (target,) = call(
        functools.partial(teacher_body, samples, seq_len, base),
        "layer_t",
        where,
        [outer, up_t, down_t],
        [attended_t, hidden_t, vector_old],
        [full],
        [pltpu.VMEM(*full), pltpu.VMEM(*low_full), pltpu.VMEM(*low_wide)],
    )
    loss_scale = 1.0 / (total_masked * model_width)
    (
        final_low,
        grad_output,
        grad_branch_two,
        grad_second,
        activation,
        slope,
        normed_low,
        hat_first,
        inverse_first,
        rows_after,
        loss_sum,
    ) = call(
        functools.partial(student_body, samples, base, loss_scale),
        "layer_s",
        where,
        [outer, up_s, down_s],
        [attended, hidden, vector_all, target, mask_rows],
        [low_full] * 3
        + [full, low_wide, full_wide, low_full, full, column, ((8, model_width), F32), ((1, 1), F32)],
        [pltpu.VMEM(*full)] * 4 + [pltpu.VMEM(*column)] * 2,
    )
    loss_local = loss_sum[0, 0] * loss_scale

    unit = model_width
    down_g = owner_grads(grad_branch_two, activation)
    grad_branch_two, down_g = tie(grad_branch_two, down_g)
    down_own = lax.psum_scatter(down_g, ("fsdp", "rep"), scatter_dimension=0, tiled=True)
    grad_pre, grad_first, grad_branch, grad_attended, rows_inner, rows_up = call(
        functools.partial(feed_back_body, samples, base),
        "feed_back",
        where,
        [outer, up_s, down_s],
        [grad_branch_two, grad_second, slope, hat_first, inverse_first, vector_all],
        [low_wide, full, low_full, low_full, ((8, model_width), F32), ((1, hidden_units), F32)],
        [pltpu.VMEM(*full)],
    )
    half = unit // 2

    def up_half(grad, number):
        places = [[(k * unit + number * half, k) for k in range(4)]]
        return unit_grads([(normed_low, grad)], places, number, half, where)

    up_a = up_half(grad_pre, 0)
    (grad_pre,) = tie_sums([grad_pre], up_a)
    up_b = up_half(grad_pre, 1)
    up_a.step()
    (grad_branch,) = tie_sums([grad_branch], up_a, up_b)
    halves = [[(0, 0), (half, 1)], [(0, 2), (half, 3)]]
    edge_g = unit_grads(
        [(final_low, grad_output), (attended, grad_branch)], halves, 0, half, where
    )
    up_a.step()
    up_b.step()
    (grad_attended,) = tie_sums([grad_attended], up_b, edge_g)
    grad_query, grad_key, grad_value = attention_backward(
        query, key_rows, value_rows, logsum, grad_attended, samples, seq_len
    )
    edge_g.step()
    grad_query, grad_key, grad_value = tie_sums([grad_query, grad_key, grad_value], edge_g)
    up_b.step()
    vector_count = vector_weights.shape[0]
    count = lax.axis_size("fsdp")
    quarter = vector_all.shape[0] // 4
    vector_block = ((2 * count, quarter, model_width // count), F32)
    grad_embed, *vector_g = call(
        functools.partial(embed_back_body, samples, seq_len, base, reduce_order(0)),
        "embed_back",
        where,
        [entry_s],
        [grad_query, grad_key, grad_value, grad_first, mask_rows, rows_after, rows_inner, rows_up],
        [low_full, vector_block, vector_block],
        [pltpu.VMEM(vector_all.shape, F32), pltpu.VMEM((pad_len, model_width), F32)],
    )

    def entry_half(grad, number):
        pairs = [(hidden_low, grad_query), (hidden_low, grad_key), (hidden_low, grad_value), (patch_rows, grad)]
        return unit_grads(pairs, [[(number * half, k)] for k in range(4)], number, half, where)

    vector_g = Summing(*vector_g, 0)
    edge_g.step()
    (grad_embed,) = tie_sums([grad_embed], up_b, up_a)
    qkv_a = entry_half(grad_embed, 0)
    up_b.step()
    up_a.step()
    vector_g.step()
    (grad_embed,) = tie_sums([grad_embed], up_a, edge_g, vector_g, qkv_a)
    qkv_b = entry_half(grad_embed, 1)
    up_a.step()
    edge_g.step()
    qkv_a.step()
    vector_g.step()
    (down_own,) = tie_sums([down_own], qkv_a, qkv_b, up_b, vector_g, up_a)
    qkv_a.step()
    qkv_b.step()
    up_b.step()
    up_a.step()
    vector_g.step()
    tie_sums([], qkv_b, up_b, vector_g)
    qkv_b.step()
    up_b.step()
    vector_g.step()
    tie_sums([], edge_g, vector_g, up_b, qkv_a, qkv_b)
    edge_g.step()

    edge_own = edge_g.finish()
    vector_own = vector_g.finish()
    up_own = jnp.concatenate([up_a.finish(), up_b.finish()], axis=1)
    qkv_own = jnp.concatenate([qkv_a.finish(), qkv_b.finish()], axis=1)
    squares_own = (
        jnp.sum(down_own * down_own)
        + jnp.sum(up_own * up_own)
        + jnp.sum(edge_own * edge_own)
        + jnp.sum(qkv_own * qkv_own)
        + jnp.sum(vector_own * vector_own)
    )
    totals = jnp.stack([squares_own, loss_local])
    for bit in fsdp_bits():
        totals = totals + swap(totals, ("fsdp", bit))
    for bit in (2, 1):
        totals = totals + swap(totals, ("rep", bit))
    norm_squared, loss_value = totals[0], totals[1]

    def ordered(own_units):
        shared = share_units(own_units)
        return [lax.dynamic_index_in_dim(shared, rep ^ k, keepdims=False) for k in range(4)]

    early_u = ordered(jnp.concatenate([down_own, up_own, edge_own], axis=1))
    late_u = ordered(
        jnp.concatenate([qkv_own, vector_own.reshape(qkv_own.shape[0], quarter)], axis=1)
    )
    qkv_u = [own[:, :unit] for own in late_u]
    vector_share = jnp.concatenate(
        [own[:, unit:].reshape(vector_own.shape[1:]) for own in late_u], axis=0
    )[:vector_count]
    down_u = [own[:, :unit] for own in early_u]
    up_u = [own[:, unit : 2 * unit] for own in early_u]
    edge_u = [own[:, 2 * unit :] for own in early_u]
    feed_grad = jnp.stack([jnp.concatenate(up_u, axis=1), jnp.concatenate(down_u, axis=1)])[None]
    square_grad = jnp.stack(
        [
            qkv_u[3],
            qkv_u[0],
            qkv_u[1],
            qkv_u[2],
            jnp.concatenate(edge_u[2:], axis=1),
            jnp.concatenate(edge_u[:2], axis=1),
        ]
    )
    grad_norm = jnp.sqrt(norm_squared)
    limit = clip_scale / math.sqrt(total_masked)
    factor = limit / jnp.maximum(grad_norm, limit)
    square_step, square_one, square_two = adam_step(
        square_weights, square_first, square_second, square_grad, factor
    )
    feed_step, feed_one, feed_two = adam_step(
        feed_weights, feed_first, feed_second, feed_grad, factor
    )
    vector_step, vector_one, vector_two = adam_step(
        vector_weights, vector_first, vector_second, vector_share, factor
    )
    square_moved = teacher_move(square_weights, square_teacher, square_step)
    feed_moved = teacher_move(feed_weights, feed_teacher, feed_step)
    vector_moved = teacher_move(vector_weights, vector_teacher, vector_step)
    return (
        loss_value,
        grad_norm,
        square_step,
        square_one,
        square_two,
        square_moved,
        feed_step,
        feed_one,
        feed_two,
        feed_moved,
        vector_step,
        vector_one,
        vector_two,
        vector_moved,
    )


def solution(mesh):
    placed = (
        P(("rep", "fsdp"), None, None),
        P(("rep", "fsdp"), None),
        P(None, "fsdp", None),
        P(None, "fsdp", None),
        P(None, "fsdp", None),
        P(None, "fsdp", None),
        P(None, None, "fsdp", None),
        P(None, None, "fsdp", None),
        P(None, None, "fsdp", None),
        P(None, None, "fsdp", None),
        P(None, "fsdp"),
        P(None, "fsdp"),
        P(None, "fsdp"),
        P(None, "fsdp"),
    )
    return jax.shard_map(
        per_device,
        mesh=mesh,
        in_specs=placed,
        out_specs=(
            P(),
            P(),
            P(None, "fsdp", None),
            P(None, "fsdp", None),
            P(None, "fsdp", None),
            P(None, "fsdp", None),
            P(None, None, "fsdp", None),
            P(None, None, "fsdp", None),
            P(None, None, "fsdp", None),
            P(None, None, "fsdp", None),
            P(None, "fsdp"),
            P(None, "fsdp"),
            P(None, "fsdp"),
            P(None, "fsdp"),
        ),
        check_vma=False,
    )
```

```python
import functools
import math

import jax
import jax.numpy as jnp
from jax import lax
from jax.experimental import pallas as pl
from jax.experimental.pallas import tpu as pltpu
from jax.sharding import PartitionSpec as P

HEADS = 12
ADAM_STEP = 10


ln_eps = 1e-05
beta_one = 0.9
beta_two = 0.999
adam_eps = 1e-08
learn_rate = 0.01
decay_rate = 0.05
ema_keep = 0.999
huber_delta = 1.0
clip_scale = 1.25

VMEM_LIMIT = 60 * 1024 * 1024
SHARE = 0.0
MICROSECONDS = dict(
    gather_vectors=3,
    embed_t=9,
    embed_s=9,
    attention=7,
    layer_t=23,
    layer_s=33,
    owner_grads=8,
    feed_back=23,
    unit_grads=7,
    attention_back=16,
    embed_back=9,
)


def cost(name):
    flops = int(SHARE * MICROSECONDS[name] * 1.15e9)
    return pl.CostEstimate(flops=flops, bytes_accessed=1024, transcendentals=0)
BF16 = jnp.bfloat16
F32 = jnp.float32


def to_low(values):
    return values.astype(BF16)


def matmul(left, right):
    return jnp.dot(left, right, preferred_element_type=F32)


def matmul_tn(left, right):
    return lax.dot_general(left, right, (((0,), (0,)), ((), ())), preferred_element_type=F32)


def matmul_nt(left, right):
    return lax.dot_general(left, right, (((1,), (1,)), ((), ())), preferred_element_type=F32)


tail_scale = 0.21
tail_terms = (
    0.08371158707086396,
    0.08506867712628283,
    0.06919339848407204,
    0.1248680487092072,
    -0.09391427181816406,
    0.34938494294095396,
    -0.3302388882989717,
    0.2835812219436135,
    -0.07165470896901999,
)


def gelu_exact(values):
    t = 1.0 / (1.0 + tail_scale * jnp.abs(values))
    tail = jnp.full_like(t, tail_terms[-1])
    for term in tail_terms[-2::-1]:
        tail = tail * t + term
    bell = jnp.exp(-0.5 * (values * values))
    tail = tail * t * bell
    normal = jnp.where(values < 0, tail, 1.0 - tail)
    return values * normal, normal + values * bell * (1.0 / math.sqrt(2.0 * math.pi))


def norm_parts(values):
    centred = values - jnp.mean(values, axis=-1, keepdims=True)
    inverse = lax.rsqrt(jnp.mean(centred * centred, axis=-1, keepdims=True) + ln_eps)
    return centred * inverse, inverse


def norm_back(grad, hat, inverse, gain):
    scaled = grad * gain
    return inverse * (
        scaled
        - jnp.mean(scaled, axis=-1, keepdims=True)
        - hat * jnp.mean(scaled * hat, axis=-1, keepdims=True)
    )


def any_spec():
    return pl.BlockSpec(memory_space=pl.ANY)


def vmem_spec():
    return pl.BlockSpec(memory_space=pltpu.VMEM)


def smem_spec():
    return pl.BlockSpec(memory_space=pltpu.SMEM)


def swap(values, stage):
    axis, bit = stage
    return lax.ppermute(values, axis, [(i, i ^ bit) for i in range(lax.axis_size(axis))])


def fsdp_bits():
    count = lax.axis_size("fsdp")
    return [1 << k for k in reversed(range(count.bit_length() - 1))]


def stage_order(kind):
    stages = [("fsdp", bit) for bit in fsdp_bits()]
    place = len(stages) if kind == 0 else len(stages) - 1
    return stages[:place] + [("rep", 2)] + stages[place:]


def tie(*values):
    return lax.optimization_barrier(values)


class Group:
    def __init__(self, mine, kind, wide, where, before=None):
        self.wide, self.where = wide, where
        self.rows, self.width = mine.shape
        count = lax.axis_size("fsdp")
        depth = self.rows * count
        self.shape = (depth, 4 * self.width) if wide else (4, depth, self.width)
        self.blocks = 4 * count
        if before is not None:
            mine, before.arrays[0] = tie(mine, before.arrays[0])
        self.arrays, self.labels = [mine], [[(0, 0)]]
        self.stages = stage_order(kind)
        self.step()

    def step(self):
        axis, bit = self.stages.pop(0)
        got = swap(self.arrays[0], (axis, bit))
        moved = [
            (u ^ bit, e) if axis == "rep" else (u, e ^ bit) for u, e in self.labels[0]
        ]
        if self.stages:
            self.arrays = [jnp.concatenate([self.arrays[0], got], axis=0)]
            self.labels = [self.labels[0] + moved]
        else:
            self.arrays, self.labels = self.arrays + [got], self.labels + [moved]

    def fabric(self):
        while self.stages:
            self.step()
        return self

    def finish(self):
        self.arrays = self.arrays + [swap(a, ("rep", 1)) for a in self.arrays]
        self.labels = self.labels + [[(u ^ 1, e) for u, e in block] for block in self.labels]
        if self.rows % 16:
            count = lax.axis_size("fsdp")
            flat = jnp.concatenate(self.arrays, axis=0).reshape(-1, self.rows, self.width)
            order = [label for block in self.labels for label in block]
            place = {label: number for number, label in enumerate(order)}
            table = jnp.array(
                [[place[(u, e)] for e in range(count)] for u in range(4)], jnp.int32
            )
            units = jnp.arange(4, dtype=jnp.int32)[:, None] ^ self.where[0]
            owners = jnp.arange(count, dtype=jnp.int32)[None] ^ self.where[1]
            whole = flat[table[units, owners]].reshape(4, -1, self.width)
            self.whole(whole)
        return self

    def whole(self, units):
        if self.wide:
            units = units.transpose(1, 0, 2).reshape(self.shape)
        self.arrays, self.labels, self.blocks = [units], None, 1

    def copies(self, where_ref, arrays, out, sems):
        if self.labels is None:
            return [pltpu.make_async_copy(arrays[0], out, sems.at[0])]
        rep, own = where_ref[0], where_ref[1]
        copies = []
        for array, block in zip(arrays, self.labels):
            for number, (u, e) in enumerate(block):
                unit = jnp.bitwise_xor(rep, u)
                rows = pl.ds(pl.multiple_of(jnp.bitwise_xor(own, e) * self.rows, 16), self.rows)
                if self.wide:
                    columns = pl.ds(pl.multiple_of(unit * self.width, 128), self.width)
                    target = out.at[rows, columns]
                else:
                    target = out.at[unit, rows, :]
                source = array.at[pl.ds(number * self.rows, self.rows), :]
                copies.append(pltpu.make_async_copy(source, target, sems.at[len(copies)]))
        return copies


def tie_groups(values, *groups):
    tied = tie(*values, *[array for group in groups for array in group.arrays])
    values, arrays = tied[: len(values)], list(tied[len(values) :])
    for group in groups:
        group.arrays = [arrays.pop(0) for _ in group.arrays]
    return values


class Gathered(Group):
    def __init__(self, gathered, number, groups, wide, where):
        count = lax.axis_size("fsdp")
        self.wide, self.where = wide, where
        self.rows, self.width = gathered.shape[0] // (4 * count * groups), gathered.shape[1]
        depth = self.rows * count
        self.shape = (depth, 4 * self.width) if wide else (4, depth, self.width)
        self.arrays, self.labels, self.blocks = [gathered], (), 4 * count
        self.number, self.groups = number, groups
        if self.rows % 16:
            blocks = gathered.reshape(count, 4, groups, self.rows, self.width)[:, :, number]
            self.whole(blocks.transpose(1, 0, 2, 3).reshape(4, depth, self.width))

    def copies(self, where_ref, arrays, out, sems):
        if self.labels is None:
            return [pltpu.make_async_copy(arrays[0], out, sems.at[0])]
        copies = []
        for place in range(self.blocks):
            owner, unit = place // 4, place % 4
            rows = slice(owner * self.rows, (owner + 1) * self.rows)
            if self.wide:
                target = out.at[rows, unit * self.width : (unit + 1) * self.width]
            else:
                target = out.at[unit, rows, :]
            first = (place * self.groups + self.number) * self.rows
            source = arrays[0].at[first : first + self.rows, :]
            copies.append(pltpu.make_async_copy(source, target, sems.at[place]))
        return copies


class Loading:
    def __init__(self, copies, ref):
        self.pending, self.ref = copies, ref
        for copy in copies:
            copy.start()

    def __call__(self):
        for copy in self.pending:
            copy.wait()
        self.pending = []
        return self.ref


def call(body, name, where, groups, ins, outs, scratch=()):
    sizes = [len(group.arrays) for group in groups]

    def kernel(where_ref, *refs):
        refs = list(refs)
        arrays = [[refs.pop(0) for _ in range(size)] for size in sizes]
        in_refs = [refs.pop(0) for _ in ins]
        out_refs = [refs.pop(0) for _ in outs]
        places = [refs.pop(0) for _ in groups]
        sems = [refs.pop(0) for _ in groups]
        loads = [
            Loading(group.copies(where_ref, given, place, sem), place)
            for group, given, place, sem in zip(groups, arrays, places, sems)
        ]
        body(where_ref, loads, in_refs, out_refs, refs)

    return pl.pallas_call(
        kernel,
        out_shape=tuple(jax.ShapeDtypeStruct(*out) for out in outs),
        in_specs=[smem_spec()] + [any_spec()] * sum(sizes) + [vmem_spec()] * len(ins),
        out_specs=(vmem_spec(),) * len(outs),
        scratch_shapes=[pltpu.VMEM(group.shape, BF16) for group in groups]
        + [pltpu.SemaphoreType.DMA((group.blocks,)) for group in groups]
        + list(scratch),
        compiler_params=pltpu.CompilerParams(vmem_limit_bytes=VMEM_LIMIT),
        cost_estimate=cost(name),
        name=name,
    )(where, *[array for group in groups for array in group.arrays], *ins)


def vector_kernel(where_ref, pieces_ref, out_ref):
    _, two, rows, width = pieces_ref.shape
    count = pieces_ref.shape[0] // 4
    for u in range(4):
        for k in range(count):
            place = jnp.bitwise_xor(where_ref[0], u) * count + jnp.bitwise_xor(where_ref[1], k)
            out_ref[:, u * rows : (u + 1) * rows, k * width : (k + 1) * width] = pieces_ref[place]


def gather_vectors(both, where):
    rows = -(-both.shape[1] // 32) * 8
    both = jnp.pad(both, ((0, 0), (0, 4 * rows - both.shape[1]), (0, 0)))
    pieces = lax.dynamic_slice_in_dim(both, where[0] * rows, rows, axis=1)[None]
    for stage in [("fsdp", bit) for bit in reversed(fsdp_bits())] + [("rep", 1), ("rep", 2)]:
        pieces = jnp.concatenate([pieces, swap(pieces, stage)], axis=0)
    return pieces


def place_vectors(pieces, where):
    count, two, rows, width = pieces.shape
    return pl.pallas_call(
        vector_kernel,
        out_shape=jax.ShapeDtypeStruct((two, 4 * rows, count // 4 * width), pieces.dtype),
        in_specs=[smem_spec(), vmem_spec()],
        out_specs=vmem_spec(),
        compiler_params=pltpu.CompilerParams(vmem_limit_bytes=VMEM_LIMIT),
        cost_estimate=cost("gather_vectors"),
        name="gather_vectors",
    )(where, pieces)


def reduce_order(kind):
    stages = [("fsdp", bit) for bit in reversed(fsdp_bits())]
    place = 0 if kind == 0 else 1
    return stages[:place] + [("rep", 2)] + stages[place:]


def position(stages, unit, owner):
    place = 0
    for axis, bit in stages:
        value = unit if axis == "rep" else owner
        place = place * 2 + jnp.where(jnp.bitwise_and(value, bit) != 0, 1, 0)
    return place


def grad_kernel(unit_of, kind_stages, rows, width, where_ref, *refs):
    count = len(unit_of)
    lefts, rights = refs[:count], refs[count : 2 * count]
    keep, send = refs[2 * count], refs[2 * count + 1]
    rep, own = where_ref[0], where_ref[1]
    owners = lefts[0].shape[1] // rows
    for pair in range(count):
        left = lefts[pair][...]
        for column, unit in unit_of[pair]:
            product = matmul_tn(left, rights[pair][:, column : column + width])
            shifted = jnp.bitwise_xor(rep, unit)
            for other, target in ((0, keep), (1, send)):

                @pl.when(jnp.bitwise_and(shifted, 1) == other)
                def _():
                    for f in range(owners):
                        place = position(kind_stages, shifted, jnp.bitwise_xor(own, f))
                        target[pl.ds(pl.multiple_of(place * rows, 8), rows), :] = product[
                            f * rows : (f + 1) * rows, :
                        ]


def unit_grads(pairs, unit_of, kind, width, where):
    depth = pairs[0][0].shape[1]
    rows = depth // lax.axis_size("fsdp")
    shape = jax.ShapeDtypeStruct((2 * depth, width), F32)
    return Summing(
        *pl.pallas_call(
            functools.partial(grad_kernel, unit_of, reduce_order(kind), rows, width),
            out_shape=(shape, shape),
            in_specs=[smem_spec()] + [vmem_spec()] * (2 * len(pairs)),
            out_specs=(vmem_spec(), vmem_spec()),
            compiler_params=pltpu.CompilerParams(vmem_limit_bytes=VMEM_LIMIT),
            cost_estimate=cost("unit_grads"),
            name="unit_grads",
        )(where, *[left for left, _ in pairs], *[right for _, right in pairs]),
        kind,
    )


class Summing:
    def __init__(self, keep, send, kind):
        self.parts, self.stages = (keep, send), [("rep", 1)] + reduce_order(kind)

    def step(self):
        keep, send = self.parts
        got = swap(send, self.stages.pop(0))
        if self.stages:
            half = keep.shape[0] // 2
            self.parts = keep[:half] + got[:half], keep[half:] + got[half:]
        else:
            self.parts = (keep + got,)

    def finish(self):
        while self.stages:
            self.step()
        return self.parts[0]


def tie_sums(values, *sums):
    tied = tie(*values, *[part for one in sums for part in one.parts])
    values, parts = tied[: len(values)], list(tied[len(values) :])
    for one in sums:
        one.parts = tuple(parts.pop(0) for _ in one.parts)
    return values


def owner_kernel(count, width, left_ref, right_ref, out_ref):
    rows = left_ref.shape[1] // count
    left = left_ref[...]
    for unit in range(4):
        product = matmul_tn(left, right_ref[:, unit * width : (unit + 1) * width])
        for owner in range(count):
            place = (owner * 4 + unit) * rows
            out_ref[place : place + rows, :] = product[owner * rows : (owner + 1) * rows, :]


def owner_grads(left, right):
    depth, width = left.shape[1], right.shape[1] // 4
    return pl.pallas_call(
        functools.partial(owner_kernel, lax.axis_size("fsdp"), width),
        out_shape=jax.ShapeDtypeStruct((4 * depth, width), F32),
        in_specs=[vmem_spec()] * 2,
        out_specs=vmem_spec(),
        compiler_params=pltpu.CompilerParams(vmem_limit_bytes=VMEM_LIMIT),
        cost_estimate=cost("owner_grads"),
        name="owner_grads",
    )(left, right)


def share_units(own):
    far = swap(own, ("rep", 2))
    near, cross = swap(own, ("rep", 1)), swap(far, ("rep", 1))
    return jnp.stack([own, near, far, cross])


def scores_of(query, key_rows, valid, scaling):
    scores = matmul_nt(query, key_rows) * scaling
    return jnp.where(valid, scores, -1e30)


def attention_kernel(seq_len, head_dim, q_ref, k_ref, v_ref, out_ref, log_ref):
    rows, model_width = q_ref.shape
    scaling = head_dim**-0.5
    valid = lax.broadcasted_iota(jnp.int32, (rows, rows), 1) < seq_len
    lane = lax.broadcasted_iota(jnp.int32, (rows, 2 * head_dim), 1)
    zero = jnp.zeros((rows, 2 * head_dim), BF16)
    for pair in range(model_width // (2 * head_dim)):
        columns = slice(pair * 2 * head_dim, (pair + 1) * 2 * head_dim)
        query, key_rows, values = q_ref[:, columns], k_ref[:, columns], v_ref[:, columns]
        results = []
        for sub in range(2):
            picked = lane >= head_dim if sub else lane < head_dim
            scores = scores_of(jnp.where(picked, query, zero), key_rows, valid, scaling)
            highest = jnp.max(scores, axis=-1, keepdims=True)
            logsum = highest + jnp.log(jnp.sum(jnp.exp(scores - highest), axis=-1, keepdims=True))
            log_ref[:, 2 * pair + sub : 2 * pair + sub + 1] = logsum
            results.append(matmul(to_low(jnp.exp(scores - logsum)), values))
        out_ref[:, columns] = to_low(jnp.where(lane < head_dim, results[0], results[1]))


def attention_forward(query, key_rows, value_rows, samples, seq_len):
    row_count, model_width = query.shape
    rows = row_count // samples
    head_dim = model_width // HEADS
    block = pl.BlockSpec((rows, model_width), lambda i: (i, 0))
    small = pl.BlockSpec((rows, 128), lambda i: (i, 0))
    return pl.pallas_call(
        functools.partial(attention_kernel, seq_len, head_dim),
        grid=(samples,),
        out_shape=(
            jax.ShapeDtypeStruct(query.shape, BF16),
            jax.ShapeDtypeStruct((row_count, 128), F32),
        ),
        in_specs=[block] * 3,
        out_specs=(block, small),
        compiler_params=pltpu.CompilerParams(vmem_limit_bytes=VMEM_LIMIT),
        cost_estimate=cost("attention"),
        name="attention",
    )(query, key_rows, value_rows)


def attention_back_kernel(
    seq_len, head_dim, q_ref, k_ref, v_ref, da_ref, log_ref, dq_ref, dk_ref, dv_ref
):
    rows, model_width = q_ref.shape
    scaling = head_dim**-0.5
    valid = lax.broadcasted_iota(jnp.int32, (rows, rows), 1) < seq_len
    lane = lax.broadcasted_iota(jnp.int32, (rows, 2 * head_dim), 1)
    zero = jnp.zeros((rows, 2 * head_dim), BF16)
    for pair in range(model_width // (2 * head_dim)):
        columns = slice(pair * 2 * head_dim, (pair + 1) * 2 * head_dim)
        query, key_rows = q_ref[:, columns], k_ref[:, columns]
        values, grad = v_ref[:, columns], da_ref[:, columns]
        results = []
        for sub in range(2):
            picked = lane >= head_dim if sub else lane < head_dim
            scores = scores_of(jnp.where(picked, query, zero), key_rows, valid, scaling)
            soft = jnp.exp(scores - log_ref[:, 2 * pair + sub : 2 * pair + sub + 1])
            grad_soft = matmul_nt(jnp.where(picked, grad, zero), values)
            total = jnp.sum(grad_soft * soft, axis=-1, keepdims=True)
            grad_scores = to_low(soft * (grad_soft - total))
            results.append(
                (
                    matmul(grad_scores, key_rows) * scaling,
                    matmul_tn(grad_scores, query) * scaling,
                    matmul_tn(to_low(soft), grad),
                )
            )
        for target, first, second in zip((dq_ref, dk_ref, dv_ref), *results):
            target[:, columns] = to_low(jnp.where(lane < head_dim, first, second))


def attention_backward(query, key_rows, value_rows, logsum, grad, samples, seq_len):
    row_count, model_width = query.shape
    rows = row_count // samples
    head_dim = model_width // HEADS
    block = pl.BlockSpec((rows, model_width), lambda i: (i, 0))
    small = pl.BlockSpec((rows, 128), lambda i: (i, 0))
    return pl.pallas_call(
        functools.partial(attention_back_kernel, seq_len, head_dim),
        grid=(samples,),
        out_shape=(jax.ShapeDtypeStruct(query.shape, BF16),) * 3,
        in_specs=[block] * 4 + [small],
        out_specs=(block,) * 3,
        compiler_params=pltpu.CompilerParams(vmem_limit_bytes=VMEM_LIMIT),
        cost_estimate=cost("attention_back"),
        name="attention_back",
    )(query, key_rows, value_rows, grad, logsum)


TILE = 256
UNROLL = 3


def tiles(width, body):
    def step(number, carry):
        body(pl.ds(pl.multiple_of(number * TILE, TILE), TILE))
        return carry

    lax.fori_loop(0, width // TILE, step, 0, unroll=min(UNROLL, width // TILE))


def embed_body(samples, masked, base, where_ref, loads, ins, outs, scratch):
    patch_ref, vec_ref, pos_ref = ins[:3]
    hid_ref, low_ref, q_ref, k_ref, v_ref = outs
    weights = loads[0]()
    rows = patch_ref.shape[0] // samples
    width = patch_ref.shape[1]

    def embed(columns):
        product = matmul(patch_ref[...], weights[0, :, columns]) + vec_ref[0:1, columns]
        if masked:
            product = jnp.where(ins[3][...] > 0, vec_ref[1:2, columns], product)
        for s in range(samples):
            part = product[s * rows : (s + 1) * rows] + pos_ref[:, columns]
            hid_ref[s * rows : (s + 1) * rows, columns] = part
            low_ref[s * rows : (s + 1) * rows, columns] = to_low(part)

    tiles(width, embed)

    def project(columns):
        low = low_ref[...]
        q_ref[:, columns] = to_low(
            matmul(low, weights[1, :, columns]) + vec_ref[base : base + 1, columns]
        )
        k_ref[:, columns] = to_low(matmul(low, weights[2, :, columns]))
        v_ref[:, columns] = to_low(
            matmul(low, weights[3, :, columns]) + vec_ref[base + 1 : base + 2, columns]
        )

    tiles(width, project)


def feed_forward(samples, base, unit, loads, ins, student, refs):
    att_ref, hid_ref, vec_ref = ins
    sum_ref, low_ref, act_ref = refs[:3]
    rows, width = hid_ref.shape[0] // samples, hid_ref.shape[1]
    squares = loads[0]()

    def project(columns):
        sum_ref[:, columns] = (
            hid_ref[:, columns]
            + matmul(att_ref[...], squares[unit, :, columns])
            + vec_ref[base + 2 : base + 3, columns]
        )

    tiles(width, project)
    for s in range(samples):
        part = slice(s * rows, (s + 1) * rows)
        hat, inverse = norm_parts(sum_ref[part, :])
        if student:
            refs[3][part, :], refs[4][part, :] = hat, inverse
        normed = hat * vec_ref[base + 3 : base + 4, :] + vec_ref[base + 4 : base + 5, :]
        sum_ref[part, :] = normed
        low_ref[part, :] = to_low(normed)
    up = loads[1]()
    hidden_units = up.shape[1]

    def widen(columns, bias):
        pre_act = matmul(low_ref[...], up[:, columns]) + bias
        value, slope = gelu_exact(pre_act)
        act_ref[:, columns] = to_low(value)
        if student:
            refs[5][:, columns] = slope

    for quarter in range(4):
        size = hidden_units // 4

        def step(number, carry, quarter=quarter):
            inner = pl.ds(pl.multiple_of(number * TILE, TILE), TILE)
            outer = pl.ds(pl.multiple_of(quarter * size + number * TILE, TILE), TILE)
            widen(outer, vec_ref[base + 8 + quarter : base + 9 + quarter, inner])
            return carry

        lax.fori_loop(0, size // TILE, step, 0, unroll=min(UNROLL, size // TILE))
    down = loads[2]()

    def narrow(columns, target_ref, residual):
        branch = (
            matmul_nt(act_ref[...], down[columns, :]) + vec_ref[base + 5 : base + 6, columns]
        )
        target_ref[:, columns] = sum_ref[:, columns] + branch if residual else branch

    return narrow


def teacher_body(samples, seq_len, base, where_ref, loads, ins, outs, scratch):
    target_ref = outs[0]
    narrow = feed_forward(samples, base, 0, loads, ins, False, scratch)
    rows, width = target_ref.shape[0] // samples, target_ref.shape[1]
    tiles(width, lambda columns: narrow(columns, target_ref, False))
    valid = lax.broadcasted_iota(jnp.int32, (rows, width), 0) < seq_len
    for s in range(samples):
        part = slice(s * rows, (s + 1) * rows)
        values = target_ref[part, :]
        total = jnp.sum(jnp.where(valid, values, 0.0), axis=0, keepdims=True)
        centred = values - total * (1.0 / seq_len)
        spread = jnp.sum(jnp.where(valid, centred * centred, 0.0), axis=0, keepdims=True)
        target_ref[part, :] = centred * lax.rsqrt(spread * (1.0 / seq_len) + ln_eps)


def student_body(samples, base, loss_scale, where_ref, loads, ins, outs, scratch):
    target_ref, mask_ref = ins[3:]
    final_ref, dy_ref, gb2_ref, g2_ref, act_ref, slope_ref, low_ref, hat_ref, inv_ref = outs[:9]
    rows_ref, loss_ref = outs[9:]
    sum_ref, hat2_ref, hatf_ref, gf_ref, inv2_ref, invf_ref = scratch
    narrow = feed_forward(
        samples, base, 1, loads, ins[:3], True, (sum_ref, low_ref, act_ref, hat_ref, inv_ref, slope_ref)
    )
    vec_ref = ins[2]
    squares = loads[0]()
    width = sum_ref.shape[1]
    rows = sum_ref.shape[0] // samples
    final_base = base + 12
    tiles(width, lambda columns: narrow(columns, gf_ref, True))
    for s in range(samples):
        part = slice(s * rows, (s + 1) * rows)
        hat, inverse = norm_parts(gf_ref[part, :])
        hat2_ref[part, :], inv2_ref[part, :] = hat, inverse
        result = hat * vec_ref[base + 6 : base + 7, :] + vec_ref[base + 7 : base + 8, :]
        hat, inverse = norm_parts(result)
        hatf_ref[part, :], invf_ref[part, :] = hat, inverse
        final_ref[part, :] = to_low(
            hat * vec_ref[final_base : final_base + 1, :]
            + vec_ref[final_base + 1 : final_base + 2, :]
        )
    rows_ref[...] = jnp.zeros_like(rows_ref)
    loss_ref[...] = jnp.zeros_like(loss_ref)

    def head(columns):
        output = matmul(final_ref[...], squares[2, :, columns])
        residue = output + vec_ref[final_base + 2 : final_base + 3, columns] - target_ref[:, columns]
        magnitude = jnp.abs(residue)
        terms = jnp.where(
            magnitude <= huber_delta,
            0.5 * residue * residue,
            huber_delta * (magnitude - 0.5 * huber_delta),
        )
        loss_ref[...] += jnp.sum(
            jnp.sum(terms * mask_ref[...], axis=0, keepdims=True), axis=1, keepdims=True
        )
        grad = to_low(jnp.clip(residue, -huber_delta, huber_delta) * mask_ref[...] * loss_scale)
        dy_ref[:, columns] = grad
        rows_ref[0:1, columns] = jnp.sum(grad.astype(F32), axis=0, keepdims=True)

    tiles(width, head)

    def back(columns):
        gf_ref[:, columns] = matmul_nt(dy_ref[...], squares[2, columns, :])

    tiles(width, back)
    for s in range(samples):
        part = slice(s * rows, (s + 1) * rows)
        grad, hat = gf_ref[part, :], hatf_ref[part, :]
        rows_ref[1:2, :] += jnp.sum(grad * hat, axis=0, keepdims=True)
        rows_ref[2:3, :] += jnp.sum(grad, axis=0, keepdims=True)
        grad = norm_back(grad, hat, invf_ref[part, :], vec_ref[final_base : final_base + 1, :])
        hat = hat2_ref[part, :]
        rows_ref[3:4, :] += jnp.sum(grad * hat, axis=0, keepdims=True)
        rows_ref[4:5, :] += jnp.sum(grad, axis=0, keepdims=True)
        grad = norm_back(grad, hat, inv2_ref[part, :], vec_ref[base + 6 : base + 7, :])
        g2_ref[part, :] = grad
        low = to_low(grad)
        gb2_ref[part, :] = low
        rows_ref[5:6, :] += jnp.sum(low.astype(F32), axis=0, keepdims=True)


def feed_back_body(samples, base, where_ref, loads, ins, outs, scratch):
    gb2_ref, g2_ref, slope_ref, hat_ref, inv_ref, vec_ref = ins
    gpre_ref, gfirst_ref, gbranch_ref, gatt_ref, rows_ref, up_ref = outs
    grad_ref = scratch[0]
    squares, up, down = loads
    down = down()
    width, hidden_units = down.shape
    rows = gb2_ref.shape[0] // samples

    def widen(columns):
        grad = to_low(matmul(gb2_ref[...], down[:, columns]) * slope_ref[:, columns])
        gpre_ref[:, columns] = grad
        up_ref[:, columns] = jnp.sum(grad.astype(F32), axis=0, keepdims=True)

    tiles(hidden_units, widen)
    up = up()

    def narrow(columns):
        grad_ref[:, columns] = g2_ref[:, columns] + matmul_nt(gpre_ref[...], up[columns, :])

    tiles(width, narrow)
    rows_ref[...] = jnp.zeros_like(rows_ref)
    for s in range(samples):
        part = slice(s * rows, (s + 1) * rows)
        grad, hat = grad_ref[part, :], hat_ref[part, :]
        rows_ref[0:1, :] += jnp.sum(grad * hat, axis=0, keepdims=True)
        rows_ref[1:2, :] += jnp.sum(grad, axis=0, keepdims=True)
        grad = norm_back(grad, hat, inv_ref[part, :], vec_ref[base + 3 : base + 4, :])
        gfirst_ref[part, :] = grad
        low = to_low(grad)
        gbranch_ref[part, :] = low
        rows_ref[2:3, :] += jnp.sum(low.astype(F32), axis=0, keepdims=True)
    squares = squares()

    def project(columns):
        gatt_ref[:, columns] = to_low(matmul_nt(gbranch_ref[...], squares[1, columns, :]))

    tiles(width, project)


def embed_back_body(samples, seq_len, base, stages, where_ref, loads, ins, outs, scratch):
    gq_ref, gk_ref, gv_ref, gfirst_ref, mask_ref, after_ref, inner_ref, up_ref = ins
    ge_ref, keep_ref, send_ref = outs
    all_ref, pos_ref = scratch
    weights = loads[0]()
    width = gq_ref.shape[1]
    rows = gq_ref.shape[0] // samples

    def project(columns):
        grad = gfirst_ref[:, columns] + matmul_nt(gq_ref[...], weights[1, columns, :])
        grad += matmul_nt(gk_ref[...], weights[2, columns, :])
        grad += matmul_nt(gv_ref[...], weights[3, columns, :])
        hidden = grad * mask_ref[...]
        all_ref[1:2, columns] = jnp.sum(hidden, axis=0, keepdims=True)
        low = to_low(grad * (1.0 - mask_ref[...]))
        ge_ref[:, columns] = low
        all_ref[0:1, columns] = jnp.sum(low.astype(F32), axis=0, keepdims=True)
        total = grad[0:rows]
        for s in range(1, samples):
            total += grad[s * rows : (s + 1) * rows]
        pos_ref[:, columns] = total
        all_ref[base : base + 1, columns] = jnp.sum(
            gq_ref[:, columns].astype(F32), axis=0, keepdims=True
        )
        all_ref[base + 1 : base + 2, columns] = jnp.sum(
            gv_ref[:, columns].astype(F32), axis=0, keepdims=True
        )

    tiles(width, project)
    all_ref[2 : 2 + seq_len, :] = pos_ref[0:seq_len, :]
    all_ref[base + 2 : base + 3, :] = inner_ref[2:3, :]
    all_ref[base + 3 : base + 5, :] = inner_ref[0:2, :]
    all_ref[base + 5 : base + 6, :] = after_ref[5:6, :]
    all_ref[base + 6 : base + 8, :] = after_ref[3:5, :]
    for k in range(4):
        all_ref[base + 8 + k : base + 9 + k, :] = up_ref[:, k * width : (k + 1) * width]
    all_ref[base + 12 : base + 14, :] = after_ref[1:3, :]
    all_ref[base + 14 : base + 15, :] = after_ref[0:1, :]
    quarter, size = keep_ref.shape[1:]
    used = base + 15
    all_ref[used:, :] = jnp.zeros_like(all_ref[used:, :])
    for unit in range(4):
        shifted = jnp.bitwise_xor(where_ref[0], unit)
        for other, target in ((0, keep_ref), (1, send_ref)):

            @pl.when(jnp.bitwise_and(shifted, 1) == other)
            def _():
                for f in range(width // size):
                    place = position(stages, shifted, jnp.bitwise_xor(where_ref[1], f))
                    target[place] = all_ref[
                        unit * quarter : (unit + 1) * quarter, f * size : (f + 1) * size
                    ]


def adam_step(master, moment_one, moment_two, gradient, factor):
    clipped = gradient * factor
    one_new = beta_one * moment_one + (1.0 - beta_one) * clipped
    two_new = beta_two * moment_two + (1.0 - beta_two) * clipped * clipped
    one_hat = one_new / (1.0 - beta_one**ADAM_STEP)
    two_hat = two_new / (1.0 - beta_two**ADAM_STEP)
    step_value = -learn_rate * (one_hat / (jnp.sqrt(two_hat) + adam_eps) + decay_rate * master)
    return (step_value, one_new, two_new)


def teacher_move(master, teacher, step_value):
    return (1.0 - ema_keep) * (master - teacher + step_value)


def per_device(
    patches,
    mask_places,
    square_weights,
    square_first,
    square_second,
    square_teacher,
    feed_weights,
    feed_first,
    feed_second,
    feed_teacher,
    vector_weights,
    vector_first,
    vector_second,
    vector_teacher,
):
    samples, seq_len, model_width = patches.shape
    total_masked = samples * mask_places.shape[1] * lax.axis_size("rep") * lax.axis_size("fsdp")
    rep, own = lax.axis_index("rep"), lax.axis_index("fsdp")
    where = jnp.stack([rep, own]).astype(jnp.int32)
    pad_len = -(-seq_len // 8) * 8
    row_count = samples * pad_len
    hidden_units = feed_weights.shape[3]
    patch_rows = jnp.pad(patches, ((0, 0), (0, pad_len - seq_len), (0, 0))).reshape(
        row_count, model_width
    )
    places = jnp.arange(pad_len, dtype=jnp.int32)
    mask_rows = jnp.sum(
        (mask_places[:, :, None] == places[None, None, :]).astype(F32), axis=1
    ).reshape(row_count, 1)

    def pick(array, index):
        return to_low(lax.dynamic_index_in_dim(array, index, keepdims=False))

    def columns_of(array, number):
        width = array.shape[3] // 4
        return to_low(lax.dynamic_slice_in_dim(array[0, number], rep * width, width, axis=1))

    pieces = gather_vectors(jnp.stack([vector_weights, vector_teacher]), where)
    both_s = lax.all_gather(
        jnp.concatenate([columns_of(feed_weights, 0), columns_of(feed_weights, 1)]),
        ("fsdp", "rep"),
        axis=0,
        tiled=True,
    )
    up_s = Gathered(both_s, 0, 2, True, where)
    down_s = Gathered(both_s, 1, 2, True, where)
    others = jnp.where(
        rep == 0, to_low(square_teacher[4]), pick(square_weights, jnp.clip(rep + 3, 4, 5))
    )
    entry_t = Group(pick(square_teacher, rep), 0, False, where)
    entry_s = Group(pick(square_weights, rep), 1, False, where, entry_t)
    outer = Group(others, 0, False, where, entry_s)
    up_t = Group(columns_of(feed_teacher, 0), 1, True, where, outer)
    down_t = Group(columns_of(feed_teacher, 1), 0, True, where, up_t)
    entry_t.step(), entry_t.step()
    (pieces,) = tie_groups([pieces], entry_t)
    vector_old_new = place_vectors(pieces, where)
    vector_all, vector_old = vector_old_new[0], vector_old_new[1]
    for group in (entry_t, entry_s, outer):
        group.fabric()
    for group in (up_t, down_t):
        group.step(), group.step()
    (patch_rows_t,) = tie_groups([patch_rows], up_t)
    base = 2 + seq_len

    def positions(vector):
        return jnp.pad(vector[2 : 2 + seq_len], ((0, pad_len - seq_len), (0, 0)))

    full, low_full = ((row_count, model_width), F32), ((row_count, model_width), BF16)
    low_wide, full_wide = ((row_count, hidden_units), BF16), ((row_count, hidden_units), F32)
    column = ((row_count, 1), F32)

    def entry(patch_rows, group, vector, masked, name):
        return call(
            functools.partial(embed_body, samples, masked, base),
            name,
            where,
            [group],
            [patch_rows, vector, positions(vector)] + ([mask_rows] if masked else []),
            [full] + [low_full] * 4,
        )

    hidden_t, _, query, key_rows, value_rows = entry(
        patch_rows_t, entry_t.finish(), vector_old, False, "embed_t"
    )
    up_t.fabric()
    (query,) = tie_groups([query], down_t)
    down_t.fabric()
    attended_t, _ = attention_forward(query, key_rows, value_rows, samples, seq_len)
    (attended_t,) = tie_groups([attended_t], entry_s, outer)
    hidden, hidden_low, query, key_rows, value_rows = entry(
        patch_rows, entry_s.finish(), vector_all, True, "embed_s"
    )
    attended, logsum = attention_forward(query, key_rows, value_rows, samples, seq_len)
    outer.finish()
    (attended,) = tie_groups([attended], up_t, down_t)
    up_t.finish(), down_t.finish()
    (target,) = call(
        functools.partial(teacher_body, samples, seq_len, base),
        "layer_t",
        where,
        [outer, up_t, down_t],
        [attended_t, hidden_t, vector_old],
        [full],
        [pltpu.VMEM(*full), pltpu.VMEM(*low_full), pltpu.VMEM(*low_wide)],
    )
    loss_scale = 1.0 / (total_masked * model_width)
    (
        final_low,
        grad_output,
        grad_branch_two,
        grad_second,
        activation,
        slope,
        normed_low,
        hat_first,
        inverse_first,
        rows_after,
        loss_sum,
    ) = call(
        functools.partial(student_body, samples, base, loss_scale),
        "layer_s",
        where,
        [outer, up_s, down_s],
        [attended, hidden, vector_all, target, mask_rows],
        [low_full] * 3
        + [full, low_wide, full_wide, low_full, full, column, ((8, model_width), F32), ((1, 1), F32)],
        [pltpu.VMEM(*full)] * 4 + [pltpu.VMEM(*column)] * 2,
    )
    loss_local = loss_sum[0, 0] * loss_scale

    unit = model_width
    down_g = owner_grads(grad_branch_two, activation)
    grad_branch_two, down_g = tie(grad_branch_two, down_g)
    down_own = lax.psum_scatter(down_g, ("fsdp", "rep"), scatter_dimension=0, tiled=True)
    grad_pre, grad_first, grad_branch, grad_attended, rows_inner, rows_up = call(
        functools.partial(feed_back_body, samples, base),
        "feed_back",
        where,
        [outer, up_s, down_s],
        [grad_branch_two, grad_second, slope, hat_first, inverse_first, vector_all],
        [low_wide, full, low_full, low_full, ((8, model_width), F32), ((1, hidden_units), F32)],
        [pltpu.VMEM(*full)],
    )
    half = unit // 2

    def up_half(grad, number):
        places = [[(k * unit + number * half, k) for k in range(4)]]
        return unit_grads([(normed_low, grad)], places, number, half, where)

    up_a = up_half(grad_pre, 0)
    (grad_pre,) = tie_sums([grad_pre], up_a)
    up_b = up_half(grad_pre, 1)
    up_a.step()
    (grad_branch,) = tie_sums([grad_branch], up_a, up_b)
    halves = [[(0, 0), (half, 1)], [(0, 2), (half, 3)]]
    edge_g = unit_grads(
        [(final_low, grad_output), (attended, grad_branch)], halves, 0, half, where
    )
    up_a.step()
    up_b.step()
    (grad_attended,) = tie_sums([grad_attended], up_b, edge_g)
    grad_query, grad_key, grad_value = attention_backward(
        query, key_rows, value_rows, logsum, grad_attended, samples, seq_len
    )
    edge_g.step()
    grad_query, grad_key, grad_value = tie_sums([grad_query, grad_key, grad_value], edge_g)
    up_b.step()
    vector_count = vector_weights.shape[0]
    count = lax.axis_size("fsdp")
    quarter = vector_all.shape[0] // 4
    vector_block = ((2 * count, quarter, model_width // count), F32)
    grad_embed, *vector_g = call(
        functools.partial(embed_back_body, samples, seq_len, base, reduce_order(0)),
        "embed_back",
        where,
        [entry_s],
        [grad_query, grad_key, grad_value, grad_first, mask_rows, rows_after, rows_inner, rows_up],
        [low_full, vector_block, vector_block],
        [pltpu.VMEM(vector_all.shape, F32), pltpu.VMEM((pad_len, model_width), F32)],
    )

    def entry_half(grad, number):
        pairs = [(hidden_low, grad_query), (hidden_low, grad_key), (hidden_low, grad_value), (patch_rows, grad)]
        return unit_grads(pairs, [[(number * half, k)] for k in range(4)], number, half, where)

    vector_g = Summing(*vector_g, 0)
    edge_g.step()
    (grad_embed,) = tie_sums([grad_embed], up_b, up_a)
    qkv_a = entry_half(grad_embed, 0)
    up_b.step()
    up_a.step()
    vector_g.step()
    (grad_embed,) = tie_sums([grad_embed], up_a, edge_g, vector_g, qkv_a)
    qkv_b = entry_half(grad_embed, 1)
    up_a.step()
    edge_g.step()
    qkv_a.step()
    vector_g.step()
    (down_own,) = tie_sums([down_own], qkv_a, qkv_b, up_b, vector_g, up_a)
    qkv_a.step()
    qkv_b.step()
    up_b.step()
    up_a.step()
    vector_g.step()
    tie_sums([], qkv_b, up_b, vector_g)
    qkv_b.step()
    up_b.step()
    vector_g.step()
    tie_sums([], edge_g, vector_g, up_b, qkv_a, qkv_b)
    edge_g.step()

    edge_own = edge_g.finish()
    vector_own = vector_g.finish()
    up_own = jnp.concatenate([up_a.finish(), up_b.finish()], axis=1)
    qkv_own = jnp.concatenate([qkv_a.finish(), qkv_b.finish()], axis=1)
    squares_own = (
        jnp.sum(down_own * down_own)
        + jnp.sum(up_own * up_own)
        + jnp.sum(edge_own * edge_own)
        + jnp.sum(qkv_own * qkv_own)
        + jnp.sum(vector_own * vector_own)
    )
    totals = jnp.stack([squares_own, loss_local])
    for bit in fsdp_bits():
        totals = totals + swap(totals, ("fsdp", bit))
    for bit in (2, 1):
        totals = totals + swap(totals, ("rep", bit))
    norm_squared, loss_value = totals[0], totals[1]

    def ordered(own_units):
        shared = share_units(own_units)
        return [lax.dynamic_index_in_dim(shared, rep ^ k, keepdims=False) for k in range(4)]

    early_u = ordered(jnp.concatenate([down_own, up_own, edge_own], axis=1))
    late_u = ordered(
        jnp.concatenate([qkv_own, vector_own.reshape(qkv_own.shape[0], quarter)], axis=1)
    )
    qkv_u = [own[:, :unit] for own in late_u]
    vector_share = jnp.concatenate(
        [own[:, unit:].reshape(vector_own.shape[1:]) for own in late_u], axis=0
    )[:vector_count]
    down_u = [own[:, :unit] for own in early_u]
    up_u = [own[:, unit : 2 * unit] for own in early_u]
    edge_u = [own[:, 2 * unit :] for own in early_u]
    feed_grad = jnp.stack([jnp.concatenate(up_u, axis=1), jnp.concatenate(down_u, axis=1)])[None]
    square_grad = jnp.stack(
        [
            qkv_u[3],
            qkv_u[0],
            qkv_u[1],
            qkv_u[2],
            jnp.concatenate(edge_u[2:], axis=1),
            jnp.concatenate(edge_u[:2], axis=1),
        ]
    )
    grad_norm = jnp.sqrt(norm_squared)
    limit = clip_scale / math.sqrt(total_masked)
    factor = limit / jnp.maximum(grad_norm, limit)
    square_step, square_one, square_two = adam_step(
        square_weights, square_first, square_second, square_grad, factor
    )
    feed_step, feed_one, feed_two = adam_step(
        feed_weights, feed_first, feed_second, feed_grad, factor
    )
    vector_step, vector_one, vector_two = adam_step(
        vector_weights, vector_first, vector_second, vector_share, factor
    )
    square_moved = teacher_move(square_weights, square_teacher, square_step)
    feed_moved = teacher_move(feed_weights, feed_teacher, feed_step)
    vector_moved = teacher_move(vector_weights, vector_teacher, vector_step)
    return (
        loss_value,
        grad_norm,
        square_step,
        square_one,
        square_two,
        square_moved,
        feed_step,
        feed_one,
        feed_two,
        feed_moved,
        vector_step,
        vector_one,
        vector_two,
        vector_moved,
    )


def solution(mesh):
    placed = (
        P(("rep", "fsdp"), None, None),
        P(("rep", "fsdp"), None),
        P(None, "fsdp", None),
        P(None, "fsdp", None),
        P(None, "fsdp", None),
        P(None, "fsdp", None),
        P(None, None, "fsdp", None),
        P(None, None, "fsdp", None),
        P(None, None, "fsdp", None),
        P(None, None, "fsdp", None),
        P(None, "fsdp"),
        P(None, "fsdp"),
        P(None, "fsdp"),
        P(None, "fsdp"),
    )
    return jax.shard_map(
        per_device,
        mesh=mesh,
        in_specs=placed,
        out_specs=(
            P(),
            P(),
            P(None, "fsdp", None),
            P(None, "fsdp", None),
            P(None, "fsdp", None),
            P(None, "fsdp", None),
            P(None, None, "fsdp", None),
            P(None, None, "fsdp", None),
            P(None, None, "fsdp", None),
            P(None, None, "fsdp", None),
            P(None, "fsdp"),
            P(None, "fsdp"),
            P(None, "fsdp"),
            P(None, "fsdp"),
        ),
        check_vma=False,
    )
```

```python
import functools
import math

import jax
import jax.numpy as jnp
from jax import lax
from jax.experimental import pallas as pl
from jax.experimental.pallas import tpu as pltpu
from jax.sharding import PartitionSpec as P

HEADS = 12
ADAM_STEP = 10


ln_eps = 1e-05
beta_one = 0.9
beta_two = 0.999
adam_eps = 1e-08
learn_rate = 0.01
decay_rate = 0.05
ema_keep = 0.999
huber_delta = 1.0
clip_scale = 1.25

VMEM_LIMIT = 60 * 1024 * 1024
SHARE = 0.0
MICROSECONDS = dict(
    gather_vectors=3,
    embed_t=9,
    embed_s=9,
    attention=7,
    layer_t=23,
    layer_s=33,
    owner_grads=8,
    feed_back=23,
    unit_grads=7,
    attention_back=16,
    embed_back=9,
)


def cost(name):
    flops = int(SHARE * MICROSECONDS[name] * 1.15e9)
    return pl.CostEstimate(flops=flops, bytes_accessed=1024, transcendentals=0)
BF16 = jnp.bfloat16
F32 = jnp.float32


def to_low(values):
    return values.astype(BF16)


def matmul(left, right):
    return jnp.dot(left, right, preferred_element_type=F32)


def matmul_tn(left, right):
    return lax.dot_general(left, right, (((0,), (0,)), ((), ())), preferred_element_type=F32)


def matmul_nt(left, right):
    return lax.dot_general(left, right, (((1,), (1,)), ((), ())), preferred_element_type=F32)


tail_scale = 0.21
tail_terms = (
    0.08371158707086396,
    0.08506867712628283,
    0.06919339848407204,
    0.1248680487092072,
    -0.09391427181816406,
    0.34938494294095396,
    -0.3302388882989717,
    0.2835812219436135,
    -0.07165470896901999,
)


def gelu_exact(values):
    t = 1.0 / (1.0 + tail_scale * jnp.abs(values))
    tail = jnp.full_like(t, tail_terms[-1])
    for term in tail_terms[-2::-1]:
        tail = tail * t + term
    bell = jnp.exp(-0.5 * (values * values))
    tail = tail * t * bell
    normal = jnp.where(values < 0, tail, 1.0 - tail)
    return values * normal, normal + values * bell * (1.0 / math.sqrt(2.0 * math.pi))


def norm_parts(values):
    centred = values - jnp.mean(values, axis=-1, keepdims=True)
    inverse = lax.rsqrt(jnp.mean(centred * centred, axis=-1, keepdims=True) + ln_eps)
    return centred * inverse, inverse


def norm_back(grad, hat, inverse, gain):
    scaled = grad * gain
    return inverse * (
        scaled
        - jnp.mean(scaled, axis=-1, keepdims=True)
        - hat * jnp.mean(scaled * hat, axis=-1, keepdims=True)
    )


def any_spec():
    return pl.BlockSpec(memory_space=pl.ANY)


def vmem_spec():
    return pl.BlockSpec(memory_space=pltpu.VMEM)


def smem_spec():
    return pl.BlockSpec(memory_space=pltpu.SMEM)


def swap(values, stage):
    axis, bit = stage
    return lax.ppermute(values, axis, [(i, i ^ bit) for i in range(lax.axis_size(axis))])


def fsdp_bits():
    count = lax.axis_size("fsdp")
    return [1 << k for k in reversed(range(count.bit_length() - 1))]


def stage_order(kind):
    stages = [("fsdp", bit) for bit in fsdp_bits()]
    place = len(stages) if kind == 0 else len(stages) - 1
    return stages[:place] + [("rep", 2)] + stages[place:]


def tie(*values):
    return lax.optimization_barrier(values)


class Group:
    def __init__(self, mine, kind, wide, where, before=None):
        self.wide, self.where = wide, where
        self.rows, self.width = mine.shape
        count = lax.axis_size("fsdp")
        depth = self.rows * count
        self.shape = (depth, 4 * self.width) if wide else (4, depth, self.width)
        self.blocks = 4 * count
        if before is not None:
            mine, before.arrays[0] = tie(mine, before.arrays[0])
        self.arrays, self.labels = [mine], [[(0, 0)]]
        self.stages = stage_order(kind)
        self.step()

    def step(self):
        axis, bit = self.stages.pop(0)
        got = swap(self.arrays[0], (axis, bit))
        moved = [
            (u ^ bit, e) if axis == "rep" else (u, e ^ bit) for u, e in self.labels[0]
        ]
        if self.stages:
            self.arrays = [jnp.concatenate([self.arrays[0], got], axis=0)]
            self.labels = [self.labels[0] + moved]
        else:
            self.arrays, self.labels = self.arrays + [got], self.labels + [moved]

    def fabric(self):
        while self.stages:
            self.step()
        return self

    def finish(self):
        self.arrays = self.arrays + [swap(a, ("rep", 1)) for a in self.arrays]
        self.labels = self.labels + [[(u ^ 1, e) for u, e in block] for block in self.labels]
        if self.rows % 16:
            count = lax.axis_size("fsdp")
            flat = jnp.concatenate(self.arrays, axis=0).reshape(-1, self.rows, self.width)
            order = [label for block in self.labels for label in block]
            place = {label: number for number, label in enumerate(order)}
            table = jnp.array(
                [[place[(u, e)] for e in range(count)] for u in range(4)], jnp.int32
            )
            units = jnp.arange(4, dtype=jnp.int32)[:, None] ^ self.where[0]
            owners = jnp.arange(count, dtype=jnp.int32)[None] ^ self.where[1]
            whole = flat[table[units, owners]].reshape(4, -1, self.width)
            self.whole(whole)
        return self

    def whole(self, units):
        if self.wide:
            units = units.transpose(1, 0, 2).reshape(self.shape)
        self.arrays, self.labels, self.blocks = [units], None, 1

    def copies(self, where_ref, arrays, out, sems):
        if self.labels is None:
            return [pltpu.make_async_copy(arrays[0], out, sems.at[0])]
        rep, own = where_ref[0], where_ref[1]
        copies = []
        for array, block in zip(arrays, self.labels):
            for number, (u, e) in enumerate(block):
                unit = jnp.bitwise_xor(rep, u)
                rows = pl.ds(pl.multiple_of(jnp.bitwise_xor(own, e) * self.rows, 16), self.rows)
                if self.wide:
                    columns = pl.ds(pl.multiple_of(unit * self.width, 128), self.width)
                    target = out.at[rows, columns]
                else:
                    target = out.at[unit, rows, :]
                source = array.at[pl.ds(number * self.rows, self.rows), :]
                copies.append(pltpu.make_async_copy(source, target, sems.at[len(copies)]))
        return copies


def tie_groups(values, *groups):
    tied = tie(*values, *[array for group in groups for array in group.arrays])
    values, arrays = tied[: len(values)], list(tied[len(values) :])
    for group in groups:
        group.arrays = [arrays.pop(0) for _ in group.arrays]
    return values


class Gathered(Group):
    def __init__(self, gathered, number, groups, wide, where):
        count = lax.axis_size("fsdp")
        self.wide, self.where = wide, where
        self.rows, self.width = gathered.shape[0] // (4 * count * groups), gathered.shape[1]
        depth = self.rows * count
        self.shape = (depth, 4 * self.width) if wide else (4, depth, self.width)
        self.arrays, self.labels, self.blocks = [gathered], (), 4 * count
        self.number, self.groups = number, groups
        if self.rows % 16:
            blocks = gathered.reshape(count, 4, groups, self.rows, self.width)[:, :, number]
            self.whole(blocks.transpose(1, 0, 2, 3).reshape(4, depth, self.width))

    def copies(self, where_ref, arrays, out, sems):
        if self.labels is None:
            return [pltpu.make_async_copy(arrays[0], out, sems.at[0])]
        copies = []
        for place in range(self.blocks):
            owner, unit = place // 4, place % 4
            rows = slice(owner * self.rows, (owner + 1) * self.rows)
            if self.wide:
                target = out.at[rows, unit * self.width : (unit + 1) * self.width]
            else:
                target = out.at[unit, rows, :]
            first = (place * self.groups + self.number) * self.rows
            source = arrays[0].at[first : first + self.rows, :]
            copies.append(pltpu.make_async_copy(source, target, sems.at[place]))
        return copies


class Loading:
    def __init__(self, copies, ref):
        self.pending, self.ref = copies, ref
        for copy in copies:
            copy.start()

    def __call__(self):
        for copy in self.pending:
            copy.wait()
        self.pending = []
        return self.ref


def call(body, name, where, groups, ins, outs, scratch=()):
    sizes = [len(group.arrays) for group in groups]

    def kernel(where_ref, *refs):
        refs = list(refs)
        arrays = [[refs.pop(0) for _ in range(size)] for size in sizes]
        in_refs = [refs.pop(0) for _ in ins]
        out_refs = [refs.pop(0) for _ in outs]
        places = [refs.pop(0) for _ in groups]
        sems = [refs.pop(0) for _ in groups]
        loads = [
            Loading(group.copies(where_ref, given, place, sem), place)
            for group, given, place, sem in zip(groups, arrays, places, sems)
        ]
        body(where_ref, loads, in_refs, out_refs, refs)

    return pl.pallas_call(
        kernel,
        out_shape=tuple(jax.ShapeDtypeStruct(*out) for out in outs),
        in_specs=[smem_spec()] + [any_spec()] * sum(sizes) + [vmem_spec()] * len(ins),
        out_specs=(vmem_spec(),) * len(outs),
        scratch_shapes=[pltpu.VMEM(group.shape, BF16) for group in groups]
        + [pltpu.SemaphoreType.DMA((group.blocks,)) for group in groups]
        + list(scratch),
        compiler_params=pltpu.CompilerParams(vmem_limit_bytes=VMEM_LIMIT),
        cost_estimate=cost(name),
        name=name,
    )(where, *[array for group in groups for array in group.arrays], *ins)


def vector_kernel(where_ref, pieces_ref, out_ref):
    _, two, rows, width = pieces_ref.shape
    count = pieces_ref.shape[0] // 4
    for u in range(4):
        for k in range(count):
            place = jnp.bitwise_xor(where_ref[0], u) * count + jnp.bitwise_xor(where_ref[1], k)
            out_ref[:, u * rows : (u + 1) * rows, k * width : (k + 1) * width] = pieces_ref[place]


def gather_vectors(both, where):
    rows = -(-both.shape[1] // 32) * 8
    both = jnp.pad(both, ((0, 0), (0, 4 * rows - both.shape[1]), (0, 0)))
    pieces = lax.dynamic_slice_in_dim(both, where[0] * rows, rows, axis=1)[None]
    for stage in [("fsdp", bit) for bit in reversed(fsdp_bits())] + [("rep", 1), ("rep", 2)]:
        pieces = jnp.concatenate([pieces, swap(pieces, stage)], axis=0)
    return pieces


def place_vectors(pieces, where):
    count, two, rows, width = pieces.shape
    return pl.pallas_call(
        vector_kernel,
        out_shape=jax.ShapeDtypeStruct((two, 4 * rows, count // 4 * width), pieces.dtype),
        in_specs=[smem_spec(), vmem_spec()],
        out_specs=vmem_spec(),
        compiler_params=pltpu.CompilerParams(vmem_limit_bytes=VMEM_LIMIT),
        cost_estimate=cost("gather_vectors"),
        name="gather_vectors",
    )(where, pieces)


def reduce_order(kind):
    stages = [("fsdp", bit) for bit in reversed(fsdp_bits())]
    place = 0 if kind == 0 else 1
    return stages[:place] + [("rep", 2)] + stages[place:]


def position(stages, unit, owner):
    place = 0
    for axis, bit in stages:
        value = unit if axis == "rep" else owner
        place = place * 2 + jnp.where(jnp.bitwise_and(value, bit) != 0, 1, 0)
    return place


def grad_kernel(unit_of, kind_stages, rows, width, where_ref, *refs):
    count = len(unit_of)
    lefts, rights = refs[:count], refs[count : 2 * count]
    keep, send = refs[2 * count], refs[2 * count + 1]
    rep, own = where_ref[0], where_ref[1]
    owners = lefts[0].shape[1] // rows
    for pair in range(count):
        left = lefts[pair][...]
        for column, unit in unit_of[pair]:
            product = matmul_tn(left, rights[pair][:, column : column + width])
            shifted = jnp.bitwise_xor(rep, unit)
            for other, target in ((0, keep), (1, send)):

                @pl.when(jnp.bitwise_and(shifted, 1) == other)
                def _():
                    for f in range(owners):
                        place = position(kind_stages, shifted, jnp.bitwise_xor(own, f))
                        target[pl.ds(pl.multiple_of(place * rows, 8), rows), :] = product[
                            f * rows : (f + 1) * rows, :
                        ]


def unit_grads(pairs, unit_of, kind, width, where):
    depth = pairs[0][0].shape[1]
    rows = depth // lax.axis_size("fsdp")
    shape = jax.ShapeDtypeStruct((2 * depth, width), F32)
    return Summing(
        *pl.pallas_call(
            functools.partial(grad_kernel, unit_of, reduce_order(kind), rows, width),
            out_shape=(shape, shape),
            in_specs=[smem_spec()] + [vmem_spec()] * (2 * len(pairs)),
            out_specs=(vmem_spec(), vmem_spec()),
            compiler_params=pltpu.CompilerParams(vmem_limit_bytes=VMEM_LIMIT),
            cost_estimate=cost("unit_grads"),
            name="unit_grads",
        )(where, *[left for left, _ in pairs], *[right for _, right in pairs]),
        kind,
    )


class Summing:
    def __init__(self, keep, send, kind):
        self.parts, self.stages = (keep, send), [("rep", 1)] + reduce_order(kind)

    def step(self):
        keep, send = self.parts
        got = swap(send, self.stages.pop(0))
        if self.stages:
            half = keep.shape[0] // 2
            self.parts = keep[:half] + got[:half], keep[half:] + got[half:]
        else:
            self.parts = (keep + got,)

    def finish(self):
        while self.stages:
            self.step()
        return self.parts[0]


def tie_sums(values, *sums):
    tied = tie(*values, *[part for one in sums for part in one.parts])
    values, parts = tied[: len(values)], list(tied[len(values) :])
    for one in sums:
        one.parts = tuple(parts.pop(0) for _ in one.parts)
    return values


def owner_kernel(count, width, left_ref, right_ref, out_ref):
    rows = left_ref.shape[1] // count
    left = left_ref[...]
    for unit in range(4):
        product = matmul_tn(left, right_ref[:, unit * width : (unit + 1) * width])
        for owner in range(count):
            place = (owner * 4 + unit) * rows
            out_ref[place : place + rows, :] = product[owner * rows : (owner + 1) * rows, :]


def owner_grads(left, right):
    depth, width = left.shape[1], right.shape[1] // 4
    return pl.pallas_call(
        functools.partial(owner_kernel, lax.axis_size("fsdp"), width),
        out_shape=jax.ShapeDtypeStruct((4 * depth, width), F32),
        in_specs=[vmem_spec()] * 2,
        out_specs=vmem_spec(),
        compiler_params=pltpu.CompilerParams(vmem_limit_bytes=VMEM_LIMIT),
        cost_estimate=cost("owner_grads"),
        name="owner_grads",
    )(left, right)


def share_units(own):
    far = swap(own, ("rep", 2))
    near, cross = swap(own, ("rep", 1)), swap(far, ("rep", 1))
    return jnp.stack([own, near, far, cross])


def scores_of(query, key_rows, valid, scaling):
    scores = matmul_nt(query, key_rows) * scaling
    return jnp.where(valid, scores, -1e30)


def attention_kernel(seq_len, head_dim, q_ref, k_ref, v_ref, out_ref, log_ref):
    rows, model_width = q_ref.shape
    scaling = head_dim**-0.5
    valid = lax.broadcasted_iota(jnp.int32, (rows, rows), 1) < seq_len
    lane = lax.broadcasted_iota(jnp.int32, (rows, 2 * head_dim), 1)
    zero = jnp.zeros((rows, 2 * head_dim), BF16)
    for pair in range(model_width // (2 * head_dim)):
        columns = slice(pair * 2 * head_dim, (pair + 1) * 2 * head_dim)
        query, key_rows, values = q_ref[:, columns], k_ref[:, columns], v_ref[:, columns]
        results = []
        for sub in range(2):
            picked = lane >= head_dim if sub else lane < head_dim
            scores = scores_of(jnp.where(picked, query, zero), key_rows, valid, scaling)
            highest = jnp.max(scores, axis=-1, keepdims=True)
            logsum = highest + jnp.log(jnp.sum(jnp.exp(scores - highest), axis=-1, keepdims=True))
            log_ref[:, 2 * pair + sub : 2 * pair + sub + 1] = logsum
            results.append(matmul(to_low(jnp.exp(scores - logsum)), values))
        out_ref[:, columns] = to_low(jnp.where(lane < head_dim, results[0], results[1]))


def attention_forward(query, key_rows, value_rows, samples, seq_len):
    row_count, model_width = query.shape
    rows = row_count // samples
    head_dim = model_width // HEADS
    block = pl.BlockSpec((rows, model_width), lambda i: (i, 0))
    small = pl.BlockSpec((rows, 128), lambda i: (i, 0))
    return pl.pallas_call(
        functools.partial(attention_kernel, seq_len, head_dim),
        grid=(samples,),
        out_shape=(
            jax.ShapeDtypeStruct(query.shape, BF16),
            jax.ShapeDtypeStruct((row_count, 128), F32),
        ),
        in_specs=[block] * 3,
        out_specs=(block, small),
        compiler_params=pltpu.CompilerParams(vmem_limit_bytes=VMEM_LIMIT),
        cost_estimate=cost("attention"),
        name="attention",
    )(query, key_rows, value_rows)


def attention_back_kernel(
    seq_len, head_dim, q_ref, k_ref, v_ref, da_ref, log_ref, dq_ref, dk_ref, dv_ref
):
    rows, model_width = q_ref.shape
    scaling = head_dim**-0.5
    valid = lax.broadcasted_iota(jnp.int32, (rows, rows), 1) < seq_len
    lane = lax.broadcasted_iota(jnp.int32, (rows, 2 * head_dim), 1)
    zero = jnp.zeros((rows, 2 * head_dim), BF16)
    for pair in range(model_width // (2 * head_dim)):
        columns = slice(pair * 2 * head_dim, (pair + 1) * 2 * head_dim)
        query, key_rows = q_ref[:, columns], k_ref[:, columns]
        values, grad = v_ref[:, columns], da_ref[:, columns]
        results = []
        for sub in range(2):
            picked = lane >= head_dim if sub else lane < head_dim
            scores = scores_of(jnp.where(picked, query, zero), key_rows, valid, scaling)
            soft = jnp.exp(scores - log_ref[:, 2 * pair + sub : 2 * pair + sub + 1])
            grad_soft = matmul_nt(jnp.where(picked, grad, zero), values)
            total = jnp.sum(grad_soft * soft, axis=-1, keepdims=True)
            grad_scores = to_low(soft * (grad_soft - total))
            results.append(
                (
                    matmul(grad_scores, key_rows) * scaling,
                    matmul_tn(grad_scores, query) * scaling,
                    matmul_tn(to_low(soft), grad),
                )
            )
        for target, first, second in zip((dq_ref, dk_ref, dv_ref), *results):
            target[:, columns] = to_low(jnp.where(lane < head_dim, first, second))


def attention_backward(query, key_rows, value_rows, logsum, grad, samples, seq_len):
    row_count, model_width = query.shape
    rows = row_count // samples
    head_dim = model_width // HEADS
    block = pl.BlockSpec((rows, model_width), lambda i: (i, 0))
    small = pl.BlockSpec((rows, 128), lambda i: (i, 0))
    return pl.pallas_call(
        functools.partial(attention_back_kernel, seq_len, head_dim),
        grid=(samples,),
        out_shape=(jax.ShapeDtypeStruct(query.shape, BF16),) * 3,
        in_specs=[block] * 4 + [small],
        out_specs=(block,) * 3,
        compiler_params=pltpu.CompilerParams(vmem_limit_bytes=VMEM_LIMIT),
        cost_estimate=cost("attention_back"),
        name="attention_back",
    )(query, key_rows, value_rows, grad, logsum)


TILE = 256
UNROLL = 3


def tiles(width, body):
    def step(number, carry):
        body(pl.ds(pl.multiple_of(number * TILE, TILE), TILE))
        return carry

    lax.fori_loop(0, width // TILE, step, 0, unroll=min(UNROLL, width // TILE))


def embed_body(samples, masked, base, where_ref, loads, ins, outs, scratch):
    patch_ref, vec_ref, pos_ref = ins[:3]
    hid_ref, low_ref, q_ref, k_ref, v_ref = outs
    weights = loads[0]()
    rows = patch_ref.shape[0] // samples
    width = patch_ref.shape[1]

    def embed(columns):
        product = matmul(patch_ref[...], weights[0, :, columns]) + vec_ref[0:1, columns]
        if masked:
            product = jnp.where(ins[3][...] > 0, vec_ref[1:2, columns], product)
        for s in range(samples):
            part = product[s * rows : (s + 1) * rows] + pos_ref[:, columns]
            hid_ref[s * rows : (s + 1) * rows, columns] = part
            low_ref[s * rows : (s + 1) * rows, columns] = to_low(part)

    tiles(width, embed)

    def project(columns):
        low = low_ref[...]
        q_ref[:, columns] = to_low(
            matmul(low, weights[1, :, columns]) + vec_ref[base : base + 1, columns]
        )
        k_ref[:, columns] = to_low(matmul(low, weights[2, :, columns]))
        v_ref[:, columns] = to_low(
            matmul(low, weights[3, :, columns]) + vec_ref[base + 1 : base + 2, columns]
        )

    tiles(width, project)


def feed_forward(samples, base, unit, loads, ins, student, refs):
    att_ref, hid_ref, vec_ref = ins
    sum_ref, low_ref, act_ref = refs[:3]
    rows, width = hid_ref.shape[0] // samples, hid_ref.shape[1]
    squares = loads[0]()

    def project(columns):
        sum_ref[:, columns] = (
            hid_ref[:, columns]
            + matmul(att_ref[...], squares[unit, :, columns])
            + vec_ref[base + 2 : base + 3, columns]
        )

    tiles(width, project)
    for s in range(samples):
        part = slice(s * rows, (s + 1) * rows)
        hat, inverse = norm_parts(sum_ref[part, :])
        if student:
            refs[3][part, :], refs[4][part, :] = hat, inverse
        normed = hat * vec_ref[base + 3 : base + 4, :] + vec_ref[base + 4 : base + 5, :]
        sum_ref[part, :] = normed
        low_ref[part, :] = to_low(normed)
    up = loads[1]()
    hidden_units = up.shape[1]

    def widen(columns, bias):
        pre_act = matmul(low_ref[...], up[:, columns]) + bias
        value, slope = gelu_exact(pre_act)
        act_ref[:, columns] = to_low(value)
        if student:
            refs[5][:, columns] = slope

    for quarter in range(4):
        size = hidden_units // 4

        def step(number, carry, quarter=quarter):
            inner = pl.ds(pl.multiple_of(number * TILE, TILE), TILE)
            outer = pl.ds(pl.multiple_of(quarter * size + number * TILE, TILE), TILE)
            widen(outer, vec_ref[base + 8 + quarter : base + 9 + quarter, inner])
            return carry

        lax.fori_loop(0, size // TILE, step, 0, unroll=min(UNROLL, size // TILE))
    down = loads[2]()

    def narrow(columns, target_ref, residual):
        branch = (
            matmul_nt(act_ref[...], down[columns, :]) + vec_ref[base + 5 : base + 6, columns]
        )
        target_ref[:, columns] = sum_ref[:, columns] + branch if residual else branch

    return narrow


def teacher_body(samples, seq_len, base, where_ref, loads, ins, outs, scratch):
    target_ref = outs[0]
    narrow = feed_forward(samples, base, 0, loads, ins, False, scratch)
    rows, width = target_ref.shape[0] // samples, target_ref.shape[1]
    tiles(width, lambda columns: narrow(columns, target_ref, False))
    valid = lax.broadcasted_iota(jnp.int32, (rows, width), 0) < seq_len
    for s in range(samples):
        part = slice(s * rows, (s + 1) * rows)
        values = target_ref[part, :]
        total = jnp.sum(jnp.where(valid, values, 0.0), axis=0, keepdims=True)
        centred = values - total * (1.0 / seq_len)
        spread = jnp.sum(jnp.where(valid, centred * centred, 0.0), axis=0, keepdims=True)
        target_ref[part, :] = centred * lax.rsqrt(spread * (1.0 / seq_len) + ln_eps)


def student_body(samples, base, loss_scale, where_ref, loads, ins, outs, scratch):
    target_ref, mask_ref = ins[3:]
    final_ref, dy_ref, gb2_ref, g2_ref, act_ref, slope_ref, low_ref, hat_ref, inv_ref = outs[:9]
    rows_ref, loss_ref = outs[9:]
    sum_ref, hat2_ref, hatf_ref, gf_ref, inv2_ref, invf_ref = scratch
    narrow = feed_forward(
        samples, base, 1, loads, ins[:3], True, (sum_ref, low_ref, act_ref, hat_ref, inv_ref, slope_ref)
    )
    vec_ref = ins[2]
    squares = loads[0]()
    width = sum_ref.shape[1]
    rows = sum_ref.shape[0] // samples
    final_base = base + 12
    tiles(width, lambda columns: narrow(columns, gf_ref, True))
    for s in range(samples):
        part = slice(s * rows, (s + 1) * rows)
        hat, inverse = norm_parts(gf_ref[part, :])
        hat2_ref[part, :], inv2_ref[part, :] = hat, inverse
        result = hat * vec_ref[base + 6 : base + 7, :] + vec_ref[base + 7 : base + 8, :]
        hat, inverse = norm_parts(result)
        hatf_ref[part, :], invf_ref[part, :] = hat, inverse
        final_ref[part, :] = to_low(
            hat * vec_ref[final_base : final_base + 1, :]
            + vec_ref[final_base + 1 : final_base + 2, :]
        )
    rows_ref[...] = jnp.zeros_like(rows_ref)
    loss_ref[...] = jnp.zeros_like(loss_ref)

    def head(columns):
        output = matmul(final_ref[...], squares[2, :, columns])
        residue = output + vec_ref[final_base + 2 : final_base + 3, columns] - target_ref[:, columns]
        magnitude = jnp.abs(residue)
        terms = jnp.where(
            magnitude <= huber_delta,
            0.5 * residue * residue,
            huber_delta * (magnitude - 0.5 * huber_delta),
        )
        loss_ref[...] += jnp.sum(
            jnp.sum(terms * mask_ref[...], axis=0, keepdims=True), axis=1, keepdims=True
        )
        grad = to_low(jnp.clip(residue, -huber_delta, huber_delta) * mask_ref[...] * loss_scale)
        dy_ref[:, columns] = grad
        rows_ref[0:1, columns] = jnp.sum(grad.astype(F32), axis=0, keepdims=True)

    tiles(width, head)

    def back(columns):
        gf_ref[:, columns] = matmul_nt(dy_ref[...], squares[2, columns, :])

    tiles(width, back)
    for s in range(samples):
        part = slice(s * rows, (s + 1) * rows)
        grad, hat = gf_ref[part, :], hatf_ref[part, :]
        rows_ref[1:2, :] += jnp.sum(grad * hat, axis=0, keepdims=True)
        rows_ref[2:3, :] += jnp.sum(grad, axis=0, keepdims=True)
        grad = norm_back(grad, hat, invf_ref[part, :], vec_ref[final_base : final_base + 1, :])
        hat = hat2_ref[part, :]
        rows_ref[3:4, :] += jnp.sum(grad * hat, axis=0, keepdims=True)
        rows_ref[4:5, :] += jnp.sum(grad, axis=0, keepdims=True)
        grad = norm_back(grad, hat, inv2_ref[part, :], vec_ref[base + 6 : base + 7, :])
        g2_ref[part, :] = grad
        low = to_low(grad)
        gb2_ref[part, :] = low
        rows_ref[5:6, :] += jnp.sum(low.astype(F32), axis=0, keepdims=True)


def feed_back_body(samples, base, where_ref, loads, ins, outs, scratch):
    gb2_ref, g2_ref, slope_ref, hat_ref, inv_ref, vec_ref = ins
    gpre_ref, gfirst_ref, gbranch_ref, gatt_ref, rows_ref, up_ref = outs
    grad_ref = scratch[0]
    squares, up, down = loads
    down = down()
    width, hidden_units = down.shape
    rows = gb2_ref.shape[0] // samples

    def widen(columns):
        grad = to_low(matmul(gb2_ref[...], down[:, columns]) * slope_ref[:, columns])
        gpre_ref[:, columns] = grad
        up_ref[:, columns] = jnp.sum(grad.astype(F32), axis=0, keepdims=True)

    tiles(hidden_units, widen)
    up = up()

    def narrow(columns):
        grad_ref[:, columns] = g2_ref[:, columns] + matmul_nt(gpre_ref[...], up[columns, :])

    tiles(width, narrow)
    rows_ref[...] = jnp.zeros_like(rows_ref)
    for s in range(samples):
        part = slice(s * rows, (s + 1) * rows)
        grad, hat = grad_ref[part, :], hat_ref[part, :]
        rows_ref[0:1, :] += jnp.sum(grad * hat, axis=0, keepdims=True)
        rows_ref[1:2, :] += jnp.sum(grad, axis=0, keepdims=True)
        grad = norm_back(grad, hat, inv_ref[part, :], vec_ref[base + 3 : base + 4, :])
        gfirst_ref[part, :] = grad
        low = to_low(grad)
        gbranch_ref[part, :] = low
        rows_ref[2:3, :] += jnp.sum(low.astype(F32), axis=0, keepdims=True)
    squares = squares()

    def project(columns):
        gatt_ref[:, columns] = to_low(matmul_nt(gbranch_ref[...], squares[1, columns, :]))

    tiles(width, project)


def embed_back_body(samples, seq_len, base, stages, where_ref, loads, ins, outs, scratch):
    gq_ref, gk_ref, gv_ref, gfirst_ref, mask_ref, after_ref, inner_ref, up_ref = ins
    ge_ref, keep_ref, send_ref = outs
    all_ref, pos_ref = scratch
    weights = loads[0]()
    width = gq_ref.shape[1]
    rows = gq_ref.shape[0] // samples

    def project(columns):
        grad = gfirst_ref[:, columns] + matmul_nt(gq_ref[...], weights[1, columns, :])
        grad += matmul_nt(gk_ref[...], weights[2, columns, :])
        grad += matmul_nt(gv_ref[...], weights[3, columns, :])
        hidden = grad * mask_ref[...]
        all_ref[1:2, columns] = jnp.sum(hidden, axis=0, keepdims=True)
        low = to_low(grad * (1.0 - mask_ref[...]))
        ge_ref[:, columns] = low
        all_ref[0:1, columns] = jnp.sum(low.astype(F32), axis=0, keepdims=True)
        total = grad[0:rows]
        for s in range(1, samples):
            total += grad[s * rows : (s + 1) * rows]
        pos_ref[:, columns] = total
        all_ref[base : base + 1, columns] = jnp.sum(
            gq_ref[:, columns].astype(F32), axis=0, keepdims=True
        )
        all_ref[base + 1 : base + 2, columns] = jnp.sum(
            gv_ref[:, columns].astype(F32), axis=0, keepdims=True
        )

    tiles(width, project)
    all_ref[2 : 2 + seq_len, :] = pos_ref[0:seq_len, :]
    all_ref[base + 2 : base + 3, :] = inner_ref[2:3, :]
    all_ref[base + 3 : base + 5, :] = inner_ref[0:2, :]
    all_ref[base + 5 : base + 6, :] = after_ref[5:6, :]
    all_ref[base + 6 : base + 8, :] = after_ref[3:5, :]
    for k in range(4):
        all_ref[base + 8 + k : base + 9 + k, :] = up_ref[:, k * width : (k + 1) * width]
    all_ref[base + 12 : base + 14, :] = after_ref[1:3, :]
    all_ref[base + 14 : base + 15, :] = after_ref[0:1, :]
    quarter, size = keep_ref.shape[1:]
    used = base + 15
    all_ref[used:, :] = jnp.zeros_like(all_ref[used:, :])
    for unit in range(4):
        shifted = jnp.bitwise_xor(where_ref[0], unit)
        for other, target in ((0, keep_ref), (1, send_ref)):

            @pl.when(jnp.bitwise_and(shifted, 1) == other)
            def _():
                for f in range(width // size):
                    place = position(stages, shifted, jnp.bitwise_xor(where_ref[1], f))
                    target[place] = all_ref[
                        unit * quarter : (unit + 1) * quarter, f * size : (f + 1) * size
                    ]


def adam_step(master, moment_one, moment_two, gradient, factor):
    clipped = gradient * factor
    one_new = beta_one * moment_one + (1.0 - beta_one) * clipped
    two_new = beta_two * moment_two + (1.0 - beta_two) * clipped * clipped
    one_hat = one_new / (1.0 - beta_one**ADAM_STEP)
    two_hat = two_new / (1.0 - beta_two**ADAM_STEP)
    step_value = -learn_rate * (one_hat / (jnp.sqrt(two_hat) + adam_eps) + decay_rate * master)
    return (step_value, one_new, two_new)


def teacher_move(master, teacher, step_value):
    return (1.0 - ema_keep) * (master - teacher + step_value)


def per_device(
    patches,
    mask_places,
    square_weights,
    square_first,
    square_second,
    square_teacher,
    feed_weights,
    feed_first,
    feed_second,
    feed_teacher,
    vector_weights,
    vector_first,
    vector_second,
    vector_teacher,
):
    samples, seq_len, model_width = patches.shape
    total_masked = samples * mask_places.shape[1] * lax.axis_size("rep") * lax.axis_size("fsdp")
    rep, own = lax.axis_index("rep"), lax.axis_index("fsdp")
    where = jnp.stack([rep, own]).astype(jnp.int32)
    pad_len = -(-seq_len // 8) * 8
    row_count = samples * pad_len
    hidden_units = feed_weights.shape[3]
    patch_rows = jnp.pad(patches, ((0, 0), (0, pad_len - seq_len), (0, 0))).reshape(
        row_count, model_width
    )
    places = jnp.arange(pad_len, dtype=jnp.int32)
    mask_rows = jnp.sum(
        (mask_places[:, :, None] == places[None, None, :]).astype(F32), axis=1
    ).reshape(row_count, 1)

    def pick(array, index):
        return to_low(lax.dynamic_index_in_dim(array, index, keepdims=False))

    def columns_of(array, number):
        width = array.shape[3] // 4
        return to_low(lax.dynamic_slice_in_dim(array[0, number], rep * width, width, axis=1))

    pieces = gather_vectors(jnp.stack([vector_weights, vector_teacher]), where)
    both_s = lax.all_gather(
        jnp.concatenate([columns_of(feed_weights, 0), columns_of(feed_weights, 1)]),
        ("fsdp", "rep"),
        axis=0,
        tiled=True,
    )
    up_s = Gathered(both_s, 0, 2, True, where)
    down_s = Gathered(both_s, 1, 2, True, where)
    others = jnp.where(
        rep == 0, to_low(square_teacher[4]), pick(square_weights, jnp.clip(rep + 3, 4, 5))
    )
    entry_t = Group(pick(square_teacher, rep), 0, False, where)
    entry_s = Group(pick(square_weights, rep), 1, False, where, entry_t)
    outer = Group(others, 0, False, where, entry_s)
    up_t = Group(columns_of(feed_teacher, 0), 1, True, where, outer)
    down_t = Group(columns_of(feed_teacher, 1), 0, True, where, up_t)
    entry_t.step(), entry_t.step()
    (pieces,) = tie_groups([pieces], entry_t)
    vector_old_new = place_vectors(pieces, where)
    vector_all, vector_old = vector_old_new[0], vector_old_new[1]
    for group in (entry_t, entry_s, outer):
        group.fabric()
    up_t.fabric(), down_t.fabric()
    base = 2 + seq_len

    def positions(vector):
        return jnp.pad(vector[2 : 2 + seq_len], ((0, pad_len - seq_len), (0, 0)))

    full, low_full = ((row_count, model_width), F32), ((row_count, model_width), BF16)
    low_wide, full_wide = ((row_count, hidden_units), BF16), ((row_count, hidden_units), F32)
    column = ((row_count, 1), F32)

    def entry(patch_rows, group, vector, masked, name):
        return call(
            functools.partial(embed_body, samples, masked, base),
            name,
            where,
            [group],
            [patch_rows, vector, positions(vector)] + ([mask_rows] if masked else []),
            [full] + [low_full] * 4,
        )

    hidden_t, _, query, key_rows, value_rows = entry(
        patch_rows, entry_t.finish(), vector_old, False, "embed_t"
    )
    attended_t, _ = attention_forward(query, key_rows, value_rows, samples, seq_len)
    (attended_t,) = tie_groups([attended_t], entry_s, outer)
    hidden, hidden_low, query, key_rows, value_rows = entry(
        patch_rows, entry_s.finish(), vector_all, True, "embed_s"
    )
    attended, logsum = attention_forward(query, key_rows, value_rows, samples, seq_len)
    outer.finish()
    (attended,) = tie_groups([attended], up_t, down_t)
    up_t.finish(), down_t.finish()
    (target,) = call(
        functools.partial(teacher_body, samples, seq_len, base),
        "layer_t",
        where,
        [outer, up_t, down_t],
        [attended_t, hidden_t, vector_old],
        [full],
        [pltpu.VMEM(*full), pltpu.VMEM(*low_full), pltpu.VMEM(*low_wide)],
    )
    loss_scale = 1.0 / (total_masked * model_width)
    (
        final_low,
        grad_output,
        grad_branch_two,
        grad_second,
        activation,
        slope,
        normed_low,
        hat_first,
        inverse_first,
        rows_after,
        loss_sum,
    ) = call(
        functools.partial(student_body, samples, base, loss_scale),
        "layer_s",
        where,
        [outer, up_s, down_s],
        [attended, hidden, vector_all, target, mask_rows],
        [low_full] * 3
        + [full, low_wide, full_wide, low_full, full, column, ((8, model_width), F32), ((1, 1), F32)],
        [pltpu.VMEM(*full)] * 4 + [pltpu.VMEM(*column)] * 2,
    )
    loss_local = loss_sum[0, 0] * loss_scale

    unit = model_width
    down_g = owner_grads(grad_branch_two, activation)
    grad_branch_two, down_g = tie(grad_branch_two, down_g)
    down_own = lax.psum_scatter(down_g, ("fsdp", "rep"), scatter_dimension=0, tiled=True)
    grad_pre, grad_first, grad_branch, grad_attended, rows_inner, rows_up = call(
        functools.partial(feed_back_body, samples, base),
        "feed_back",
        where,
        [outer, up_s, down_s],
        [grad_branch_two, grad_second, slope, hat_first, inverse_first, vector_all],
        [low_wide, full, low_full, low_full, ((8, model_width), F32), ((1, hidden_units), F32)],
        [pltpu.VMEM(*full)],
    )
    half = unit // 2

    def up_half(grad, number):
        places = [[(k * unit + number * half, k) for k in range(4)]]
        return unit_grads([(normed_low, grad)], places, number, half, where)

    up_a = up_half(grad_pre, 0)
    (grad_pre,) = tie_sums([grad_pre], up_a)
    up_b = up_half(grad_pre, 1)
    up_a.step()
    (grad_branch,) = tie_sums([grad_branch], up_a, up_b)
    halves = [[(0, 0), (half, 1)], [(0, 2), (half, 3)]]
    edge_g = unit_grads(
        [(final_low, grad_output), (attended, grad_branch)], halves, 0, half, where
    )
    up_a.step()
    up_b.step()
    (grad_attended,) = tie_sums([grad_attended], up_b, edge_g)
    grad_query, grad_key, grad_value = attention_backward(
        query, key_rows, value_rows, logsum, grad_attended, samples, seq_len
    )
    edge_g.step()
    grad_query, grad_key, grad_value = tie_sums([grad_query, grad_key, grad_value], edge_g)
    up_b.step()
    vector_count = vector_weights.shape[0]
    count = lax.axis_size("fsdp")
    quarter = vector_all.shape[0] // 4
    vector_block = ((2 * count, quarter, model_width // count), F32)
    grad_embed, *vector_g = call(
        functools.partial(embed_back_body, samples, seq_len, base, reduce_order(0)),
        "embed_back",
        where,
        [entry_s],
        [grad_query, grad_key, grad_value, grad_first, mask_rows, rows_after, rows_inner, rows_up],
        [low_full, vector_block, vector_block],
        [pltpu.VMEM(vector_all.shape, F32), pltpu.VMEM((pad_len, model_width), F32)],
    )

    def entry_half(grad, number):
        pairs = [(hidden_low, grad_query), (hidden_low, grad_key), (hidden_low, grad_value), (patch_rows, grad)]
        return unit_grads(pairs, [[(number * half, k)] for k in range(4)], number, half, where)

    vector_g = Summing(*vector_g, 0)
    edge_g.step()
    (grad_embed,) = tie_sums([grad_embed], up_a)
    qkv_a = entry_half(grad_embed, 0)
    up_a.step()
    vector_g.step()
    (grad_embed,) = tie_sums([grad_embed], up_b, vector_g, qkv_a)
    qkv_b = entry_half(grad_embed, 1)
    up_b.step()
    qkv_a.step()
    tie_sums([], qkv_a, qkv_b, up_a, edge_g)
    qkv_a.step()
    qkv_b.step()
    up_a.step()
    edge_g.step()
    vector_g.step()
    tie_sums([], qkv_b, up_b, vector_g, up_a)
    up_b.step()
    up_a.step()
    vector_g.step()
    tie_sums([], qkv_b, up_b, vector_g)
    qkv_b.step()
    up_b.step()
    vector_g.step()
    (down_own,) = tie_sums([down_own], edge_g, vector_g, up_b, qkv_a, qkv_b)
    edge_g.step()

    edge_own = edge_g.finish()
    vector_own = vector_g.finish()
    up_own = jnp.concatenate([up_a.finish(), up_b.finish()], axis=1)
    qkv_own = jnp.concatenate([qkv_a.finish(), qkv_b.finish()], axis=1)
    squares_own = (
        jnp.sum(down_own * down_own)
        + jnp.sum(up_own * up_own)
        + jnp.sum(edge_own * edge_own)
        + jnp.sum(qkv_own * qkv_own)
        + jnp.sum(vector_own * vector_own)
    )
    totals = jnp.stack([squares_own, loss_local])
    for bit in fsdp_bits():
        totals = totals + swap(totals, ("fsdp", bit))
    for bit in (2, 1):
        totals = totals + swap(totals, ("rep", bit))
    norm_squared, loss_value = totals[0], totals[1]

    def ordered(own_units):
        shared = share_units(own_units)
        return [lax.dynamic_index_in_dim(shared, rep ^ k, keepdims=False) for k in range(4)]

    early_u = ordered(jnp.concatenate([down_own, up_own, edge_own], axis=1))
    late_u = ordered(
        jnp.concatenate([qkv_own, vector_own.reshape(qkv_own.shape[0], quarter)], axis=1)
    )
    qkv_u = [own[:, :unit] for own in late_u]
    vector_share = jnp.concatenate(
        [own[:, unit:].reshape(vector_own.shape[1:]) for own in late_u], axis=0
    )[:vector_count]
    down_u = [own[:, :unit] for own in early_u]
    up_u = [own[:, unit : 2 * unit] for own in early_u]
    edge_u = [own[:, 2 * unit :] for own in early_u]
    feed_grad = jnp.stack([jnp.concatenate(up_u, axis=1), jnp.concatenate(down_u, axis=1)])[None]
    square_grad = jnp.stack(
        [
            qkv_u[3],
            qkv_u[0],
            qkv_u[1],
            qkv_u[2],
            jnp.concatenate(edge_u[2:], axis=1),
            jnp.concatenate(edge_u[:2], axis=1),
        ]
    )
    grad_norm = jnp.sqrt(norm_squared)
    limit = clip_scale / math.sqrt(total_masked)
    factor = limit / jnp.maximum(grad_norm, limit)
    square_step, square_one, square_two = adam_step(
        square_weights, square_first, square_second, square_grad, factor
    )
    feed_step, feed_one, feed_two = adam_step(
        feed_weights, feed_first, feed_second, feed_grad, factor
    )
    vector_step, vector_one, vector_two = adam_step(
        vector_weights, vector_first, vector_second, vector_share, factor
    )
    square_moved = teacher_move(square_weights, square_teacher, square_step)
    feed_moved = teacher_move(feed_weights, feed_teacher, feed_step)
    vector_moved = teacher_move(vector_weights, vector_teacher, vector_step)
    return (
        loss_value,
        grad_norm,
        square_step,
        square_one,
        square_two,
        square_moved,
        feed_step,
        feed_one,
        feed_two,
        feed_moved,
        vector_step,
        vector_one,
        vector_two,
        vector_moved,
    )


def solution(mesh):
    placed = (
        P(("rep", "fsdp"), None, None),
        P(("rep", "fsdp"), None),
        P(None, "fsdp", None),
        P(None, "fsdp", None),
        P(None, "fsdp", None),
        P(None, "fsdp", None),
        P(None, None, "fsdp", None),
        P(None, None, "fsdp", None),
        P(None, None, "fsdp", None),
        P(None, None, "fsdp", None),
        P(None, "fsdp"),
        P(None, "fsdp"),
        P(None, "fsdp"),
        P(None, "fsdp"),
    )
    return jax.shard_map(
        per_device,
        mesh=mesh,
        in_specs=placed,
        out_specs=(
            P(),
            P(),
            P(None, "fsdp", None),
            P(None, "fsdp", None),
            P(None, "fsdp", None),
            P(None, "fsdp", None),
            P(None, None, "fsdp", None),
            P(None, None, "fsdp", None),
            P(None, None, "fsdp", None),
            P(None, None, "fsdp", None),
            P(None, "fsdp"),
            P(None, "fsdp"),
            P(None, "fsdp"),
            P(None, "fsdp"),
        ),
        check_vma=False,
    )
```
